32 devices in a mesh: lat: 4 (over y, core), lon: 8 (over z, x).
Axes of the slice: x: 2, y: 2, z: 4, core: 2. Of those that a mesh axis runs over, the one named last changes fastest.
Arguments:
- background: bfloat16 [256, 512, 128], P('lat', 'lon'), may hold values from -6 to 6
- diffusivity: float32 [256, 512, 128], P('lat', 'lon'), may hold values from 0.12 to 0.245
- tile_index: int32 [16384, 1], P(('lat', 'lon')), may hold values from 0 to 31; in each aligned block of 512 rows (0 to 511, 512 to 1023, ...) at most 32 rows name the same one
- anchor: int32 [16384], P(('lat', 'lon')), may hold values from 0 to 3968
- weights: float32 [16384, 4], P(('lat', 'lon')), may hold values from 0.2 to 1
- observed: float32 [16384, 128], P(('lat', 'lon')), may hold values from -6 to 6
- accept: int32 [16384, 128], P(('lat', 'lon')), may hold values 0 or 1
- absorb: float32 [128, 128], replicated, may hold values from 0.001 to 0.1
- sensitivity: float32 [128], replicated, may hold values from -0.5 to 0.5
- inverse_variance: float32 [128], replicated, may hold values from 0.25 to 4
Outputs:
- departure: float32 [16384, 128], P(('lat', 'lon'))
- increment: float32 [256, 512, 128], P('lat', 'lon')
The draws below stay inside these ranges and needn't reach their ends.
Inputs may be any that keep to these rules, and one draw needn't show every extreme that they name: `tile_index`: among the 512 footprints of one device no tile is named more than 32 times, a bound that some block reaches.
All inputs are finite; a program needn't handle non-finite values. No bound on the sum of `accept` on one device may be relied on, other than what follows from the above.
Results may differ from the reference program's by a relative error of at most 0.0003.
Values may be sent and summed in bfloat16 or wider, within the bound.
No kernel may reach another device: no remote copies, remote signals or barrier semaphores. Data moves between devices by JAX's collectives and lax.ppermute only.
A program may use at most 64 MiB of HBM per device.

```python
import math
import jax
import jax.numpy as jnp
import numpy as np
from jax import lax

LEV = 128
CHAN = 128
TLAT = 64
TLON = 64
FP_DEV = 512
STEPS = 8
MOST = 32
NLAT = 256
NLON = 512
FOOT = 16384
N_LON = 8
DEVICES = 32


def draw_background(key, part):
    field = jnp.clip(jax.random.normal(key, (NLAT, NLON, LEV), jnp.float32), -6.0, 6.0)
    return field.astype(jnp.bfloat16)


def draw_diffusivity(key, part):
    uniform_draw = jax.random.uniform(key, (NLAT, NLON, LEV), jnp.float32)
    field = 0.12 + 0.125 * uniform_draw
    return field.astype(jnp.float32)


def plant(values, own_key, least, high):
    dims = values.shape
    index_at = [jax.random.randint(jax.random.fold_in(own_key, axis), (), 0, dims[axis]) for axis in range(len(dims))]
    values = values.at[tuple(index_at)].set(least)
    longest = dims.index(max(dims))
    index_at[longest] = (index_at[longest] + 1) % dims[longest]
    return values.at[tuple(index_at)].set(high)


def level_of(stream_key, shape, shards, smallest, top_value):
    level = 1.0
    for axis_at, parts in shards:
        steps = jax.random.uniform(jax.random.fold_in(jax.random.fold_in(stream_key, 6), axis_at), (parts,), jnp.float32, smallest / len(shards), top_value / len(shards))
        level = level * jnp.repeat(jnp.exp(steps), shape[axis_at] // parts).reshape((-1,) + (1,) * (len(shape) - 1 - axis_at))
    return level


def assign_block(stream_key, own, number, rows, count, top, most, slope):
    sequence = jax.random.permutation(stream_key, count)
    crowded, common = portions_of(count, rows * top, most, slope, True), portions_of(count, rows * top, most, slope, False)
    places = jnp.arange(count)

    def named(tallies, turn):
        used = int((tallies > 0).sum())
        fixed = max(1, used // 4)
        passed = fixed + (places - fixed + turn * (used - fixed)) % max(1, count - fixed)
        return jnp.zeros((count,), jnp.int32).at[sequence[jnp.where(places < fixed, places, passed)]].set(jnp.asarray(tallies, jnp.int32))

    tallies = jnp.where(number % 4 == 0, named(crowded, number // 4), named(common, number - number // 4 - 1))
    mixed = jax.random.permutation(jax.random.fold_in(own, 3), count)
    giver, receiver = mixed[0:count // 2 * 2:2], mixed[1:count // 2 * 2:2]
    room = jnp.minimum(tallies[giver] - 1, most - tallies[receiver]) // 2
    room = jnp.where((giver == sequence[0]) | (receiver == sequence[0]) | (tallies[receiver] == 0), 0, jnp.maximum(room, 0))
    passed = jax.random.randint(jax.random.fold_in(own, 4), (count // 2,), 0, 1 << 20) % (room + 1)
    tallies = tallies.at[giver].add(-passed).at[receiver].add(passed)
    members = jnp.searchsorted(jnp.cumsum(tallies), jnp.arange(rows * top), side="right").astype(jnp.int32)
    grid = members.reshape(top, rows).T
    grid = grid[jax.random.permutation(jax.random.fold_in(own, 1), rows)]
    turn = jax.random.randint(jax.random.fold_in(own, 2), (rows, 1), 0, top)
    return jnp.take_along_axis(grid, (jnp.arange(top)[None, :] + turn) % top, axis=1)


def portions_of(number_of, total, most, lean, full):
    weights = [(1 << 20) // math.isqrt(rank ** lean) + 1 for rank in range(1, number_of + 1)]
    largest = most if full else min(most, max(-(-total // number_of), total * weights[0] // sum(weights)))
    least = 1 if total - largest >= number_of - 1 else 0
    given, rest = [largest] + [least] * (number_of - 1), total - largest - least * (number_of - 1)
    while rest > 0:
        candidates = [i for i in range(1, number_of) if given[i] < largest] or [i for i in range(1, number_of) if given[i] < most]
        whole, left = sum([weights[i] for i in candidates]), rest
        for i in candidates:
            extra = min(most - given[i], max(1, left * weights[i] // whole), rest)
            given[i] = given[i] + extra
            rest = rest - extra
    return np.array(given)


def bell_draw(stream_key, dims, width, bound, shards=(), held_as=jnp.bfloat16):
    array = width * jax.random.normal(stream_key, dims, jnp.float32)
    if shards:
        array = array * level_of(stream_key, dims, shards, -0.22, 0.18)
    return jnp.clip(array, -bound, bound).astype(held_as)


def setup_inputs(seed: int = 0) -> dict:
    seeds = jax.random.split(jax.random.key(seed), 11)
    background = draw_background(jax.random.fold_in(seeds[10], 71), 0)
    diffusivity = draw_diffusivity(jax.random.fold_in(seeds[10], 71), 0)
    tile_index_keys = jax.random.split(jax.random.fold_in(seeds[2], 1), FOOT // FP_DEV)
    tile_index_turns = jax.random.permutation(jax.random.fold_in(seeds[2], 3), FOOT // FP_DEV)
    tile_index = jax.vmap(lambda own, number: assign_block(jax.random.fold_in(seeds[2], 2), own, number, FP_DEV, DEVICES, 1, MOST, 1))(tile_index_keys, tile_index_turns).reshape((FOOT, 1))
    anchor = plant(jax.random.randint(seeds[3], (FOOT,), 0, (TLAT - 1) * (TLON - 1)), jax.random.fold_in(seeds[3], 1), 0, ((TLAT - 1) * (TLON - 1)) - 1).astype(jnp.int32)
    weights = jnp.clip(jnp.exp(math.log(1.0) - 1.609438 * jax.random.uniform(seeds[4], (FOOT, 4), jnp.float32) ** level_of(seeds[4], (FOOT, 4), ((0, 32),), -0.2, 0.2)), 0.2, 1.0)
    observed = bell_draw(seeds[5], (FOOT, CHAN), 1.0, 6.0, ((0, 32),), jnp.float32)
    accept = plant((jax.random.randint(seeds[6], (FOOT, CHAN), 0, 4) < 3).astype(jnp.int32), jax.random.fold_in(seeds[6], 1), 0, 1)
    absorb = jnp.clip(jnp.exp(jax.random.uniform(seeds[7], (LEV, CHAN), jnp.float32, math.log(0.001), math.log(0.1))), 0.001, 0.1)
    sensitivity = jnp.clip(jax.random.uniform(seeds[8], (CHAN,), jnp.float32, -0.5, 0.5), -0.5, 0.5)
    inverse_variance = jnp.clip(jnp.exp(jax.random.uniform(seeds[9], (CHAN,), jnp.float32, math.log(0.25), math.log(4.0))), 0.25, 4.0)
    return dict(background=background, diffusivity=diffusivity, tile_index=tile_index, anchor=anchor, weights=weights, observed=observed, accept=accept, absorb=absorb, sensitivity=sensitivity, inverse_variance=inverse_variance)


NEIGHBOURS = ((-1, 0), (1, 0), (0, -1), (0, 1))

def evolve(profile, absorb, sensitivity):
    layer_depth = absorb[None, :, :] * jnp.exp(sensitivity[None, None, :] * profile[:, :, None])
    optical = jnp.cumsum(layer_depth, axis=1)
    transmit = jnp.exp(-optical)
    transmit_above = jnp.concatenate([jnp.ones_like(transmit[:, :1, :]), transmit[:, :-1, :]], axis=1)
    layered = lax.optimization_barrier(jnp.sum(profile[:, :, None] * (transmit_above - transmit), axis=1))
    return layered + profile[:, -1:] * transmit[:, -1, :]

def assess(profile, observed, accept, absorb, sensitivity, inverse_variance):
    evolved, pullback = jax.vjp(lambda prof_in: evolve(prof_in, absorb, sensitivity), profile)
    departure = observed - evolved
    adjoint, = pullback(-(accept.astype(jnp.float32) * inverse_variance[None, :] * departure))
    return (departure, adjoint)

def shift_rows(grid_field, offset):
    zero_row = jnp.zeros_like(grid_field[:1])
    if offset < 0:
        return jnp.concatenate([zero_row, grid_field[:-1]], axis=0)
    return jnp.concatenate([grid_field[1:], zero_row], axis=0)

def relax_global(grid_field, diffusivity):
    summed = grid_field
    for d_row, d_col in NEIGHBOURS:
        if d_row != 0:
            neighbour = shift_rows(grid_field, d_row)
            kappa_near = shift_rows(diffusivity, d_row)
        else:
            neighbour = jnp.roll(grid_field, -d_col, axis=1)
            kappa_near = jnp.roll(diffusivity, -d_col, axis=1)
        summed = summed + 0.5 * (diffusivity + kappa_near) * (neighbour - grid_field)
    return summed

def reference(background, diffusivity, tile_index, anchor, weights, observed, accept, absorb, sensitivity, inverse_variance):
    owner_tile = tile_index[:, 0]
    base_row = owner_tile // N_LON * TLAT + anchor // (TLON - 1)
    base_col = owner_tile % N_LON * TLON + anchor % (TLON - 1)
    row_ids = jnp.stack([base_row, base_row, base_row + 1, base_row + 1], axis=1)
    col_ids = jnp.stack([base_col, base_col + 1, base_col, base_col + 1], axis=1)
    column_ids = (row_ids * NLON + col_ids).astype(jnp.int32)
    shares = weights / lax.optimization_barrier(jnp.sum(weights, axis=1, keepdims=True))
    flat_bg = background.reshape(NLAT * NLON, LEV)
    profile = lax.optimization_barrier(jnp.sum(shares[:, :, None] * flat_bg[column_ids].astype(jnp.float32), axis=1))
    block_count = FOOT // 1024
    departure, adjoint = lax.map(lambda packed: assess(packed[0], packed[1], packed[2], absorb, sensitivity, inverse_variance), (profile.reshape(block_count, 1024, LEV), observed.reshape(block_count, 1024, CHAN), accept.reshape(block_count, 1024, CHAN)))
    departure = departure.reshape(FOOT, CHAN)
    adjoint = adjoint.reshape(FOOT, LEV)
    adjoint_terms = -(shares[:, :, None] * adjoint[:, None, :])
    increment = jnp.zeros((NLAT * NLON, LEV), jnp.float32).at[column_ids.reshape(-1)].add(adjoint_terms.reshape(FOOT * 4, LEV))
    grid_field = increment.reshape(NLAT, NLON, LEV)
    for repeat_index in range(STEPS):
        grid_field = relax_global(grid_field, diffusivity)
    return (departure, grid_field)
```

```python
import functools
import math

import jax
import jax.numpy as jnp
from jax import lax
from jax.experimental import pallas as pl
from jax.experimental.pallas import tpu as pltpu
from jax.sharding import PartitionSpec as P

STEPS = 8
REJECTED = 64.0
META = 8
LOG2E = math.log2(math.e)
LN2 = math.log(2.0)
VMEM_LIMIT = 60 * 1024 * 1024


def thirds(x):
    high = x.astype(jnp.bfloat16)
    rest = x - high.astype(jnp.float32)
    mid = rest.astype(jnp.bfloat16)
    low = (rest - mid.astype(jnp.float32)).astype(jnp.bfloat16)
    return high, mid, low


def dot_f32(a, b, contract):
    return lax.dot_general(a, b, (contract, ((), ())), preferred_element_type=jnp.float32)


def iota(shape, dim):
    return lax.broadcasted_iota(jnp.int32, shape, dim)


def pack_kernel(
    dev_count, capacity, tile_cols, lane_ref, tile_ref, anchor_ref, weights_ref, observed_ref,
    accept_ref, send_ref, slot_ref, vals_ref
):
    foot_count, channels = observed_ref.shape
    bf16 = jnp.bfloat16
    tile = tile_ref[...]
    onehot = jnp.where(iota((dev_count, foot_count), 0) == tile, 1.0, 0.0)
    earlier = jnp.where(
        iota((foot_count, foot_count), 0) < iota((foot_count, foot_count), 1), 1.0, 0.0
    ).astype(bf16)
    before = dot_f32(onehot.astype(bf16), earlier, ((1,), (0,)))
    rank = jnp.sum(before * onehot, axis=0, keepdims=True).astype(jnp.int32)
    slot = tile * capacity + rank
    slot_ref[...] = slot

    chosen = jnp.where(accept_ref[...] != 0, observed_ref[...], REJECTED)
    parts = thirds(chosen)
    per_chunk = max(1, 128 // capacity)
    chunk = per_chunk * capacity
    for start in range(0, dev_count, per_chunk):
        place = jnp.where(
            iota((chunk, foot_count), 0) + start * capacity == slot, 1.0, 0.0
        ).astype(bf16)
        rows = [dot_f32(place, part, ((1,), (0,))) for part in parts]
        rows = (rows[0] + rows[1]) + rows[2]
        send_ref[start : start + per_chunk, :capacity, :] = rows.reshape(
            per_chunk, capacity, channels
        )

    anchor = anchor_ref[...]
    line = jnp.floor((anchor.astype(jnp.float32) + 0.5) * (1.0 / (tile_cols - 1)))
    base = anchor.astype(jnp.float32) + line
    weights = weights_ref[...]
    shares = weights / jnp.sum(weights, axis=0, keepdims=True)
    meta = jnp.concatenate(
        [base, shares, jnp.zeros((META - 5, foot_count), jnp.float32)], axis=0
    )
    for dev in range(dev_count):
        vals_ref[dev * META : (dev + 1) * META, :] = jnp.where(tile == dev, meta, 0.0)
    lanes = jnp.where(
        iota((channels, foot_count), 0) == rank + lane_ref[0], 1.0, 0.0
    ).astype(bf16)
    rows = [dot_f32(part, lanes, ((1,), (1,))) for part in thirds(vals_ref[...])]
    rows = (rows[0] + rows[1]) + rows[2]
    send_ref[:, capacity:, :] = rows.reshape(dev_count, META, channels)


def column_kernel(
    capacity, halo, recv_ref, recv_any, background_ref, absorb_ref, sensitivity_ref, inverse_ref,
    evolved_ref, field_ref, top_ref, bottom_ref, left_ref, right_ref,
    base_ref, sem, cells_ref, absorb_b, slope_b, inverse_b, taken_ref, profile_ref, rise_ref,
    obs_ref, evo_ref, depth_ref, trans_ref, weigh_ref, slant_ref, sums_ref
):
    dev_count = recv_ref.shape[0]
    tile_rows, tile_cols, levels = background_ref.shape
    cells = tile_rows * tile_cols
    channels = absorb_ref.shape[1]
    lanes = 128
    group = lanes // capacity
    blocks = dev_count // group
    slots = dev_count * capacity
    wide = 32

    copy = pltpu.make_async_copy(recv_any.at[:, capacity, :], base_ref, sem)
    copy.start()

    cells_ref[...] = background_ref[...].reshape(cells, levels).astype(jnp.float32)
    slope_b[...] = jnp.broadcast_to(sensitivity_ref[...] * LOG2E, (lanes, channels)).T
    inverse_b[...] = jnp.broadcast_to(inverse_ref[...], (lanes, channels)).T

    def spread(i, carry):
        turned = (absorb_ref[pl.ds(i * 8, 8), :] * LOG2E).T
        for u in range(8):
            absorb_b[i * 8 + u] = jnp.broadcast_to(turned[:, u : u + 1], (channels, lanes))
        return carry

    lax.fori_loop(0, levels // 8, spread, 0)
    sums_ref[...] = jnp.zeros_like(sums_ref)
    copy.wait()

    def gather(i, carry):
        for u in range(8):
            slot = i * 8 + u
            base = base_ref[lax.div(i * 8, capacity), lax.rem(i * 8, lanes) + u].astype(jnp.int32)
            for k, step in enumerate((0, 1, tile_cols, tile_cols + 1)):
                taken_ref[k, pl.ds(slot, 1), :] = cells_ref[pl.ds(base + step, 1), :]
        return carry

    lax.fori_loop(0, slots // 8, gather, 0)

    def block(f, carry):
        first = pl.multiple_of(f * lanes, lanes)
        mine = recv_ref[pl.ds(f * group, group)]
        shares = jnp.sum(mine[:, capacity:, :], axis=0)
        obs_ref[...] = mine[:, :capacity, :].reshape(lanes, channels).T
        profile = shares[1:2] * taken_ref[0, pl.ds(first, lanes), :].T
        for k in range(1, 4):
            profile = profile + shares[k + 1 : k + 2] * taken_ref[k, pl.ds(first, lanes), :].T
        profile_ref[...] = profile
        rise_ref[0 : levels - 1, :] = profile[1:] - profile[:-1]
        rise_ref[levels - 1 : levels, :] = jnp.zeros((1, lanes), jnp.float32)
        weigh_ref[...] = jnp.zeros_like(weigh_ref)
        slant_ref[...] = jnp.zeros_like(slant_ref)

        def some_channels(c, carry):
            at = pl.multiple_of(c * wide, wide)
            slope = slope_b[pl.ds(at, wide), :]

            def down(i, state):
                path, total = state
                for u in range(8):
                    level = i * 8 + u
                    depth = absorb_b[level, pl.ds(at, wide), :] * jnp.exp2(
                        slope * profile_ref[pl.ds(level, 1), :]
                    )
                    path = path - depth
                    trans = jnp.exp2(path)
                    total = total + trans * rise_ref[pl.ds(level, 1), :]
                    depth_ref[level] = depth
                    trans_ref[level] = trans
                return path, total

            zero = jnp.zeros((wide, lanes), jnp.float32)
            _, total = lax.fori_loop(0, levels // 8, down, (zero, zero))
            evolved = total + profile_ref[0:1, :]
            evo_ref[pl.ds(at, wide), :] = evolved
            obs = obs_ref[pl.ds(at, wide), :]
            force = jnp.where(
                obs < 0.5 * REJECTED, inverse_b[pl.ds(at, wide), :] * (obs - evolved), 0.0
            )
            pull = force * (slope * (LN2 * LN2))

            def up(i, above):
                for u in range(8):
                    level = levels - 1 - (i * 8 + u)
                    trans = trans_ref[level]
                    above = above + (pull * trans) * rise_ref[pl.ds(level, 1), :]
                    weigh = force * trans
                    slant = depth_ref[level] * above
                    weigh_ref[level] += jnp.sum(weigh.reshape(wide // 8, 8, lanes), axis=0)
                    slant_ref[level] += jnp.sum(slant.reshape(wide // 8, 8, lanes), axis=0)
                return above

            lax.fori_loop(0, levels // 8, up, zero)
            return carry

        lax.fori_loop(0, channels // wide, some_channels, 0)
        evolved_ref[pl.ds(f * group, group)] = evo_ref[...].T.reshape(group, capacity, channels)
        weigh = jnp.sum(weigh_ref[...], axis=1)
        slant = jnp.sum(slant_ref[...], axis=1)
        force_all = jnp.zeros((1, lanes), jnp.float32)
        for c in range(channels // wide):
            obs = obs_ref[c * wide : (c + 1) * wide, :]
            force = jnp.where(
                obs < 0.5 * REJECTED,
                inverse_b[c * wide : (c + 1) * wide, :]
                * (obs - evo_ref[c * wide : (c + 1) * wide, :]),
                0.0,
            )
            force_all = force_all + jnp.sum(force, axis=0, keepdims=True)
        over = jnp.concatenate([force_all, weigh[:-1]], axis=0)
        under = jnp.concatenate([weigh[:-1], jnp.zeros((1, lanes), jnp.float32)], axis=0)
        push = (over - under) - slant
        for k in range(4):
            taken_ref[k, pl.ds(first, lanes), :] = (shares[k + 1 : k + 2] * push).T
        return carry

    lax.fori_loop(0, blocks, block, 0)

    def scatter(i, carry):
        for u in range(8):
            slot = i * 8 + u
            base = base_ref[lax.div(i * 8, capacity), lax.rem(i * 8, lanes) + u].astype(jnp.int32)
            for k, step in enumerate((0, 1, tile_cols, tile_cols + 1)):
                sums_ref[k, pl.ds(base + step, 1), :] += taken_ref[k, pl.ds(slot, 1), :]
        return carry

    lax.fori_loop(0, slots // 8, scatter, 0)

    field = (sums_ref[0] + sums_ref[1]) + (sums_ref[2] + sums_ref[3])
    field = field.reshape(tile_rows, tile_cols, levels)
    field_ref[...] = field
    top_ref[...] = field[:halo]
    bottom_ref[...] = field[tile_rows - halo :]
    left_ref[...] = field[:, :halo]
    right_ref[...] = field[:, tile_cols - halo :]


def relax_kernel(
    halo, inside_ref, field_refs, kappa_refs, out_ref, first_ref, second_ref, east_ref, south_ref
):
    tile_rows, tile_cols, levels = out_ref.shape
    height, breadth = tile_rows + 2 * halo, tile_cols + 2 * halo

    def lay(target, refs):
        centre, north, south, west, east, wests, easts = refs
        low, high = slice(0, halo), slice(halo, 2 * halo)
        mid_r, mid_c = slice(halo, halo + tile_rows), slice(halo, halo + tile_cols)
        end_r, end_c = slice(halo + tile_rows, height), slice(halo + tile_cols, breadth)
        target[mid_r, mid_c] = centre[...]
        target[low, mid_c] = north[...]
        target[end_r, mid_c] = south[...]
        target[mid_r, low] = west[...]
        target[mid_r, end_c] = east[...]
        target[low, low] = wests[low]
        target[end_r, low] = wests[high]
        target[low, end_c] = easts[low]
        target[end_r, end_c] = easts[high]

    lay(first_ref, kappa_refs)

    def edges(i, carry):
        here = first_ref[i]
        east_ref[i] = 0.5 * (here + pltpu.roll(here, breadth - 1, 0))
        south_ref[i] = 0.5 * (here + first_ref[i + 1])
        return carry

    lax.fori_loop(0, height - 1, edges, 0)
    lay(first_ref, field_refs)

    source, target = first_ref, second_ref
    for step in range(1, halo + 1):
        last = step == halo

        def row(i, carry, scale=None, source=source, target=target, last=last):
            here, from_north = carry
            below = source[i + 1]
            to_east = east_ref[i] * (pltpu.roll(here, breadth - 1, 0) - here)
            from_south = south_ref[i] * (below - here)
            value = here + (to_east - pltpu.roll(to_east, 1, 0)) + (from_south - from_north)
            if scale is not None:
                value = value * scale
            if last:
                out_ref[i - halo] = value[halo : halo + tile_cols]
            else:
                target[i] = value
            return below, from_south

        here = source[step]
        carry = (here, south_ref[step - 1] * (here - source[step - 1]))
        carry = lax.fori_loop(
            step, halo, functools.partial(row, scale=inside_ref[0]), carry
        )
        carry = lax.fori_loop(halo, halo + tile_rows, row, carry)
        lax.fori_loop(
            halo + tile_rows, height - step, functools.partial(row, scale=inside_ref[1]), carry
        )
        if step == 1:
            target[0] = source[0]
            target[height - 1] = source[height - 1]
        source, target = target, source


def depart_kernel(slot_ref, evolved_ref, observed_ref, out_ref):
    foot_count, _ = observed_ref.shape
    slots = evolved_ref.shape[0]
    slot = slot_ref[...]
    parts = thirds(evolved_ref[...])
    chosen = jnp.where(iota((slots, foot_count), 0) == slot, 1.0, 0.0).astype(jnp.bfloat16)
    rows = [dot_f32(chosen, part, ((0,), (0,))) for part in parts]
    out_ref[...] = observed_ref[...] - ((rows[0] + rows[1]) + rows[2])


def vmem():
    return pl.BlockSpec(memory_space=pltpu.VMEM)


def smem():
    return pl.BlockSpec(memory_space=pltpu.SMEM)


def params():
    return pltpu.CompilerParams(vmem_limit_bytes=VMEM_LIMIT)


def cost(flops, transcendentals, moved):
    return pl.CostEstimate(flops=flops, transcendentals=transcendentals, bytes_accessed=moved)


def neighbours(axis, periodic):
    count = lax.axis_size(axis)
    forward = [(i, i + 1) for i in range(count - 1)]
    if periodic:
        forward.append((count - 1, 0))
    return forward, [(target, source) for source, target in forward]


def halos(top, bottom, left, right):
    lat_up, lat_down = neighbours("lat", False)
    lon_up, lon_down = neighbours("lon", True)
    halo = top.shape[0]
    west = lax.ppermute(right, "lon", lon_up)
    east = lax.ppermute(left, "lon", lon_down)
    north = lax.ppermute(bottom, "lat", lat_up)
    south = lax.ppermute(top, "lat", lat_down)
    wests = lax.ppermute(
        jnp.concatenate([north[:, -halo:], south[:, -halo:]], axis=0), "lon", lon_up
    )
    easts = lax.ppermute(
        jnp.concatenate([north[:, :halo], south[:, :halo]], axis=0), "lon", lon_down
    )
    return north, south, west, east, wests, easts


def local(
    background, diffusivity, tile_index, anchor, weights, observed, accept, absorb, sensitivity,
    inverse_variance
):
    f32 = jnp.float32
    lat_count = lax.axis_size("lat")
    lon_count = lax.axis_size("lon")
    dev_count = lat_count * lon_count
    foot_count, channels = observed.shape
    capacity = max(2, 2 * foot_count // dev_count)
    tile_rows, tile_cols, levels = background.shape
    slots = dev_count * capacity
    lanes = 128
    group = lanes // capacity
    cells = tile_rows * tile_cols
    halo = STEPS

    kappa_halos = halos(
        diffusivity[:halo], diffusivity[-halo:], diffusivity[:, :halo], diffusivity[:, -halo:]
    )

    me = lax.axis_index("lat") * lon_count + lax.axis_index("lon")
    lane = (lax.rem(me, group) * capacity).astype(jnp.int32).reshape(1)
    send, slot = pl.pallas_call(
        functools.partial(pack_kernel, dev_count, capacity, tile_cols),
        out_shape=(
            jax.ShapeDtypeStruct((dev_count, capacity + META, channels), f32),
            jax.ShapeDtypeStruct((1, foot_count), jnp.int32),
        ),
        in_specs=[smem()] + [vmem()] * 5,
        out_specs=(vmem(), vmem()),
        scratch_shapes=[pltpu.VMEM((dev_count * META, foot_count), f32)],
        compiler_params=params(),
        cost_estimate=cost(2 * slots * foot_count * channels * 3, 0, 4 * slots * channels * 3),
        name="pack",
    )(
        lane, tile_index.reshape(1, foot_count), anchor.reshape(1, foot_count), weights.T,
        observed, accept
    )
    recv = lax.all_to_all(send, ("lat", "lon"), split_axis=0, concat_axis=0, tiled=True)

    wide = 32
    evolved, field, top, bottom, left, right = pl.pallas_call(
        functools.partial(column_kernel, capacity, halo),
        out_shape=(
            jax.ShapeDtypeStruct((dev_count, capacity, channels), f32),
            jax.ShapeDtypeStruct((tile_rows, tile_cols, levels), f32),
            jax.ShapeDtypeStruct((halo, tile_cols, levels), f32),
            jax.ShapeDtypeStruct((halo, tile_cols, levels), f32),
            jax.ShapeDtypeStruct((tile_rows, halo, levels), f32),
            jax.ShapeDtypeStruct((tile_rows, halo, levels), f32),
        ),
        in_specs=[vmem(), pl.BlockSpec(memory_space=pl.ANY)] + [vmem()] * 4,
        out_specs=(vmem(),) * 6,
        scratch_shapes=[
            pltpu.SMEM((dev_count, channels), f32),
            pltpu.SemaphoreType.DMA,
            pltpu.VMEM((cells, levels), f32),
            pltpu.VMEM((levels, channels, lanes), f32),
            pltpu.VMEM((channels, lanes), f32),
            pltpu.VMEM((channels, lanes), f32),
            pltpu.VMEM((4, slots, levels), f32),
            pltpu.VMEM((levels, lanes), f32),
            pltpu.VMEM((levels, lanes), f32),
            pltpu.VMEM((channels, lanes), f32),
            pltpu.VMEM((channels, lanes), f32),
            pltpu.VMEM((levels, wide, lanes), f32),
            pltpu.VMEM((levels, wide, lanes), f32),
            pltpu.VMEM((levels, 8, lanes), f32),
            pltpu.VMEM((levels, 8, lanes), f32),
            pltpu.VMEM((4, cells, levels), f32),
        ],
        compiler_params=params(),
        cost_estimate=cost(
            14 * slots * levels * channels, 2 * slots * levels * channels, 12 * cells * levels
        ),
        name="column",
    )(
        recv, recv, background, absorb, sensitivity.reshape(1, channels),
        inverse_variance.reshape(1, channels)
    )

    returned = lax.all_to_all(evolved, ("lat", "lon"), split_axis=0, concat_axis=0, tiled=True)
    field_halos = halos(top, bottom, left, right)

    departure = pl.pallas_call(
        depart_kernel,
        out_shape=jax.ShapeDtypeStruct((foot_count, channels), f32),
        in_specs=[vmem()] * 3,
        out_specs=vmem(),
        compiler_params=params(),
        cost_estimate=cost(2 * slots * foot_count * channels * 3, 0, 4 * slots * channels * 2),
        name="depart",
    )(slot, returned.reshape(slots, channels), observed)

    lat_at = lax.axis_index("lat")
    inside = jnp.stack([lat_at > 0, lat_at < lat_count - 1]).astype(f32)
    height, breadth = tile_rows + 2 * halo, tile_cols + 2 * halo

    def relax_body(inside_ref, *refs):
        relax_kernel(halo, inside_ref, refs[:7], refs[7:14], *refs[14:])

    increment = pl.pallas_call(
        relax_body,
        out_shape=jax.ShapeDtypeStruct((tile_rows, tile_cols, levels), f32),
        in_specs=[smem()] + [vmem()] * 14,
        out_specs=vmem(),
        scratch_shapes=[pltpu.VMEM((height, breadth, levels), f32)] * 4,
        compiler_params=params(),
        cost_estimate=cost(10 * STEPS * height * breadth * levels, 0, 16 * cells * levels),
        name="relax",
    )(inside, field, *field_halos, diffusivity, *kappa_halos)
    return (departure, increment)


def solution(mesh):
    in_specs = (
        P("lat", "lon", None),
        P("lat", "lon", None),
        P(("lat", "lon"), None),
        P(("lat", "lon")),
        P(("lat", "lon"), None),
        P(("lat", "lon"), None),
        P(("lat", "lon"), None),
        P(),
        P(),
        P(),
    )
    out_specs = (P(("lat", "lon"), None), P("lat", "lon", None))
    return jax.shard_map(local, mesh=mesh, in_specs=in_specs, out_specs=out_specs, check_vma=False)
```

```python
import functools
import math

import jax
import jax.numpy as jnp
from jax import lax
from jax.experimental import pallas as pl
from jax.experimental.pallas import tpu as pltpu
from jax.sharding import PartitionSpec as P

STEPS = 8
REJECTED = 64.0
META = 8
LOG2E = math.log2(math.e)
LN2 = math.log(2.0)
MIB = 1024 * 1024
UNROLL = 16


def thirds(x):
    high = x.astype(jnp.bfloat16)
    rest = x - high.astype(jnp.float32)
    mid = rest.astype(jnp.bfloat16)
    low = (rest - mid.astype(jnp.float32)).astype(jnp.bfloat16)
    return high, mid, low


def dot_f32(a, b, contract):
    return lax.dot_general(a, b, (contract, ((), ())), preferred_element_type=jnp.float32)


def iota(shape, dim):
    return lax.broadcasted_iota(jnp.int32, shape, dim)


def pack_kernel(
    dev_count, capacity, tile_cols, lane_ref, tile_ref, anchor_ref, weights_ref, observed_ref,
    accept_ref, send_ref, slot_ref, vals_ref
):
    foot_count, channels = observed_ref.shape
    bf16 = jnp.bfloat16
    tile = tile_ref[...]
    onehot = jnp.where(iota((dev_count, foot_count), 0) == tile, 1.0, 0.0)
    earlier = jnp.where(
        iota((foot_count, foot_count), 0) < iota((foot_count, foot_count), 1), 1.0, 0.0
    ).astype(bf16)
    before = dot_f32(onehot.astype(bf16), earlier, ((1,), (0,)))
    rank = jnp.sum(before * onehot, axis=0, keepdims=True).astype(jnp.int32)
    slot = tile * capacity + rank
    slot_ref[...] = slot

    chosen = jnp.where(accept_ref[...] != 0, observed_ref[...], REJECTED)
    parts = thirds(chosen)
    per_chunk = max(1, 128 // capacity)
    chunk = per_chunk * capacity
    for start in range(0, dev_count, per_chunk):
        place = jnp.where(
            iota((chunk, foot_count), 0) + start * capacity == slot, 1.0, 0.0
        ).astype(bf16)
        rows = [dot_f32(place, part, ((1,), (0,))) for part in parts]
        rows = (rows[0] + rows[1]) + rows[2]
        send_ref[start : start + per_chunk, :capacity, :] = rows.reshape(
            per_chunk, capacity, channels
        )

    anchor = anchor_ref[...]
    line = jnp.floor((anchor.astype(jnp.float32) + 0.5) * (1.0 / (tile_cols - 1)))
    base = anchor.astype(jnp.float32) + line
    weights = weights_ref[...]
    shares = weights / jnp.sum(weights, axis=0, keepdims=True)
    meta = jnp.concatenate(
        [base, shares, jnp.zeros((META - 5, foot_count), jnp.float32)], axis=0
    )
    for dev in range(dev_count):
        vals_ref[dev * META : (dev + 1) * META, :] = jnp.where(tile == dev, meta, 0.0)
    lanes = jnp.where(
        iota((channels, foot_count), 0) == rank + lane_ref[0], 1.0, 0.0
    ).astype(bf16)
    rows = [dot_f32(part, lanes, ((1,), (1,))) for part in thirds(vals_ref[...])]
    rows = (rows[0] + rows[1]) + rows[2]
    send_ref[:, capacity:, :] = rows.reshape(dev_count, META, channels)


def column_kernel(
    capacity, halo, recv_ref, background_ref, absorb_ref, sensitivity_ref, inverse_ref,
    evolved_ref, field_ref, top_ref, bottom_ref, left_ref, right_ref,
    base_ref, sem, cells_ref, absorb_b, slope_b, inverse_b, taken_ref, terms_ref, profile_ref,
    rise_ref, obs_ref, evo_ref, main_ref, side_ref, push_ref, sums_ref
):
    dev_count = recv_ref.shape[0]
    tile_rows, tile_cols, levels = background_ref.shape
    cells = tile_rows * tile_cols
    channels = absorb_ref.shape[1]
    lanes = 128
    group = lanes // capacity
    blocks = dev_count // group
    wide = main_ref.shape[1]
    per_loop = UNROLL * wide * lanes // (levels * channels)
    corners = (0, 1, tile_cols, tile_cols + 1)

    copy = pltpu.make_async_copy(recv_ref.at[:, capacity, :], base_ref, sem)
    copy.start()

    cells_ref[...] = background_ref[...].reshape(cells, levels).astype(jnp.float32)
    slope_b[...] = jnp.broadcast_to(sensitivity_ref[...] * LOG2E, (lanes, channels)).T
    inverse_b[...] = jnp.broadcast_to(inverse_ref[...], (lanes, channels)).T

    def spread(i, carry):
        turned = (absorb_ref[pl.ds(i * 8, 8), :] * LOG2E).T
        for u in range(8):
            absorb_b[i * 8 + u] = jnp.broadcast_to(turned[:, u : u + 1], (channels, lanes))
        return carry

    lax.fori_loop(0, levels // 8, spread, 0)
    sums_ref[...] = jnp.zeros_like(sums_ref)
    terms_ref[...] = jnp.zeros_like(terms_ref)
    copy.wait()

    def base_of(f, at):
        return base_ref[f * group + lax.div(at, capacity), at].astype(jnp.int32)

    def gather(f, at):
        base = base_of(f, at)
        for k, step in enumerate(corners):
            taken_ref[k, pl.ds(at, 1), :] = cells_ref[pl.ds(base + step, 1), :]

    def scatter(f, at):
        base = base_of(f, at)
        for k, step in enumerate(corners):
            sums_ref[k, pl.ds(base + step, 1), :] += terms_ref[k, pl.ds(at, 1), :]

    def gather_first(i, carry):
        for u in range(8):
            gather(0, i * 8 + u)
        return carry

    lax.fori_loop(0, lanes // 8, gather_first, 0)

    def block(f, carry):
        before = jnp.maximum(f - 1, 0)
        after = jnp.minimum(f + 1, blocks - 1)
        mine = recv_ref[pl.ds(f * group, group)]
        shares = jnp.sum(mine[:, capacity:, :], axis=0)
        obs_ref[...] = mine[:, :capacity, :].reshape(lanes, channels).T
        profile = shares[1:2] * taken_ref[0].T
        for k in range(1, 4):
            profile = profile + shares[k + 1 : k + 2] * taken_ref[k].T
        profile_ref[...] = profile
        rise_ref[0 : levels - 1, :] = profile[1:] - profile[:-1]
        rise_ref[levels - 1 : levels, :] = jnp.zeros((1, lanes), jnp.float32)
        push_ref[...] = jnp.zeros_like(push_ref)

        def some_channels(c, carry):
            at = pl.multiple_of(c * wide, wide)
            slope = slope_b[pl.ds(at, wide), :]
            scale = slope * (LN2 * LN2)

            def down(i, state):
                path, total, above = state
                for u in range(UNROLL):
                    level = i * UNROLL + u
                    depth = absorb_b[level, pl.ds(at, wide), :] * jnp.exp2(
                        slope * profile_ref[pl.ds(level, 1), :]
                    )
                    path = path - depth
                    trans = jnp.exp2(path)
                    side = depth * scale
                    side_ref[level] = side
                    main_ref[level] = (above - trans) + side * total
                    total = total + trans * rise_ref[pl.ds(level, 1), :]
                    above = trans
                for u in range(per_loop):
                    scatter(before, (c * (levels // UNROLL) + i) * per_loop + u)
                return path, total, above

            zero = jnp.zeros((wide, lanes), jnp.float32)
            _, total, last = lax.fori_loop(0, levels // UNROLL, down, (zero, zero, zero + 1.0))
            main_ref[levels - 1] += last
            evolved = total + profile_ref[0:1, :]
            evo_ref[pl.ds(at, wide), :] = evolved
            obs = obs_ref[pl.ds(at, wide), :]
            force = jnp.where(
                obs < 0.5 * REJECTED, inverse_b[pl.ds(at, wide), :] * (obs - evolved), 0.0
            )

            def up(i, carry):
                for u in range(UNROLL):
                    level = i * UNROLL + u
                    push = force * (main_ref[level] - total * side_ref[level])
                    push_ref[pl.ds(pl.multiple_of(level * 8, 8), 8), :] += jnp.sum(
                        push.reshape(wide // 8, 8, lanes), axis=0
                    )
                for u in range(per_loop):
                    gather(after, (c * (levels // UNROLL) + i) * per_loop + u)
                return carry

            lax.fori_loop(0, levels // UNROLL, up, 0)
            return carry

        lax.fori_loop(0, channels // wide, some_channels, 0)
        evolved_ref[pl.ds(f * group, group)] = evo_ref[...].T.reshape(group, capacity, channels)
        push = push_ref[pl.ds(0, levels, stride=8), :]
        for u in range(1, 8):
            push = push + push_ref[pl.ds(u, levels, stride=8), :]
        for k in range(4):
            terms_ref[k] = (shares[k + 1 : k + 2] * push).T
        return carry

    lax.fori_loop(0, blocks, block, 0)

    def scatter_last(i, carry):
        for u in range(8):
            scatter(blocks - 1, i * 8 + u)
        return carry

    lax.fori_loop(0, lanes // 8, scatter_last, 0)

    field = (sums_ref[0] + sums_ref[1]) + (sums_ref[2] + sums_ref[3])
    field = field.reshape(tile_rows, tile_cols, levels)
    field_ref[...] = field
    top_ref[...] = field[:halo]
    bottom_ref[...] = field[tile_rows - halo :]
    left_ref[...] = field[:, :halo]
    right_ref[...] = field[:, tile_cols - halo :]


def lay(halo, target, refs):
    centre, north, south, west, east, wests, easts = refs
    tile_rows, tile_cols, _ = centre.shape
    height, breadth = tile_rows + 2 * halo, tile_cols + 2 * halo
    low, high = slice(0, halo), slice(halo, 2 * halo)
    mid_r, mid_c = slice(halo, halo + tile_rows), slice(halo, halo + tile_cols)
    end_r, end_c = slice(halo + tile_rows, height), slice(halo + tile_cols, breadth)
    target[mid_r, mid_c] = centre[...]
    target[low, mid_c] = north[...]
    target[end_r, mid_c] = south[...]
    target[mid_r, low] = west[...]
    target[mid_r, end_c] = east[...]
    target[low, low] = wests[low]
    target[end_r, low] = wests[high]
    target[low, end_c] = easts[low]
    target[end_r, end_c] = easts[high]


def interleave(plain_ref, target_ref):
    stretch = target_ref.shape[1]

    def row(i, carry):
        for t in range(stretch):
            target_ref[i, t] = plain_ref[i, pl.ds(t, 8, stride=stretch), :]
        return carry

    lax.fori_loop(0, plain_ref.shape[0], row, 0)


def eastward(x):
    return jnp.concatenate([x[1:], pltpu.roll(x[0], 7, 0)[None]], axis=0)


def westward(x):
    return jnp.concatenate([pltpu.roll(x[-1], 1, 0)[None], x[:-1]], axis=0)


def edges_kernel(halo, kappa_refs, east_ref, south_ref, plain_ref, kappa_ref):
    lay(halo, plain_ref, kappa_refs)
    interleave(plain_ref, kappa_ref)
    height = plain_ref.shape[0]

    def edges(i, carry):
        here = kappa_ref[i]
        east_ref[i] = 0.5 * (here + eastward(here))
        south_ref[i] = 0.5 * (here + kappa_ref[jnp.minimum(i + 1, height - 1)])
        return carry

    lax.fori_loop(0, height, edges, 0)


def relax_kernel(
    halo, inside_ref, field_refs, east_ref, south_ref, out_ref, plain_ref, first_ref, second_ref
):
    tile_rows, tile_cols, levels = out_ref.shape
    height = tile_rows + 2 * halo
    stretch = first_ref.shape[1]
    lay(halo, plain_ref, field_refs)
    interleave(plain_ref, first_ref)

    source, target = first_ref, second_ref
    for step in range(1, halo + 1):
        last = step == halo

        def row(i, carry, scale=None, source=source, target=target, last=last):
            here, from_north = carry
            below = source[i + 1]
            to_east = east_ref[i] * (eastward(here) - here)
            from_south = south_ref[i] * (below - here)
            value = here + (to_east - westward(to_east)) + (from_south - from_north)
            if scale is not None:
                value = value * scale
            if last:
                for t in range(stretch):
                    plain_ref[i, pl.ds(t, 8, stride=stretch), :] = value[t]
            else:
                target[i] = value
            return below, from_south

        here = source[step]
        carry = (here, south_ref[step - 1] * (here - source[step - 1]))
        carry = lax.fori_loop(
            step, halo, functools.partial(row, scale=inside_ref[0]), carry, unroll=True
        )
        carry = lax.fori_loop(halo, halo + tile_rows, row, carry, unroll=4)
        lax.fori_loop(
            halo + tile_rows, height - step, functools.partial(row, scale=inside_ref[1]), carry,
            unroll=True,
        )
        source, target = target, source
    out_ref[...] = plain_ref[halo : halo + tile_rows, halo : halo + tile_cols, :]


def depart_kernel(slot_ref, evolved_ref, observed_ref, out_ref):
    foot_count, _ = observed_ref.shape
    slots = evolved_ref.shape[0]
    slot = slot_ref[...]
    parts = thirds(evolved_ref[...])
    chosen = jnp.where(iota((slots, foot_count), 0) == slot, 1.0, 0.0).astype(jnp.bfloat16)
    rows = [dot_f32(chosen, part, ((0,), (0,))) for part in parts]
    out_ref[...] = observed_ref[...] - ((rows[0] + rows[1]) + rows[2])


def vmem():
    return pl.BlockSpec(memory_space=pltpu.VMEM)


def smem():
    return pl.BlockSpec(memory_space=pltpu.SMEM)


def params(mib):
    return pltpu.CompilerParams(vmem_limit_bytes=mib * MIB)


def cost(flops, transcendentals, moved):
    return pl.CostEstimate(flops=flops, transcendentals=transcendentals, bytes_accessed=moved)


def neighbours(axis, periodic):
    count = lax.axis_size(axis)
    forward = [(i, i + 1) for i in range(count - 1)]
    if periodic:
        forward.append((count - 1, 0))
    return forward, [(target, source) for source, target in forward]


def halos(top, bottom, left, right):
    lat_up, lat_down = neighbours("lat", False)
    lon_up, lon_down = neighbours("lon", True)
    halo = top.shape[0]
    west = lax.ppermute(right, "lon", lon_up)
    east = lax.ppermute(left, "lon", lon_down)
    north = lax.ppermute(bottom, "lat", lat_up)
    south = lax.ppermute(top, "lat", lat_down)
    wests = lax.ppermute(
        jnp.concatenate([north[:, -halo:], south[:, -halo:]], axis=0), "lon", lon_up
    )
    easts = lax.ppermute(
        jnp.concatenate([north[:, :halo], south[:, :halo]], axis=0), "lon", lon_down
    )
    return north, south, west, east, wests, easts


def local(
    background, diffusivity, tile_index, anchor, weights, observed, accept, absorb, sensitivity,
    inverse_variance
):
    f32 = jnp.float32
    lat_count = lax.axis_size("lat")
    lon_count = lax.axis_size("lon")
    dev_count = lat_count * lon_count
    foot_count, channels = observed.shape
    capacity = max(2, 2 * foot_count // dev_count)
    tile_rows, tile_cols, levels = background.shape
    slots = dev_count * capacity
    lanes = 128
    group = lanes // capacity
    cells = tile_rows * tile_cols
    halo = STEPS

    me = lax.axis_index("lat") * lon_count + lax.axis_index("lon")
    lane = (lax.rem(me, group) * capacity).astype(jnp.int32).reshape(1)
    send, slot = pl.pallas_call(
        functools.partial(pack_kernel, dev_count, capacity, tile_cols),
        out_shape=(
            jax.ShapeDtypeStruct((dev_count, capacity + META, channels), f32),
            jax.ShapeDtypeStruct((1, foot_count), jnp.int32),
        ),
        in_specs=[smem()] + [vmem()] * 5,
        out_specs=(vmem(), vmem()),
        scratch_shapes=[pltpu.VMEM((dev_count * META, foot_count), f32)],
        compiler_params=params(16),
        cost_estimate=cost(2 * slots * foot_count * channels * 3, 0, 4 * slots * channels * 3),
        name="pack",
    )(
        lane, tile_index.reshape(1, foot_count), anchor.reshape(1, foot_count), weights.T,
        observed, accept
    )
    recv = lax.all_to_all(send, ("lat", "lon"), split_axis=0, concat_axis=0, tiled=True)

    recv, *strips = lax.optimization_barrier((
        recv, diffusivity[:halo], diffusivity[-halo:], diffusivity[:, :halo],
        diffusivity[:, -halo:]
    ))
    kappa_halos = halos(*strips)

    wide = 32
    evolved, field, top, bottom, left, right = pl.pallas_call(
        functools.partial(column_kernel, capacity, halo),
        out_shape=(
            jax.ShapeDtypeStruct((dev_count, capacity, channels), f32),
            jax.ShapeDtypeStruct((tile_rows, tile_cols, levels), f32),
            jax.ShapeDtypeStruct((halo, tile_cols, levels), f32),
            jax.ShapeDtypeStruct((halo, tile_cols, levels), f32),
            jax.ShapeDtypeStruct((tile_rows, halo, levels), f32),
            jax.ShapeDtypeStruct((tile_rows, halo, levels), f32),
        ),
        in_specs=[vmem()] * 5,
        out_specs=(vmem(),) * 6,
        scratch_shapes=[
            pltpu.SMEM((dev_count, channels), f32),
            pltpu.SemaphoreType.DMA,
            pltpu.VMEM((cells, levels), f32),
            pltpu.VMEM((levels, channels, lanes), f32),
            pltpu.VMEM((channels, lanes), f32),
            pltpu.VMEM((channels, lanes), f32),
            pltpu.VMEM((4, lanes, levels), f32),
            pltpu.VMEM((4, lanes, levels), f32),
            pltpu.VMEM((levels, lanes), f32),
            pltpu.VMEM((levels, lanes), f32),
            pltpu.VMEM((channels, lanes), f32),
            pltpu.VMEM((channels, lanes), f32),
            pltpu.VMEM((levels, wide, lanes), f32),
            pltpu.VMEM((levels, wide, lanes), f32),
            pltpu.VMEM((levels * 8, lanes), f32),
            pltpu.VMEM((4, cells, levels), f32),
        ],
        compiler_params=params(60),
        cost_estimate=cost(
            14 * slots * levels * channels, 2 * slots * levels * channels, 12 * cells * levels
        ),
        name="column",
    )(
        recv, background, absorb, sensitivity.reshape(1, channels),
        inverse_variance.reshape(1, channels)
    )

    returned = lax.all_to_all(evolved, ("lat", "lon"), split_axis=0, concat_axis=0, tiled=True)
    field_halos = halos(top, bottom, left, right)

    departure = pl.pallas_call(
        depart_kernel,
        out_shape=jax.ShapeDtypeStruct((foot_count, channels), f32),
        in_specs=[vmem()] * 3,
        out_specs=vmem(),
        compiler_params=params(16),
        cost_estimate=cost(2 * slots * foot_count * channels * 3, 0, 4 * slots * channels * 2),
        name="depart",
    )(slot, returned.reshape(slots, channels), observed)

    lat_at = lax.axis_index("lat")
    inside = jnp.stack([lat_at > 0, lat_at < lat_count - 1]).astype(f32)
    height, breadth = tile_rows + 2 * halo, tile_cols + 2 * halo

    plain = pltpu.VMEM((height, breadth, levels), f32)
    mixed = (height, breadth // 8, 8, levels)

    def edges_body(*refs):
        edges_kernel(halo, refs[:7], *refs[7:])

    east, south = pl.pallas_call(
        edges_body,
        out_shape=(jax.ShapeDtypeStruct(mixed, f32),) * 2,
        in_specs=[vmem()] * 7,
        out_specs=(vmem(),) * 2,
        scratch_shapes=[plain, pltpu.VMEM(mixed, f32)],
        compiler_params=params(22),
        cost_estimate=cost(4 * height * breadth * levels, 0, 12 * cells * levels),
        name="edges",
    )(diffusivity, *kappa_halos)

    def relax_body(inside_ref, *refs):
        relax_kernel(halo, inside_ref, refs[:7], *refs[7:])

    increment = pl.pallas_call(
        relax_body,
        out_shape=jax.ShapeDtypeStruct((tile_rows, tile_cols, levels), f32),
        in_specs=[smem()] + [vmem()] * 9,
        out_specs=vmem(),
        scratch_shapes=[plain, pltpu.VMEM(mixed, f32), pltpu.VMEM(mixed, f32)],
        compiler_params=params(26),
        cost_estimate=cost(10 * STEPS * height * breadth * levels, 0, 16 * cells * levels),
        name="relax",
    )(inside, field, *field_halos, east, south)
    return (departure, increment)


def solution(mesh):
    in_specs = (
        P("lat", "lon", None),
        P("lat", "lon", None),
        P(("lat", "lon"), None),
        P(("lat", "lon")),
        P(("lat", "lon"), None),
        P(("lat", "lon"), None),
        P(("lat", "lon"), None),
        P(),
        P(),
        P(),
    )
    out_specs = (P(("lat", "lon"), None), P("lat", "lon", None))
    return jax.shard_map(local, mesh=mesh, in_specs=in_specs, out_specs=out_specs, check_vma=False)
```

```python
import functools
import math

import jax
import jax.numpy as jnp
from jax import lax
from jax.experimental import pallas as pl
from jax.experimental.pallas import tpu as pltpu
from jax.sharding import PartitionSpec as P

STEPS = 8
REJECTED = 64.0
META = 8
LOG2E = math.log2(math.e)
LN2 = math.log(2.0)
MIB = 1024 * 1024
UNROLL = 16


def thirds(x):
    high = x.astype(jnp.bfloat16)
    rest = x - high.astype(jnp.float32)
    mid = rest.astype(jnp.bfloat16)
    low = (rest - mid.astype(jnp.float32)).astype(jnp.bfloat16)
    return high, mid, low


def dot_f32(a, b, contract):
    return lax.dot_general(a, b, (contract, ((), ())), preferred_element_type=jnp.float32)


def iota(shape, dim):
    return lax.broadcasted_iota(jnp.int32, shape, dim)


def pack_kernel(
    dev_count, capacity, tile_cols, lane_ref, tile_ref, anchor_ref, weights_ref, observed_ref,
    accept_ref, send_ref, slot_ref, vals_ref
):
    foot_count, channels = observed_ref.shape
    bf16 = jnp.bfloat16
    tile = tile_ref[...]
    onehot = jnp.where(iota((dev_count, foot_count), 0) == tile, 1.0, 0.0)
    earlier = jnp.where(
        iota((foot_count, foot_count), 0) < iota((foot_count, foot_count), 1), 1.0, 0.0
    ).astype(bf16)
    before = dot_f32(onehot.astype(bf16), earlier, ((1,), (0,)))
    rank = jnp.sum(before * onehot, axis=0, keepdims=True).astype(jnp.int32)
    slot = tile * capacity + rank
    slot_ref[...] = slot

    chosen = jnp.where(accept_ref[...] != 0, observed_ref[...], REJECTED)
    parts = thirds(chosen)
    per_chunk = max(1, 128 // capacity)
    chunk = per_chunk * capacity
    for start in range(0, dev_count, per_chunk):
        place = jnp.where(
            iota((chunk, foot_count), 0) + start * capacity == slot, 1.0, 0.0
        ).astype(bf16)
        rows = [dot_f32(place, part, ((1,), (0,))) for part in parts]
        rows = (rows[0] + rows[1]) + rows[2]
        send_ref[start : start + per_chunk, :capacity, :] = rows.reshape(
            per_chunk, capacity, channels
        )

    anchor = anchor_ref[...]
    line = jnp.floor((anchor.astype(jnp.float32) + 0.5) * (1.0 / (tile_cols - 1)))
    base = anchor.astype(jnp.float32) + line
    weights = weights_ref[...]
    shares = weights / jnp.sum(weights, axis=0, keepdims=True)
    meta = jnp.concatenate(
        [base, shares, jnp.zeros((META - 5, foot_count), jnp.float32)], axis=0
    )
    for dev in range(dev_count):
        vals_ref[dev * META : (dev + 1) * META, :] = jnp.where(tile == dev, meta, 0.0)
    lanes = jnp.where(
        iota((channels, foot_count), 0) == rank + lane_ref[0], 1.0, 0.0
    ).astype(bf16)
    rows = [dot_f32(part, lanes, ((1,), (1,))) for part in thirds(vals_ref[...])]
    rows = (rows[0] + rows[1]) + rows[2]
    send_ref[:, capacity:, :] = rows.reshape(dev_count, META, channels)


def spread_kernel(absorb_ref, out_ref, turned_ref):
    levels, channels, lanes = out_ref.shape
    turned_ref[...] = (absorb_ref[...] * LOG2E).T

    def some_levels(i, carry):
        turned = turned_ref[...]
        for u in range(8):
            out_ref[i * 8 + u] = jnp.broadcast_to(turned[:, u : u + 1], (channels, lanes))
        turned_ref[...] = pltpu.roll(turned, levels - 8, 1)
        return carry

    lax.fori_loop(0, levels // 8, some_levels, 0)


def column_kernel(
    capacity, halo, recv_ref, background_ref, absorb_any, sensitivity_ref, inverse_ref,
    ready_any, evolved_ref, field_ref, top_ref, bottom_ref, left_ref, right_ref, top_left_ref,
    top_right_ref, bottom_left_ref, bottom_right_ref,
    base_ref, sem, absorb_sem, cells_ref, absorb_b, slope_b, inverse_b, taken_ref, terms_ref, profile_ref,
    rise_ref, obs_ref, evo_ref, main_ref, side_ref, push_ref, sums_ref
):
    dev_count = recv_ref.shape[0]
    tile_rows, tile_cols, levels = background_ref.shape
    cells = tile_rows * tile_cols
    levels, channels, lanes = absorb_b.shape
    group = lanes // capacity
    blocks = dev_count // group
    wide = main_ref.shape[1]
    per_loop = UNROLL * wide * lanes // (levels * channels)
    corners = (0, 1, tile_cols, tile_cols + 1)

    copy = pltpu.make_async_copy(recv_ref.at[:, capacity, :], base_ref, sem)
    copy.start()
    absorb_copy = pltpu.make_async_copy(absorb_any, absorb_b, absorb_sem)
    absorb_copy.start()

    cells_ref[...] = background_ref[...].reshape(cells, levels).astype(jnp.float32)
    slope_b[...] = jnp.broadcast_to(sensitivity_ref[...] * LOG2E, (lanes, channels)).T
    inverse_b[...] = jnp.broadcast_to(inverse_ref[...], (lanes, channels)).T

    sums_ref[...] = jnp.zeros_like(sums_ref)
    terms_ref[...] = jnp.zeros_like(terms_ref)
    copy.wait()

    def base_of(f, at):
        return base_ref[f * group + lax.div(at, capacity), at].astype(jnp.int32)

    def gather(f, at):
        base = base_of(f, at)
        for k, step in enumerate(corners):
            taken_ref[k, pl.ds(at, 1), :] = cells_ref[pl.ds(base + step, 1), :]

    def scatter(f, at):
        base = base_of(f, at)
        for k, step in enumerate(corners):
            sums_ref[k, pl.ds(base + step, 1), :] += terms_ref[k, pl.ds(at, 1), :]

    def gather_first(i, carry):
        for u in range(8):
            gather(0, i * 8 + u)
        return carry

    lax.fori_loop(0, lanes // 8, gather_first, 0)
    absorb_copy.wait()

    def block(f, carry):
        before = jnp.maximum(f - 1, 0)
        after = jnp.minimum(f + 1, blocks - 1)
        mine = recv_ref[pl.ds(f * group, group)]
        shares = jnp.sum(mine[:, capacity:, :], axis=0)
        obs_ref[...] = mine[:, :capacity, :].reshape(lanes, channels).T
        profile = shares[1:2] * taken_ref[0].T
        for k in range(1, 4):
            profile = profile + shares[k + 1 : k + 2] * taken_ref[k].T
        profile_ref[...] = profile
        rise_ref[0 : levels - 1, :] = profile[1:] - profile[:-1]
        rise_ref[levels - 1 : levels, :] = jnp.zeros((1, lanes), jnp.float32)
        push_ref[...] = jnp.zeros_like(push_ref)

        def some_channels(c, carry):
            at = pl.multiple_of(c * wide, wide)
            slope = slope_b[pl.ds(at, wide), :]
            scale = slope * (LN2 * LN2)

            def down(i, state):
                path, total, above = state
                for u in range(UNROLL):
                    level = i * UNROLL + u
                    depth = absorb_b[level, pl.ds(at, wide), :] * jnp.exp2(
                        slope * profile_ref[pl.ds(level, 1), :]
                    )
                    path = path - depth
                    trans = jnp.exp2(path)
                    side = depth * scale
                    side_ref[level] = side
                    main_ref[level] = (above - trans) + side * total
                    total = total + trans * rise_ref[pl.ds(level, 1), :]
                    above = trans
                for u in range(per_loop):
                    scatter(before, (c * (levels // UNROLL) + i) * per_loop + u)
                return path, total, above

            zero = jnp.zeros((wide, lanes), jnp.float32)
            _, total, last = lax.fori_loop(0, levels // UNROLL, down, (zero, zero, zero + 1.0))
            main_ref[levels - 1] += last
            evolved = total + profile_ref[0:1, :]
            evo_ref[pl.ds(at, wide), :] = evolved
            obs = obs_ref[pl.ds(at, wide), :]
            force = jnp.where(
                obs < 0.5 * REJECTED, inverse_b[pl.ds(at, wide), :] * (obs - evolved), 0.0
            )

            def up(i, carry):
                for u in range(UNROLL):
                    level = i * UNROLL + u
                    push = force * (main_ref[level] - total * side_ref[level])
                    push_ref[pl.ds(pl.multiple_of(level * 8, 8), 8), :] += jnp.sum(
                        push.reshape(wide // 8, 8, lanes), axis=0
                    )
                for u in range(per_loop):
                    gather(after, (c * (levels // UNROLL) + i) * per_loop + u)
                return carry

            lax.fori_loop(0, levels // UNROLL, up, 0)
            return carry

        lax.fori_loop(0, channels // wide, some_channels, 0)
        evolved_ref[pl.ds(f * group, group)] = evo_ref[...].T.reshape(group, capacity, channels)
        push = push_ref[pl.ds(0, levels, stride=8), :]
        for u in range(1, 8):
            push = push + push_ref[pl.ds(u, levels, stride=8), :]
        for k in range(4):
            terms_ref[k] = (shares[k + 1 : k + 2] * push).T
        return carry

    lax.fori_loop(0, blocks, block, 0)

    def scatter_last(i, carry):
        for u in range(8):
            scatter(blocks - 1, i * 8 + u)
        return carry

    lax.fori_loop(0, lanes // 8, scatter_last, 0)

    field = (sums_ref[0] + sums_ref[1]) + (sums_ref[2] + sums_ref[3])
    field = field.reshape(tile_rows, tile_cols, levels)
    field_ref[...] = field
    top_ref[...] = field[:halo]
    bottom_ref[...] = field[tile_rows - halo :]
    left_ref[...] = field[:, :halo]
    right_ref[...] = field[:, tile_cols - halo :]
    top_left_ref[...] = field[:halo, :halo]
    top_right_ref[...] = field[:halo, tile_cols - halo :]
    bottom_left_ref[...] = field[tile_rows - halo :, :halo]
    bottom_right_ref[...] = field[tile_rows - halo :, tile_cols - halo :]


def lay(halo, target, refs):
    centre, north, south, west, east, north_west, north_east, south_west, south_east = refs
    tile_rows, tile_cols, _ = centre.shape
    height, breadth = tile_rows + 2 * halo, tile_cols + 2 * halo
    low_r, low_c = slice(0, halo), slice(0, halo)
    mid_r, mid_c = slice(halo, halo + tile_rows), slice(halo, halo + tile_cols)
    end_r, end_c = slice(halo + tile_rows, height), slice(halo + tile_cols, breadth)
    target[mid_r, mid_c] = centre[...]
    target[low_r, mid_c] = north[...]
    target[end_r, mid_c] = south[...]
    target[mid_r, low_c] = west[...]
    target[mid_r, end_c] = east[...]
    target[low_r, low_c] = north_west[...]
    target[low_r, end_c] = north_east[...]
    target[end_r, low_c] = south_west[...]
    target[end_r, end_c] = south_east[...]


KAPPA_LOW = 0.12
KAPPA_STEP = 0.125 / 65535


def encode_kappa(x):
    whole = jnp.round((x - KAPPA_LOW) * (1.0 / KAPPA_STEP))
    return (jnp.clip(whole, 0.0, 65535.0) - 32768.0).astype(jnp.int16)


def decode_kappa(x):
    whole = x.astype(jnp.int32).astype(jnp.float32) + 32768.0
    return whole * KAPPA_STEP + KAPPA_LOW


def interleave(plain_ref, target_ref):
    stretch = target_ref.shape[1]

    def row(i, carry):
        for t in range(stretch):
            target_ref[i, t] = plain_ref[i, pl.ds(t, 8, stride=stretch), :]
        return carry

    lax.fori_loop(0, plain_ref.shape[0], row, 0)


def eastward(x):
    return jnp.concatenate([x[1:], pltpu.roll(x[0], 7, 0)[None]], axis=0)


def westward(x):
    return jnp.concatenate([pltpu.roll(x[-1], 1, 0)[None], x[:-1]], axis=0)


def edges_kernel(
    halo, inside_ref, centre_ref, north_ref, south_ref, west_ref, east_side_ref, east_ref,
    south_edge_ref, plain_ref, kappa_ref
):
    tile_rows, tile_cols, _ = centre_ref.shape
    height, breadth = plain_ref.shape[:2]
    mid_r, mid_c = slice(halo, halo + tile_rows), slice(halo, halo + tile_cols)
    low, end = slice(0, halo), slice(halo + tile_rows, height)
    plain_ref[mid_r, mid_c] = centre_ref[...]
    plain_ref[:, :halo] = decode_kappa(west_ref[...])
    plain_ref[:, halo + tile_cols :] = decode_kappa(east_side_ref[...])
    plain_ref[low, mid_c] = decode_kappa(north_ref[...])
    plain_ref[end, mid_c] = decode_kappa(south_ref[...])
    plain_ref[low] = plain_ref[low] * inside_ref[0]
    plain_ref[end] = plain_ref[end] * inside_ref[1]
    interleave(plain_ref, kappa_ref)

    def edges(i, carry):
        here = kappa_ref[i]
        east_ref[i] = 0.5 * (here + eastward(here))
        south_edge_ref[i] = 0.5 * (here + kappa_ref[jnp.minimum(i + 1, height - 1)])
        return carry

    lax.fori_loop(0, height, edges, 0)


def relax_kernel(
    halo, inside_ref, field_refs, east_any, south_any, out_ref, plain_ref, first_ref, second_ref,
    east_ref, south_ref, east_sem, south_sem
):
    copies = [
        pltpu.make_async_copy(east_any, east_ref, east_sem),
        pltpu.make_async_copy(south_any, south_ref, south_sem),
    ]
    for copy in copies:
        copy.start()
    tile_rows, tile_cols, levels = out_ref.shape
    height = tile_rows + 2 * halo
    stretch = first_ref.shape[1]
    lay(halo, plain_ref, field_refs)
    interleave(plain_ref, first_ref)
    for copy in copies:
        copy.wait()

    source, target = first_ref, second_ref
    for step in range(1, halo + 1):
        last = step == halo

        def row(i, carry, scale=None, source=source, target=target, last=last):
            here, from_north = carry
            below = source[i + 1]
            to_east = east_ref[i] * (eastward(here) - here)
            from_south = south_ref[i] * (below - here)
            value = here + (to_east - westward(to_east)) + (from_south - from_north)
            if scale is not None:
                value = value * scale
            if last:
                for t in range(stretch):
                    plain_ref[i, pl.ds(t, 8, stride=stretch), :] = value[t]
            else:
                target[i] = value
            return below, from_south

        here = source[step]
        carry = (here, south_ref[step - 1] * (here - source[step - 1]))
        carry = lax.fori_loop(
            step, halo, functools.partial(row, scale=inside_ref[0]), carry, unroll=True
        )
        carry = lax.fori_loop(halo, halo + tile_rows, row, carry, unroll=4)
        lax.fori_loop(
            halo + tile_rows, height - step, functools.partial(row, scale=inside_ref[1]), carry,
            unroll=True,
        )
        source, target = target, source
    out_ref[...] = plain_ref[halo : halo + tile_rows, halo : halo + tile_cols, :]


def depart_kernel(slot_ref, evolved_ref, observed_ref, out_ref):
    foot_count, _ = observed_ref.shape
    slots = evolved_ref.shape[0]
    slot = slot_ref[...]
    parts = thirds(evolved_ref[...])
    chosen = jnp.where(iota((slots, foot_count), 0) == slot, 1.0, 0.0).astype(jnp.bfloat16)
    rows = [dot_f32(chosen, part, ((0,), (0,))) for part in parts]
    out_ref[...] = observed_ref[...] - ((rows[0] + rows[1]) + rows[2])


def vmem():
    return pl.BlockSpec(memory_space=pltpu.VMEM)


def smem():
    return pl.BlockSpec(memory_space=pltpu.SMEM)


def params(mib):
    return pltpu.CompilerParams(vmem_limit_bytes=mib * MIB)


def cost(flops, transcendentals, moved):
    return pl.CostEstimate(flops=flops, transcendentals=transcendentals, bytes_accessed=moved)


def neighbours(axis, periodic):
    count = lax.axis_size(axis)
    forward = [(i, i + 1) for i in range(count - 1)]
    if periodic:
        forward.append((count - 1, 0))
    return forward, [(target, source) for source, target in forward]


def halos(top, bottom, left, right, corners):
    lat_up, lat_down = neighbours("lat", False)
    lon_up, lon_down = neighbours("lon", True)
    lon_count = lax.axis_size("lon")

    def both(lat_pairs, lon_pairs):
        return [
            (a * lon_count + c, b * lon_count + d) for a, b in lat_pairs for c, d in lon_pairs
        ]

    west = lax.ppermute(right, "lon", lon_up)
    east = lax.ppermute(left, "lon", lon_down)
    north = lax.ppermute(bottom, "lat", lat_up)
    south = lax.ppermute(top, "lat", lat_down)
    top_left, top_right, bottom_left, bottom_right = corners
    axes = ("lat", "lon")
    north_west = lax.ppermute(bottom_right, axes, both(lat_up, lon_up))
    north_east = lax.ppermute(bottom_left, axes, both(lat_up, lon_down))
    south_west = lax.ppermute(top_right, axes, both(lat_down, lon_up))
    south_east = lax.ppermute(top_left, axes, both(lat_down, lon_down))
    return north, south, west, east, north_west, north_east, south_west, south_east


def corners_of(x, halo):
    return x[:halo, :halo], x[:halo, -halo:], x[-halo:, :halo], x[-halo:, -halo:]


def local(
    background, diffusivity, tile_index, anchor, weights, observed, accept, absorb, sensitivity,
    inverse_variance
):
    f32 = jnp.float32
    lat_count = lax.axis_size("lat")
    lon_count = lax.axis_size("lon")
    dev_count = lat_count * lon_count
    foot_count, channels = observed.shape
    capacity = max(2, 2 * foot_count // dev_count)
    tile_rows, tile_cols, levels = background.shape
    slots = dev_count * capacity
    lanes = 128
    group = lanes // capacity
    cells = tile_rows * tile_cols
    halo = STEPS

    me = lax.axis_index("lat") * lon_count + lax.axis_index("lon")
    lane = (lax.rem(me, group) * capacity).astype(jnp.int32).reshape(1)
    send, slot = pl.pallas_call(
        functools.partial(pack_kernel, dev_count, capacity, tile_cols),
        out_shape=(
            jax.ShapeDtypeStruct((dev_count, capacity + META, channels), f32),
            jax.ShapeDtypeStruct((1, foot_count), jnp.int32),
        ),
        in_specs=[smem()] + [vmem()] * 5,
        out_specs=(vmem(), vmem()),
        scratch_shapes=[pltpu.VMEM((dev_count * META, foot_count), f32)],
        compiler_params=params(60),
        cost_estimate=cost(2 * slots * foot_count * channels * 3, 0, 4 * slots * channels * 3),
        name="pack",
    )(
        lane, tile_index.reshape(1, foot_count), anchor.reshape(1, foot_count), weights.T,
        observed, accept
    )
    recv = lax.all_to_all(send, ("lat", "lon"), split_axis=0, concat_axis=0, tiled=True)

    lat_up, lat_down = neighbours("lat", False)
    lon_up, lon_down = neighbours("lon", True)
    kappa_north = lax.ppermute(encode_kappa(diffusivity[-halo:]), "lat", lat_up)
    kappa_south = lax.ppermute(encode_kappa(diffusivity[:halo]), "lat", lat_down)
    kappa_left, kappa_right = (
        jnp.concatenate([kappa_north[:, cut], encode_kappa(diffusivity[:, cut]),
                         kappa_south[:, cut]], axis=0)
        for cut in (slice(0, halo), slice(tile_cols - halo, tile_cols))
    )
    kappa_west = lax.ppermute(kappa_right, "lon", lon_up)
    kappa_east = lax.ppermute(kappa_left, "lon", lon_down)
    absorb_wide = pl.pallas_call(
        spread_kernel,
        out_shape=jax.ShapeDtypeStruct((levels, channels, lanes), f32),
        in_specs=[vmem()],
        out_specs=vmem(),
        scratch_shapes=[pltpu.VMEM((channels, levels), f32)],
        compiler_params=params(60),
        cost_estimate=cost(levels * channels * lanes, 0, 4 * levels * channels * lanes),
        name="spread",
    )(absorb)

    lat_at = lax.axis_index("lat")
    inside = jnp.stack([lat_at > 0, lat_at < lat_count - 1]).astype(f32)
    height, breadth = tile_rows + 2 * halo, tile_cols + 2 * halo

    plain = pltpu.VMEM((height, breadth, levels), f32)
    mixed = (height, breadth // 8, 8, levels)

    east, south = pl.pallas_call(
        functools.partial(edges_kernel, halo),
        out_shape=(jax.ShapeDtypeStruct(mixed, f32),) * 2,
        in_specs=[smem()] + [vmem()] * 5,
        out_specs=(vmem(),) * 2,
        scratch_shapes=[plain, pltpu.VMEM(mixed, f32)],
        compiler_params=params(60),
        cost_estimate=cost(4 * height * breadth * levels, 0, 12 * cells * levels),
        name="edges",
    )(inside, diffusivity, kappa_north, kappa_south, kappa_west, kappa_east)


    wide = 32
    evolved, field, top, bottom, left, right, *corners = pl.pallas_call(
        functools.partial(column_kernel, capacity, halo),
        out_shape=(
            jax.ShapeDtypeStruct((dev_count, capacity, channels), f32),
            jax.ShapeDtypeStruct((tile_rows, tile_cols, levels), f32),
            jax.ShapeDtypeStruct((halo, tile_cols, levels), f32),
            jax.ShapeDtypeStruct((halo, tile_cols, levels), f32),
            jax.ShapeDtypeStruct((tile_rows, halo, levels), f32),
            jax.ShapeDtypeStruct((tile_rows, halo, levels), f32),
        ) + (jax.ShapeDtypeStruct((halo, halo, levels), f32),) * 4,
        in_specs=[vmem()] * 2 + [pl.BlockSpec(memory_space=pl.ANY)]
        + [vmem()] * 2 + [pl.BlockSpec(memory_space=pl.ANY)],
        out_specs=(vmem(),) * 10,
        scratch_shapes=[
            pltpu.SMEM((dev_count, channels), f32),
            pltpu.SemaphoreType.DMA,
            pltpu.SemaphoreType.DMA,
            pltpu.VMEM((cells, levels), f32),
            pltpu.VMEM((levels, channels, lanes), f32),
            pltpu.VMEM((channels, lanes), f32),
            pltpu.VMEM((channels, lanes), f32),
            pltpu.VMEM((4, lanes, levels), f32),
            pltpu.VMEM((4, lanes, levels), f32),
            pltpu.VMEM((levels, lanes), f32),
            pltpu.VMEM((levels, lanes), f32),
            pltpu.VMEM((channels, lanes), f32),
            pltpu.VMEM((channels, lanes), f32),
            pltpu.VMEM((levels, wide, lanes), f32),
            pltpu.VMEM((levels, wide, lanes), f32),
            pltpu.VMEM((levels * 8, lanes), f32),
            pltpu.VMEM((4, cells, levels), f32),
        ],
        compiler_params=params(60),
        cost_estimate=cost(
            14 * slots * levels * channels, 2 * slots * levels * channels, 12 * cells * levels
        ),
        name="column",
    )(
        recv, background, absorb_wide, sensitivity.reshape(1, channels),
        inverse_variance.reshape(1, channels), east
    )

    field_halos = halos(top, bottom, left, right, corners)
    evolved = pl.pallas_call(
        lambda *refs: None,
        out_shape=jax.ShapeDtypeStruct(evolved.shape, f32),
        in_specs=[pl.BlockSpec(memory_space=pl.ANY)] * 9,
        out_specs=pl.BlockSpec(memory_space=pl.ANY),
        input_output_aliases={0: 0},
        name="after_halos",
    )(evolved, *field_halos)
    returned = lax.all_to_all(evolved, ("lat", "lon"), split_axis=0, concat_axis=0, tiled=True)

    departure = pl.pallas_call(
        depart_kernel,
        out_shape=jax.ShapeDtypeStruct((foot_count, channels), f32),
        in_specs=[vmem()] * 3,
        out_specs=vmem(),
        compiler_params=params(16),
        cost_estimate=cost(2 * slots * foot_count * channels * 3, 0, 4 * slots * channels * 2),
        name="depart",
    )(slot, returned.reshape(slots, channels), observed)

    def relax_body(inside_ref, *refs):
        relax_kernel(halo, inside_ref, refs[:9], *refs[9:])

    increment = pl.pallas_call(
        relax_body,
        out_shape=jax.ShapeDtypeStruct((tile_rows, tile_cols, levels), f32),
        in_specs=[smem()] + [vmem()] * 9 + [pl.BlockSpec(memory_space=pl.ANY)] * 2,
        out_specs=vmem(),
        scratch_shapes=[plain] + [pltpu.VMEM(mixed, f32)] * 4 + [pltpu.SemaphoreType.DMA] * 2,
        compiler_params=params(60),
        cost_estimate=cost(10 * STEPS * height * breadth * levels, 0, 16 * cells * levels),
        name="relax",
    )(inside, field, *field_halos, east, south)
    return (departure, increment)


def solution(mesh):
    in_specs = (
        P("lat", "lon", None),
        P("lat", "lon", None),
        P(("lat", "lon"), None),
        P(("lat", "lon")),
        P(("lat", "lon"), None),
        P(("lat", "lon"), None),
        P(("lat", "lon"), None),
        P(),
        P(),
        P(),
    )
    out_specs = (P(("lat", "lon"), None), P("lat", "lon", None))
    return jax.shard_map(local, mesh=mesh, in_specs=in_specs, out_specs=out_specs, check_vma=False)
```

```python
import functools
import math

import jax
import jax.numpy as jnp
from jax import lax
from jax.experimental import pallas as pl
from jax.experimental.pallas import tpu as pltpu
from jax.sharding import PartitionSpec as P

STEPS = 8
REJECTED = 64.0
META = 8
LOG2E = math.log2(math.e)
LN2 = math.log(2.0)
MIB = 1024 * 1024
UNROLL = 16


def thirds(x):
    high = x.astype(jnp.bfloat16)
    rest = x - high.astype(jnp.float32)
    mid = rest.astype(jnp.bfloat16)
    low = (rest - mid.astype(jnp.float32)).astype(jnp.bfloat16)
    return high, mid, low


def dot_f32(a, b, contract):
    return lax.dot_general(a, b, (contract, ((), ())), preferred_element_type=jnp.float32)


def iota(shape, dim):
    return lax.broadcasted_iota(jnp.int32, shape, dim)


def pack_kernel(
    dev_count, capacity, tile_cols, lane_ref, tile_ref, anchor_ref, weights_ref, observed_ref,
    accept_ref, send_ref, slot_ref, vals_ref
):
    foot_count, channels = observed_ref.shape
    bf16 = jnp.bfloat16
    tile = tile_ref[...]
    onehot = jnp.where(iota((dev_count, foot_count), 0) == tile, 1.0, 0.0)
    earlier = jnp.where(
        iota((foot_count, foot_count), 0) < iota((foot_count, foot_count), 1), 1.0, 0.0
    ).astype(bf16)
    before = dot_f32(onehot.astype(bf16), earlier, ((1,), (0,)))
    rank = jnp.sum(before * onehot, axis=0, keepdims=True).astype(jnp.int32)
    slot = tile * capacity + rank
    slot_ref[...] = slot

    chosen = jnp.where(accept_ref[...] != 0, observed_ref[...], REJECTED)
    parts = thirds(chosen)
    per_chunk = max(1, 128 // capacity)
    chunk = per_chunk * capacity
    for start in range(0, dev_count, per_chunk):
        place = jnp.where(
            iota((chunk, foot_count), 0) + start * capacity == slot, 1.0, 0.0
        ).astype(bf16)
        rows = [dot_f32(place, part, ((1,), (0,))) for part in parts]
        rows = (rows[0] + rows[1]) + rows[2]
        send_ref[start : start + per_chunk, :capacity, :] = rows.reshape(
            per_chunk, capacity, channels
        )

    anchor = anchor_ref[...]
    line = jnp.floor((anchor.astype(jnp.float32) + 0.5) * (1.0 / (tile_cols - 1)))
    base = anchor.astype(jnp.float32) + line
    weights = weights_ref[...]
    shares = weights / jnp.sum(weights, axis=0, keepdims=True)
    meta = jnp.concatenate(
        [base, shares, jnp.zeros((META - 5, foot_count), jnp.float32)], axis=0
    )
    for dev in range(dev_count):
        vals_ref[dev * META : (dev + 1) * META, :] = jnp.where(tile == dev, meta, 0.0)
    lanes = jnp.where(
        iota((channels, foot_count), 0) == rank + lane_ref[0], 1.0, 0.0
    ).astype(bf16)
    rows = [dot_f32(part, lanes, ((1,), (1,))) for part in thirds(vals_ref[...])]
    rows = (rows[0] + rows[1]) + rows[2]
    send_ref[:, capacity:, :] = rows.reshape(dev_count, META, channels)


def spread_kernel(absorb_ref, out_ref, turned_ref):
    levels, channels, lanes = out_ref.shape
    turned_ref[...] = (absorb_ref[...] * LOG2E).T

    def some_levels(i, carry):
        turned = turned_ref[...]
        for u in range(8):
            out_ref[i * 8 + u] = jnp.broadcast_to(turned[:, u : u + 1], (channels, lanes))
        turned_ref[...] = pltpu.roll(turned, levels - 8, 1)
        return carry

    lax.fori_loop(0, levels // 8, some_levels, 0)


def column_kernel(
    capacity, halo, recv_ref, background_ref, absorb_any, sensitivity_ref, inverse_ref,
    ready_west, ready_east, evolved_ref, field_ref, top_ref, bottom_ref, left_ref, right_ref,
    base_ref, sem, absorb_sem, cells_ref, absorb_b, slope_b, inverse_b, taken_ref, terms_ref, profile_ref,
    rise_ref, obs_ref, evo_ref, main_ref, side_ref, push_ref, sums_ref
):
    dev_count = recv_ref.shape[0]
    tile_rows, tile_cols, levels = background_ref.shape
    cells = tile_rows * tile_cols
    levels, channels, lanes = absorb_b.shape
    group = lanes // capacity
    blocks = dev_count // group
    wide = main_ref.shape[1]
    per_loop = UNROLL * wide * lanes // (levels * channels)
    corners = (0, 1, tile_cols, tile_cols + 1)

    copy = pltpu.make_async_copy(recv_ref.at[:, capacity, :], base_ref, sem)
    copy.start()
    absorb_copy = pltpu.make_async_copy(absorb_any, absorb_b, absorb_sem)
    absorb_copy.start()

    cells_ref[...] = background_ref[...].reshape(cells, levels).astype(jnp.float32)
    slope_b[...] = jnp.broadcast_to(sensitivity_ref[...] * LOG2E, (lanes, channels)).T
    inverse_b[...] = jnp.broadcast_to(inverse_ref[...], (lanes, channels)).T

    sums_ref[...] = jnp.zeros_like(sums_ref)
    terms_ref[...] = jnp.zeros_like(terms_ref)
    copy.wait()

    def base_of(f, at):
        return base_ref[f * group + lax.div(at, capacity), at].astype(jnp.int32)

    def gather(f, at):
        base = base_of(f, at)
        for k, step in enumerate(corners):
            taken_ref[k, pl.ds(at, 1), :] = cells_ref[pl.ds(base + step, 1), :]

    def scatter(f, at):
        base = base_of(f, at)
        for k, step in enumerate(corners):
            sums_ref[k, pl.ds(base + step, 1), :] += terms_ref[k, pl.ds(at, 1), :]

    def gather_first(i, carry):
        for u in range(8):
            gather(0, i * 8 + u)
        return carry

    lax.fori_loop(0, lanes // 8, gather_first, 0)
    absorb_copy.wait()

    def block(f, carry):
        before = jnp.maximum(f - 1, 0)
        after = jnp.minimum(f + 1, blocks - 1)
        mine = recv_ref[pl.ds(f * group, group)]
        shares = jnp.sum(mine[:, capacity:, :], axis=0)
        obs_ref[...] = mine[:, :capacity, :].reshape(lanes, channels).T
        profile = shares[1:2] * taken_ref[0].T
        for k in range(1, 4):
            profile = profile + shares[k + 1 : k + 2] * taken_ref[k].T
        profile_ref[...] = profile
        rise_ref[0 : levels - 1, :] = profile[1:] - profile[:-1]
        rise_ref[levels - 1 : levels, :] = jnp.zeros((1, lanes), jnp.float32)
        push_ref[...] = jnp.zeros_like(push_ref)

        def some_channels(c, carry):
            at = pl.multiple_of(c * wide, wide)
            slope = slope_b[pl.ds(at, wide), :]
            scale = slope * (LN2 * LN2)

            def down(i, state):
                path, total, above = state
                for u in range(UNROLL):
                    level = i * UNROLL + u
                    depth = absorb_b[level, pl.ds(at, wide), :] * jnp.exp2(
                        slope * profile_ref[pl.ds(level, 1), :]
                    )
                    path = path - depth
                    trans = jnp.exp2(path)
                    side = depth * scale
                    side_ref[level] = side
                    main_ref[level] = (above - trans) + side * total
                    total = total + trans * rise_ref[pl.ds(level, 1), :]
                    above = trans
                for u in range(per_loop):
                    scatter(before, (c * (levels // UNROLL) + i) * per_loop + u)
                return path, total, above

            zero = jnp.zeros((wide, lanes), jnp.float32)
            _, total, last = lax.fori_loop(0, levels // UNROLL, down, (zero, zero, zero + 1.0))
            main_ref[levels - 1] += last
            evolved = total + profile_ref[0:1, :]
            evo_ref[pl.ds(at, wide), :] = evolved
            obs = obs_ref[pl.ds(at, wide), :]
            force = jnp.where(
                obs < 0.5 * REJECTED, inverse_b[pl.ds(at, wide), :] * (obs - evolved), 0.0
            )

            def up(i, carry):
                for u in range(UNROLL):
                    level = i * UNROLL + u
                    push = force * (main_ref[level] - total * side_ref[level])
                    push_ref[pl.ds(pl.multiple_of(level * 8, 8), 8), :] += jnp.sum(
                        push.reshape(wide // 8, 8, lanes), axis=0
                    )
                for u in range(per_loop):
                    gather(after, (c * (levels // UNROLL) + i) * per_loop + u)
                return carry

            lax.fori_loop(0, levels // UNROLL, up, 0)
            return carry

        lax.fori_loop(0, channels // wide, some_channels, 0)
        evolved_ref[pl.ds(f * group, group)] = evo_ref[...].T.reshape(group, capacity, channels)
        push = push_ref[pl.ds(0, levels, stride=8), :]
        for u in range(1, 8):
            push = push + push_ref[pl.ds(u, levels, stride=8), :]
        for k in range(4):
            terms_ref[k] = (shares[k + 1 : k + 2] * push).T
        return carry

    lax.fori_loop(0, blocks, block, 0)

    def scatter_last(i, carry):
        for u in range(8):
            scatter(blocks - 1, i * 8 + u)
        return carry

    lax.fori_loop(0, lanes // 8, scatter_last, 0)

    field = (sums_ref[0] + sums_ref[1]) + (sums_ref[2] + sums_ref[3])
    field = field.reshape(tile_rows, tile_cols, levels)
    field_ref[...] = field

    borders = (
        (top_ref, field[:halo]),
        (bottom_ref, field[tile_rows - halo :]),
        (left_ref, field[:, :halo]),
        (right_ref, field[:, tile_cols - halo :]),
    )
    peak = jnp.full((1, levels), 1e-30, jnp.float32)
    for _, strip in borders:
        peak = jnp.maximum(
            peak, jnp.max(jnp.max(jnp.abs(strip), axis=0), axis=0, keepdims=True)
        )
    power = jnp.ceil(jnp.log2(peak))
    scale = jnp.exp2(15.0 - power)
    for ref, strip in borders:
        count = strip.shape[0]
        whole = jnp.floor(strip * scale + 0.5)
        whole = jnp.clip(whole, -32767.0, 32767.0)
        ref[:count] = whole.astype(jnp.int32).astype(jnp.int16)
        ref[count] = jnp.broadcast_to(power, strip.shape[1:]).astype(jnp.int32).astype(jnp.int16)


def decode_field(coded, power):
    scale = jnp.exp2(power.astype(jnp.int32).astype(jnp.float32) - 15.0)
    return coded.astype(jnp.int32).astype(jnp.float32) * scale


def lay(halo, target, centre, north, south, west, east):
    tile_rows, tile_cols, _ = centre.shape
    height, breadth = tile_rows + 2 * halo, tile_cols + 2 * halo
    mid_r, mid_c = slice(halo, halo + tile_rows), slice(halo, halo + tile_cols)
    target[mid_r, mid_c] = centre[...]
    target[:halo, mid_c] = decode_field(north[:halo], north[halo])
    target[halo + tile_rows :, mid_c] = decode_field(south[:halo], south[halo])
    for side, cols in ((west, slice(0, halo)), (east, slice(halo + tile_cols, breadth))):
        read, put = 0, 0
        for count in (halo, tile_rows, halo):
            target[put : put + count, cols] = decode_field(
                side[read : read + count], side[read + count]
            )
            read, put = read + count + 1, put + count


KAPPA_LOW = 0.12
KAPPA_STEP = 0.125 / 65535


def encode_kappa(x):
    whole = jnp.round((x - KAPPA_LOW) * (1.0 / KAPPA_STEP))
    return (jnp.clip(whole, 0.0, 65535.0) - 32768.0).astype(jnp.int16)


def decode_kappa(x):
    whole = x.astype(jnp.int32).astype(jnp.float32) + 32768.0
    return whole * KAPPA_STEP + KAPPA_LOW


def interleave(plain_ref, target_ref):
    stretch = target_ref.shape[1]

    def row(i, carry):
        for t in range(stretch):
            target_ref[i, t] = plain_ref[i, pl.ds(t, 8, stride=stretch), :]
        return carry

    lax.fori_loop(0, plain_ref.shape[0], row, 0)


def eastward(x):
    return jnp.concatenate([x[1:], pltpu.roll(x[0], 7, 0)[None]], axis=0)


def westward(x):
    return jnp.concatenate([pltpu.roll(x[-1], 1, 0)[None], x[:-1]], axis=0)


def edges_kernel(
    halo, inside_ref, centre_ref, north_ref, south_ref, west_ref, east_side_ref, east_ref,
    south_edge_ref, plain_ref, kappa_ref
):
    tile_rows, tile_cols, _ = centre_ref.shape
    height, breadth = plain_ref.shape[:2]
    mid_r, mid_c = slice(halo, halo + tile_rows), slice(halo, halo + tile_cols)
    low, end = slice(0, halo), slice(halo + tile_rows, height)
    plain_ref[mid_r, mid_c] = centre_ref[...]
    plain_ref[:, :halo] = decode_kappa(west_ref[...])
    plain_ref[:, halo + tile_cols :] = decode_kappa(east_side_ref[...])
    plain_ref[low, mid_c] = decode_kappa(north_ref[...])
    plain_ref[end, mid_c] = decode_kappa(south_ref[...])
    plain_ref[low] = plain_ref[low] * inside_ref[0]
    plain_ref[end] = plain_ref[end] * inside_ref[1]
    interleave(plain_ref, kappa_ref)

    def edges(i, carry):
        here = kappa_ref[i]
        east_ref[i] = 0.5 * (here + eastward(here))
        south_edge_ref[i] = 0.5 * (here + kappa_ref[jnp.minimum(i + 1, height - 1)])
        return carry

    lax.fori_loop(0, height, edges, 0)


def relax_kernel(
    halo, inside_ref, centre_ref, north_ref, south_ref, west_ref, east_side_ref, east_ref,
    south_edge_ref, out_ref, plain_ref, first_ref, second_ref
):
    tile_rows, tile_cols, levels = out_ref.shape
    height = tile_rows + 2 * halo
    stretch = first_ref.shape[1]
    lay(halo, plain_ref, centre_ref, north_ref, south_ref, west_ref, east_side_ref)
    interleave(plain_ref, first_ref)

    source, target = first_ref, second_ref
    for step in range(1, halo + 1):
        last = step == halo

        def row(i, carry, scale=None, source=source, target=target, last=last):
            here, from_north = carry
            below = source[i + 1]
            to_east = east_ref[i] * (eastward(here) - here)
            from_south = south_edge_ref[i] * (below - here)
            value = here + (to_east - westward(to_east)) + (from_south - from_north)
            if scale is not None:
                value = value * scale
            if last:
                for t in range(stretch):
                    plain_ref[i, pl.ds(t, 8, stride=stretch), :] = value[t]
            else:
                target[i] = value
            return below, from_south

        here = source[step]
        carry = (here, south_edge_ref[step - 1] * (here - source[step - 1]))
        carry = lax.fori_loop(
            step, halo, functools.partial(row, scale=inside_ref[0]), carry, unroll=True
        )
        carry = lax.fori_loop(halo, halo + tile_rows, row, carry, unroll=4)
        lax.fori_loop(
            halo + tile_rows, height - step, functools.partial(row, scale=inside_ref[1]), carry,
            unroll=True,
        )
        source, target = target, source
    out_ref[...] = plain_ref[halo : halo + tile_rows, halo : halo + tile_cols, :]


def depart_kernel(slot_ref, evolved_ref, observed_ref, out_ref):
    foot_count, _ = observed_ref.shape
    slots = evolved_ref.shape[0]
    slot = slot_ref[...]
    parts = thirds(evolved_ref[...])
    chosen = jnp.where(iota((slots, foot_count), 0) == slot, 1.0, 0.0).astype(jnp.bfloat16)
    rows = [dot_f32(chosen, part, ((0,), (0,))) for part in parts]
    out_ref[...] = observed_ref[...] - ((rows[0] + rows[1]) + rows[2])


def vmem():
    return pl.BlockSpec(memory_space=pltpu.VMEM)


def smem():
    return pl.BlockSpec(memory_space=pltpu.SMEM)


def anywhere():
    return pl.BlockSpec(memory_space=pl.ANY)


def params(mib):
    return pltpu.CompilerParams(vmem_limit_bytes=mib * MIB)


def cost(flops, transcendentals, moved):
    return pl.CostEstimate(flops=flops, transcendentals=transcendentals, bytes_accessed=moved)


def neighbours(axis, periodic):
    count = lax.axis_size(axis)
    forward = [(i, i + 1) for i in range(count - 1)]
    if periodic:
        forward.append((count - 1, 0))
    return forward, [(target, source) for source, target in forward]


def halos(top, bottom, left, right):
    lat_up, lat_down = neighbours("lat", False)
    lon_up, lon_down = neighbours("lon", True)
    halo = left.shape[1]
    north = lax.ppermute(bottom, "lat", lat_up)
    south = lax.ppermute(top, "lat", lat_down)
    rights = jnp.concatenate([north[:, -halo:], right, south[:, -halo:]], axis=0)
    lefts = jnp.concatenate([north[:, :halo], left, south[:, :halo]], axis=0)
    west = lax.ppermute(rights, "lon", lon_up)
    east = lax.ppermute(lefts, "lon", lon_down)
    return north, south, west, east


def local(
    background, diffusivity, tile_index, anchor, weights, observed, accept, absorb, sensitivity,
    inverse_variance
):
    f32 = jnp.float32
    lat_count = lax.axis_size("lat")
    lon_count = lax.axis_size("lon")
    dev_count = lat_count * lon_count
    foot_count, channels = observed.shape
    capacity = max(2, 2 * foot_count // dev_count)
    tile_rows, tile_cols, levels = background.shape
    slots = dev_count * capacity
    lanes = 128
    group = lanes // capacity
    cells = tile_rows * tile_cols
    halo = STEPS

    me = lax.axis_index("lat") * lon_count + lax.axis_index("lon")
    lane = (lax.rem(me, group) * capacity).astype(jnp.int32).reshape(1)
    send, slot = pl.pallas_call(
        functools.partial(pack_kernel, dev_count, capacity, tile_cols),
        out_shape=(
            jax.ShapeDtypeStruct((dev_count, capacity + META, channels), f32),
            jax.ShapeDtypeStruct((1, foot_count), jnp.int32),
        ),
        in_specs=[smem()] + [vmem()] * 5,
        out_specs=(vmem(), vmem()),
        scratch_shapes=[pltpu.VMEM((dev_count * META, foot_count), f32)],
        compiler_params=params(60),
        cost_estimate=cost(2 * slots * foot_count * channels * 3, 0, 4 * slots * channels * 3),
        name="pack",
    )(
        lane, tile_index.reshape(1, foot_count), anchor.reshape(1, foot_count), weights.T,
        observed, accept
    )
    recv = lax.all_to_all(send, ("lat", "lon"), split_axis=0, concat_axis=0, tiled=True)

    kappa_halos = halos(
        encode_kappa(diffusivity[:halo]), encode_kappa(diffusivity[-halo:]),
        encode_kappa(diffusivity[:, :halo]), encode_kappa(diffusivity[:, -halo:])
    )
    absorb_wide = pl.pallas_call(
        spread_kernel,
        out_shape=jax.ShapeDtypeStruct((levels, channels, lanes), f32),
        in_specs=[vmem()],
        out_specs=vmem(),
        scratch_shapes=[pltpu.VMEM((channels, levels), f32)],
        compiler_params=params(60),
        cost_estimate=cost(levels * channels * lanes, 0, 4 * levels * channels * lanes),
        name="spread",
    )(absorb)

    wide = 32
    evolved, field, top, bottom, left, right = pl.pallas_call(
        functools.partial(column_kernel, capacity, halo),
        out_shape=(
            jax.ShapeDtypeStruct((dev_count, capacity, channels), f32),
            jax.ShapeDtypeStruct((tile_rows, tile_cols, levels), f32),
            jax.ShapeDtypeStruct((halo + 1, tile_cols, levels), jnp.int16),
            jax.ShapeDtypeStruct((halo + 1, tile_cols, levels), jnp.int16),
            jax.ShapeDtypeStruct((tile_rows + 1, halo, levels), jnp.int16),
            jax.ShapeDtypeStruct((tile_rows + 1, halo, levels), jnp.int16),
        ),
        in_specs=[vmem()] * 2 + [anywhere()] + [vmem()] * 2 + [anywhere()] * 2,
        out_specs=(vmem(),) * 6,
        scratch_shapes=[
            pltpu.SMEM((dev_count, channels), f32),
            pltpu.SemaphoreType.DMA,
            pltpu.SemaphoreType.DMA,
            pltpu.VMEM((cells, levels), f32),
            pltpu.VMEM((levels, channels, lanes), f32),
            pltpu.VMEM((channels, lanes), f32),
            pltpu.VMEM((channels, lanes), f32),
            pltpu.VMEM((4, lanes, levels), f32),
            pltpu.VMEM((4, lanes, levels), f32),
            pltpu.VMEM((levels, lanes), f32),
            pltpu.VMEM((levels, lanes), f32),
            pltpu.VMEM((channels, lanes), f32),
            pltpu.VMEM((channels, lanes), f32),
            pltpu.VMEM((levels, wide, lanes), f32),
            pltpu.VMEM((levels, wide, lanes), f32),
            pltpu.VMEM((levels * 8, lanes), f32),
            pltpu.VMEM((4, cells, levels), f32),
        ],
        compiler_params=params(60),
        cost_estimate=cost(
            14 * slots * levels * channels, 2 * slots * levels * channels, 12 * cells * levels
        ),
        name="column",
    )(
        recv, background, absorb_wide, sensitivity.reshape(1, channels),
        inverse_variance.reshape(1, channels), *kappa_halos[2:]
    )

    field_halos = halos(top, bottom, left, right)
    lat_at = lax.axis_index("lat")
    inside = jnp.stack([lat_at > 0, lat_at < lat_count - 1]).astype(f32)
    height, breadth = tile_rows + 2 * halo, tile_cols + 2 * halo

    plain = pltpu.VMEM((height, breadth, levels), f32)
    mixed = (height, breadth // 8, 8, levels)

    east, south = pl.pallas_call(
        functools.partial(edges_kernel, halo),
        out_shape=(jax.ShapeDtypeStruct(mixed, f32),) * 2,
        in_specs=[smem()] + [vmem()] * 5,
        out_specs=(vmem(),) * 2,
        scratch_shapes=[plain, pltpu.VMEM(mixed, f32)],
        compiler_params=params(22),
        cost_estimate=cost(4 * height * breadth * levels, 0, 12 * cells * levels),
        name="edges",
    )(inside, diffusivity, *kappa_halos)


    evolved = pl.pallas_call(
        lambda *refs: None,
        out_shape=jax.ShapeDtypeStruct(evolved.shape, f32),
        in_specs=[anywhere()] + [vmem()] * 3,
        out_specs=anywhere(),
        input_output_aliases={0: 0},
        name="after_halos",
    )(evolved, field_halos[2][0], field_halos[3][0], east[0, 0])
    returned = lax.all_to_all(evolved, ("lat", "lon"), split_axis=0, concat_axis=0, tiled=True)

    departure = pl.pallas_call(
        depart_kernel,
        out_shape=jax.ShapeDtypeStruct((foot_count, channels), f32),
        in_specs=[vmem()] * 3,
        out_specs=vmem(),
        compiler_params=params(16),
        cost_estimate=cost(2 * slots * foot_count * channels * 3, 0, 4 * slots * channels * 2),
        name="depart",
    )(slot, returned.reshape(slots, channels), observed)

    increment = pl.pallas_call(
        functools.partial(relax_kernel, halo),
        out_shape=jax.ShapeDtypeStruct((tile_rows, tile_cols, levels), f32),
        in_specs=[smem()] + [vmem()] * 7,
        out_specs=vmem(),
        scratch_shapes=[plain, pltpu.VMEM(mixed, f32), pltpu.VMEM(mixed, f32)],
        compiler_params=params(26),
        cost_estimate=cost(10 * STEPS * height * breadth * levels, 0, 16 * cells * levels),
        name="relax",
    )(inside, field, *field_halos, east, south)
    return (departure, increment)


def solution(mesh):
    in_specs = (
        P("lat", "lon", None),
        P("lat", "lon", None),
        P(("lat", "lon"), None),
        P(("lat", "lon")),
        P(("lat", "lon"), None),
        P(("lat", "lon"), None),
        P(("lat", "lon"), None),
        P(),
        P(),
        P(),
    )
    out_specs = (P(("lat", "lon"), None), P("lat", "lon", None))
    return jax.shard_map(local, mesh=mesh, in_specs=in_specs, out_specs=out_specs, check_vma=False)
```

```python
import functools
import math

import jax
import jax.numpy as jnp
from jax import lax
from jax.experimental import pallas as pl
from jax.experimental.pallas import tpu as pltpu
from jax.sharding import PartitionSpec as P


STEPS = 8
REJECTED = 64.0
META = 8
LOG2E = math.log2(math.e)
LN2 = math.log(2.0)
MIB = 1024 * 1024
UNROLL = 16


def thirds(x):
    high = x.astype(jnp.bfloat16)
    rest = x - high.astype(jnp.float32)
    mid = rest.astype(jnp.bfloat16)
    low = (rest - mid.astype(jnp.float32)).astype(jnp.bfloat16)
    return high, mid, low


def dot_f32(a, b, contract):
    return lax.dot_general(a, b, (contract, ((), ())), preferred_element_type=jnp.float32)


def iota(shape, dim):
    return lax.broadcasted_iota(jnp.int32, shape, dim)


def pack_kernel(
    dev_count, capacity, tile_cols, lane_ref, tile_ref, anchor_ref, weights_ref, observed_ref,
    accept_ref, send_ref, slot_ref, vals_ref
):
    foot_count, channels = observed_ref.shape
    bf16 = jnp.bfloat16
    tile = tile_ref[...]
    onehot = jnp.where(iota((dev_count, foot_count), 0) == tile, 1.0, 0.0)
    earlier = jnp.where(
        iota((foot_count, foot_count), 0) < iota((foot_count, foot_count), 1), 1.0, 0.0
    ).astype(bf16)
    before = dot_f32(onehot.astype(bf16), earlier, ((1,), (0,)))
    rank = jnp.sum(before * onehot, axis=0, keepdims=True).astype(jnp.int32)
    slot = tile * capacity + rank
    slot_ref[...] = slot

    chosen = jnp.where(accept_ref[...] != 0, observed_ref[...], REJECTED)
    parts = thirds(chosen)
    per_chunk = max(1, 128 // capacity)
    chunk = per_chunk * capacity
    for start in range(0, dev_count, per_chunk):
        place = jnp.where(
            iota((chunk, foot_count), 0) + start * capacity == slot, 1.0, 0.0
        ).astype(bf16)
        rows = [dot_f32(place, part, ((1,), (0,))) for part in parts]
        rows = (rows[0] + rows[1]) + rows[2]
        send_ref[start : start + per_chunk, :capacity, :] = rows.reshape(
            per_chunk, capacity, channels
        )

    anchor = anchor_ref[...]
    line = jnp.floor((anchor.astype(jnp.float32) + 0.5) * (1.0 / (tile_cols - 1)))
    base = anchor.astype(jnp.float32) + line
    weights = weights_ref[...]
    shares = weights / jnp.sum(weights, axis=0, keepdims=True)
    meta = jnp.concatenate(
        [base, shares, jnp.zeros((META - 5, foot_count), jnp.float32)], axis=0
    )
    for dev in range(dev_count):
        vals_ref[dev * META : (dev + 1) * META, :] = jnp.where(tile == dev, meta, 0.0)
    lanes = jnp.where(
        iota((channels, foot_count), 0) == rank + lane_ref[0], 1.0, 0.0
    ).astype(bf16)
    rows = [dot_f32(part, lanes, ((1,), (1,))) for part in thirds(vals_ref[...])]
    rows = (rows[0] + rows[1]) + rows[2]
    send_ref[:, capacity:, :] = rows.reshape(dev_count, META, channels)


def spread_kernel(absorb_ref, out_ref, turned_ref):
    levels, channels, lanes = out_ref.shape
    turned_ref[...] = (absorb_ref[...] * LOG2E).T

    def some_levels(i, carry):
        turned = turned_ref[...]
        for u in range(8):
            out_ref[i * 8 + u] = jnp.broadcast_to(turned[:, u : u + 1], (channels, lanes))
        turned_ref[...] = pltpu.roll(turned, levels - 8, 1)
        return carry

    lax.fori_loop(0, levels // 8, some_levels, 0)


def column_kernel(
    capacity, halo, recv_ref, background_ref, absorb_any, sensitivity_ref, inverse_ref,
    ready_west, ready_east, evolved_ref, field_ref, top_ref, bottom_ref, left_ref, right_ref,
    base_ref, sem, absorb_sem, cells_ref, absorb_b, slope_b, inverse_b, taken_ref, terms_ref, profile_ref,
    rise_ref, obs_ref, evo_ref, main_ref, side_ref, push_ref, sums_ref
):
    dev_count = recv_ref.shape[0]
    tile_rows, tile_cols, levels = background_ref.shape
    cells = tile_rows * tile_cols
    levels, channels, lanes = absorb_b.shape
    group = lanes // capacity
    blocks = dev_count // group
    wide = main_ref.shape[1]
    per_loop = UNROLL * wide * lanes // (levels * channels)
    corners = (0, 1, tile_cols, tile_cols + 1)

    copy = pltpu.make_async_copy(recv_ref.at[:, capacity, :], base_ref, sem)
    copy.start()
    absorb_copy = pltpu.make_async_copy(absorb_any, absorb_b, absorb_sem)
    absorb_copy.start()

    cells_ref[...] = background_ref[...].reshape(cells, levels).astype(jnp.float32)
    slope_b[...] = jnp.broadcast_to(sensitivity_ref[...] * LOG2E, (lanes, channels)).T
    inverse_b[...] = jnp.broadcast_to(inverse_ref[...], (lanes, channels)).T

    sums_ref[...] = jnp.zeros_like(sums_ref)
    terms_ref[...] = jnp.zeros_like(terms_ref)
    copy.wait()

    def base_of(f, at):
        return base_ref[f * group + lax.div(at, capacity), at].astype(jnp.int32)

    def gather(f, at):
        base = base_of(f, at)
        for k, step in enumerate(corners):
            taken_ref[k, pl.ds(at, 1), :] = cells_ref[pl.ds(base + step, 1), :]

    def scatter(f, at):
        base = base_of(f, at)
        for k, step in enumerate(corners):
            sums_ref[k, pl.ds(base + step, 1), :] += terms_ref[k, pl.ds(at, 1), :]

    def gather_first(i, carry):
        for u in range(8):
            gather(0, i * 8 + u)
        return carry

    lax.fori_loop(0, lanes // 8, gather_first, 0)
    absorb_copy.wait()

    def block(f, carry):
        before = jnp.maximum(f - 1, 0)
        after = jnp.minimum(f + 1, blocks - 1)
        mine = recv_ref[pl.ds(f * group, group)]
        shares = jnp.sum(mine[:, capacity:, :], axis=0)
        obs_ref[...] = mine[:, :capacity, :].reshape(lanes, channels).T
        profile = shares[1:2] * taken_ref[0].T
        for k in range(1, 4):
            profile = profile + shares[k + 1 : k + 2] * taken_ref[k].T
        profile_ref[...] = profile
        rise_ref[0 : levels - 1, :] = profile[1:] - profile[:-1]
        rise_ref[levels - 1 : levels, :] = jnp.zeros((1, lanes), jnp.float32)
        push_ref[...] = jnp.zeros_like(push_ref)

        def some_channels(c, carry):
            at = pl.multiple_of(c * wide, wide)
            slope = slope_b[pl.ds(at, wide), :]
            scale = slope * (LN2 * LN2)

            def down(i, state):
                path, total, above = state
                for u in range(UNROLL):
                    level = i * UNROLL + u
                    depth = absorb_b[level, pl.ds(at, wide), :] * jnp.exp2(
                        slope * profile_ref[pl.ds(level, 1), :]
                    )
                    path = path - depth
                    trans = jnp.exp2(path)
                    side = depth * scale
                    side_ref[level] = side
                    main_ref[level] = (above - trans) + side * total
                    total = total + trans * rise_ref[pl.ds(level, 1), :]
                    above = trans
                for u in range(per_loop):
                    scatter(before, (c * (levels // UNROLL) + i) * per_loop + u)
                return path, total, above

            zero = jnp.zeros((wide, lanes), jnp.float32)
            _, total, last = lax.fori_loop(0, levels // UNROLL, down, (zero, zero, zero + 1.0))
            main_ref[levels - 1] += last
            evolved = total + profile_ref[0:1, :]
            evo_ref[pl.ds(at, wide), :] = evolved
            obs = obs_ref[pl.ds(at, wide), :]
            force = jnp.where(
                obs < 0.5 * REJECTED, inverse_b[pl.ds(at, wide), :] * (obs - evolved), 0.0
            )

            def up(i, carry):
                for u in range(UNROLL):
                    level = i * UNROLL + u
                    push = force * (main_ref[level] - total * side_ref[level])
                    push_ref[pl.ds(pl.multiple_of(level * 8, 8), 8), :] += jnp.sum(
                        push.reshape(wide // 8, 8, lanes), axis=0
                    )
                for u in range(per_loop):
                    gather(after, (c * (levels // UNROLL) + i) * per_loop + u)
                return carry

            lax.fori_loop(0, levels // UNROLL, up, 0)
            return carry

        lax.fori_loop(0, channels // wide, some_channels, 0)
        evolved_ref[pl.ds(f * group, group)] = evo_ref[...].T.reshape(group, capacity, channels)
        push = push_ref[pl.ds(0, levels, stride=8), :]
        for u in range(1, 8):
            push = push + push_ref[pl.ds(u, levels, stride=8), :]
        for k in range(4):
            terms_ref[k] = (shares[k + 1 : k + 2] * push).T
        return carry

    lax.fori_loop(0, blocks, block, 0)

    def scatter_last(i, carry):
        for u in range(8):
            scatter(blocks - 1, i * 8 + u)
        return carry

    lax.fori_loop(0, lanes // 8, scatter_last, 0)

    field = (sums_ref[0] + sums_ref[1]) + (sums_ref[2] + sums_ref[3])
    field = field.reshape(tile_rows, tile_cols, levels)
    field_ref[...] = field

    borders = (
        (top_ref, field[:halo]),
        (bottom_ref, field[tile_rows - halo :]),
        (left_ref, field[:, :halo]),
        (right_ref, field[:, tile_cols - halo :]),
    )
    peak = jnp.full((1, levels), 1e-30, jnp.float32)
    for _, strip in borders:
        peak = jnp.maximum(
            peak, jnp.max(jnp.max(jnp.abs(strip), axis=0), axis=0, keepdims=True)
        )
    power = jnp.ceil(jnp.log2(peak))
    scale = jnp.exp2(15.0 - power)
    for ref, strip in borders:
        count = strip.shape[0]
        whole = jnp.floor(strip * scale + 0.5)
        whole = jnp.clip(whole, -32767.0, 32767.0)
        ref[:count] = whole.astype(jnp.int32).astype(jnp.int16)
        ref[count] = jnp.broadcast_to(power, strip.shape[1:]).astype(jnp.int32).astype(jnp.int16)


def decode_field(coded, power):
    scale = jnp.exp2(power.astype(jnp.int32).astype(jnp.float32) - 15.0)
    return coded.astype(jnp.int32).astype(jnp.float32) * scale


def lay(halo, target, centre, north, south, west, east):
    tile_rows, tile_cols, _ = centre.shape
    breadth = tile_cols + 2 * halo
    mid_r, mid_c = slice(halo, halo + tile_rows), slice(halo, halo + tile_cols)
    target[mid_r, mid_c] = centre[...]
    target[:halo, mid_c] = decode_field(north[:halo], north[halo])
    target[halo + tile_rows :, mid_c] = decode_field(south[:halo], south[halo])
    for side, cols in ((west, slice(0, halo)), (east, slice(halo + tile_cols, breadth))):
        read, put = 0, 0
        for count in (halo, tile_rows, halo):
            target[put : put + count, cols] = decode_field(
                side[read : read + count], side[read + count]
            )
            read, put = read + count + 1, put + count


KAPPA_LOW = 0.12
KAPPA_STEP = 0.125 / 65535


def encode_kappa(x):
    whole = jnp.round((x - KAPPA_LOW) * (1.0 / KAPPA_STEP))
    return (jnp.clip(whole, 0.0, 65535.0) - 32768.0).astype(jnp.int16)


def decode_kappa(x):
    whole = x.astype(jnp.int32).astype(jnp.float32) + 32768.0
    return whole * KAPPA_STEP + KAPPA_LOW


def interleave(plain_ref, target_ref):
    stretch = target_ref.shape[1]

    def row(i, carry):
        for t in range(stretch):
            target_ref[i, t] = plain_ref[i, pl.ds(t, 8, stride=stretch), :]
        return carry

    lax.fori_loop(0, plain_ref.shape[0], row, 0)


def eastward(x):
    return jnp.concatenate([x[1:], pltpu.roll(x[0], 7, 0)[None]], axis=0)


def westward(x):
    return jnp.concatenate([pltpu.roll(x[-1], 1, 0)[None], x[:-1]], axis=0)


def edges_kernel(
    halo, inside_ref, centre_ref, north_ref, south_ref, west_ref, east_side_ref, east_ref,
    south_edge_ref, plain_ref, kappa_ref
):
    tile_rows, tile_cols, _ = centre_ref.shape
    height, _ = plain_ref.shape[:2]
    mid_r, mid_c = slice(halo, halo + tile_rows), slice(halo, halo + tile_cols)
    low, end = slice(0, halo), slice(halo + tile_rows, height)
    plain_ref[mid_r, mid_c] = centre_ref[...]
    plain_ref[:, :halo] = decode_kappa(west_ref[...])
    plain_ref[:, halo + tile_cols :] = decode_kappa(east_side_ref[...])
    plain_ref[low, mid_c] = decode_kappa(north_ref[...])
    plain_ref[end, mid_c] = decode_kappa(south_ref[...])
    plain_ref[low] = plain_ref[low] * inside_ref[0]
    plain_ref[end] = plain_ref[end] * inside_ref[1]
    interleave(plain_ref, kappa_ref)

    def edges(i, carry):
        here = kappa_ref[i]
        east_ref[i] = 0.5 * (here + eastward(here))
        south_edge_ref[i] = 0.5 * (here + kappa_ref[jnp.minimum(i + 1, height - 1)])
        return carry

    lax.fori_loop(0, height, edges, 0)


def relax_kernel(
    halo, inside_ref, centre_ref, north_ref, south_ref, west_ref, east_side_ref, east_ref,
    south_edge_ref, out_ref, plain_ref, first_ref, second_ref
):
    tile_rows, tile_cols, _ = out_ref.shape
    height = tile_rows + 2 * halo
    stretch = first_ref.shape[1]
    lay(halo, plain_ref, centre_ref, north_ref, south_ref, west_ref, east_side_ref)
    interleave(plain_ref, first_ref)

    source, target = first_ref, second_ref
    for step in range(1, halo + 1):
        last = step == halo

        def row(i, carry, scale=None, source=source, target=target, last=last):
            here, from_north = carry
            below = source[i + 1]
            to_east = east_ref[i] * (eastward(here) - here)
            from_south = south_edge_ref[i] * (below - here)
            value = here + (to_east - westward(to_east)) + (from_south - from_north)
            if scale is not None:
                value = value * scale
            if last:
                for t in range(stretch):
                    plain_ref[i, pl.ds(t, 8, stride=stretch), :] = value[t]
            else:
                target[i] = value
            return below, from_south

        here = source[step]
        carry = (here, south_edge_ref[step - 1] * (here - source[step - 1]))
        carry = lax.fori_loop(
            step, halo, functools.partial(row, scale=inside_ref[0]), carry, unroll=True
        )
        carry = lax.fori_loop(halo, halo + tile_rows, row, carry, unroll=4)
        lax.fori_loop(
            halo + tile_rows, height - step, functools.partial(row, scale=inside_ref[1]), carry,
            unroll=True,
        )
        source, target = target, source
    out_ref[...] = plain_ref[halo : halo + tile_rows, halo : halo + tile_cols, :]


def depart_kernel(slot_ref, evolved_ref, observed_ref, out_ref):
    foot_count, _ = observed_ref.shape
    slots = evolved_ref.shape[0]
    slot = slot_ref[...]
    parts = thirds(evolved_ref[...])
    chosen = jnp.where(iota((slots, foot_count), 0) == slot, 1.0, 0.0).astype(jnp.bfloat16)
    rows = [dot_f32(chosen, part, ((0,), (0,))) for part in parts]
    out_ref[...] = observed_ref[...] - ((rows[0] + rows[1]) + rows[2])


def vmem():
    return pl.BlockSpec(memory_space=pltpu.VMEM)


def smem():
    return pl.BlockSpec(memory_space=pltpu.SMEM)


def anywhere():
    return pl.BlockSpec(memory_space=pl.ANY)


def params(mib):
    return pltpu.CompilerParams(vmem_limit_bytes=mib * MIB)


def cost(flops, transcendentals, moved):
    return pl.CostEstimate(flops=flops, transcendentals=transcendentals, bytes_accessed=moved)


def neighbours(axis, periodic):
    count = lax.axis_size(axis)
    forward = [(i, i + 1) for i in range(count - 1)]
    if periodic:
        forward.append((count - 1, 0))
    return forward, [(target, source) for source, target in forward]


def halos(top, bottom, left, right):
    lat_up, lat_down = neighbours("lat", False)
    lon_up, lon_down = neighbours("lon", True)
    halo = left.shape[1]
    north = lax.ppermute(bottom, "lat", lat_up)
    south = lax.ppermute(top, "lat", lat_down)
    rights = jnp.concatenate([north[:, -halo:], right, south[:, -halo:]], axis=0)
    lefts = jnp.concatenate([north[:, :halo], left, south[:, :halo]], axis=0)
    west = lax.ppermute(rights, "lon", lon_up)
    east = lax.ppermute(lefts, "lon", lon_down)
    return north, south, west, east


def local(
    background, diffusivity, tile_index, anchor, weights, observed, accept, absorb, sensitivity,
    inverse_variance
):
    f32 = jnp.float32
    lat_count = lax.axis_size("lat")
    lon_count = lax.axis_size("lon")
    dev_count = lat_count * lon_count
    foot_count, channels = observed.shape
    capacity = max(2, 2 * foot_count // dev_count)
    tile_rows, tile_cols, levels = background.shape
    slots = dev_count * capacity
    lanes = 128
    group = lanes // capacity
    cells = tile_rows * tile_cols
    halo = STEPS

    me = lax.axis_index("lat") * lon_count + lax.axis_index("lon")
    lane = (lax.rem(me, group) * capacity).astype(jnp.int32).reshape(1)
    send, slot = pl.pallas_call(
        functools.partial(pack_kernel, dev_count, capacity, tile_cols),
        out_shape=(
            jax.ShapeDtypeStruct((dev_count, capacity + META, channels), f32),
            jax.ShapeDtypeStruct((1, foot_count), jnp.int32),
        ),
        in_specs=[smem()] + [vmem()] * 5,
        out_specs=(vmem(), vmem()),
        scratch_shapes=[pltpu.VMEM((dev_count * META, foot_count), f32)],
        compiler_params=params(60),
        cost_estimate=cost(2 * slots * foot_count * channels * 3, 0, 4 * slots * channels * 3),
        name="pack",
    )(
        lane, tile_index.reshape(1, foot_count), anchor.reshape(1, foot_count), weights.T,
        observed, accept
    )
    recv = lax.all_to_all(send, ("lat", "lon"), split_axis=0, concat_axis=0, tiled=True)

    kappa_halos = halos(
        encode_kappa(diffusivity[:halo]), encode_kappa(diffusivity[-halo:]),
        encode_kappa(diffusivity[:, :halo]), encode_kappa(diffusivity[:, -halo:])
    )
    absorb_wide = pl.pallas_call(
        spread_kernel,
        out_shape=jax.ShapeDtypeStruct((levels, channels, lanes), f32),
        in_specs=[vmem()],
        out_specs=vmem(),
        scratch_shapes=[pltpu.VMEM((channels, levels), f32)],
        compiler_params=params(60),
        cost_estimate=cost(levels * channels * lanes, 0, 4 * levels * channels * lanes),
        name="spread",
    )(absorb)

    wide = 32
    evolved, field, top, bottom, left, right = pl.pallas_call(
        functools.partial(column_kernel, capacity, halo),
        out_shape=(
            jax.ShapeDtypeStruct((dev_count, capacity, channels), f32),
            jax.ShapeDtypeStruct((tile_rows, tile_cols, levels), f32),
            jax.ShapeDtypeStruct((halo + 1, tile_cols, levels), jnp.int16),
            jax.ShapeDtypeStruct((halo + 1, tile_cols, levels), jnp.int16),
            jax.ShapeDtypeStruct((tile_rows + 1, halo, levels), jnp.int16),
            jax.ShapeDtypeStruct((tile_rows + 1, halo, levels), jnp.int16),
        ),
        in_specs=[vmem()] * 2 + [anywhere()] + [vmem()] * 2 + [anywhere()] * 2,
        out_specs=(vmem(),) * 6,
        scratch_shapes=[
            pltpu.SMEM((dev_count, channels), f32),
            pltpu.SemaphoreType.DMA,
            pltpu.SemaphoreType.DMA,
            pltpu.VMEM((cells, levels), f32),
            pltpu.VMEM((levels, channels, lanes), f32),
            pltpu.VMEM((channels, lanes), f32),
            pltpu.VMEM((channels, lanes), f32),
            pltpu.VMEM((4, lanes, levels), f32),
            pltpu.VMEM((4, lanes, levels), f32),
            pltpu.VMEM((levels, lanes), f32),
            pltpu.VMEM((levels, lanes), f32),
            pltpu.VMEM((channels, lanes), f32),
            pltpu.VMEM((channels, lanes), f32),
            pltpu.VMEM((levels, wide, lanes), f32),
            pltpu.VMEM((levels, wide, lanes), f32),
            pltpu.VMEM((levels * 8, lanes), f32),
            pltpu.VMEM((4, cells, levels), f32),
        ],
        compiler_params=params(60),
        cost_estimate=cost(
            14 * slots * levels * channels, 2 * slots * levels * channels, 12 * cells * levels
        ),
        name="column",
    )(
        recv, background, absorb_wide, sensitivity.reshape(1, channels),
        inverse_variance.reshape(1, channels), *kappa_halos[2:]
    )

    field_halos = halos(top, bottom, left, right)
    lat_at = lax.axis_index("lat")
    inside = jnp.stack([lat_at > 0, lat_at < lat_count - 1]).astype(f32)
    height, breadth = tile_rows + 2 * halo, tile_cols + 2 * halo

    plain = pltpu.VMEM((height, breadth, levels), f32)
    mixed = (height, breadth // 8, 8, levels)

    east, south = pl.pallas_call(
        functools.partial(edges_kernel, halo),
        out_shape=(jax.ShapeDtypeStruct(mixed, f32),) * 2,
        in_specs=[smem()] + [vmem()] * 5,
        out_specs=(vmem(),) * 2,
        scratch_shapes=[plain, pltpu.VMEM(mixed, f32)],
        compiler_params=params(22),
        cost_estimate=cost(4 * height * breadth * levels, 0, 12 * cells * levels),
        name="edges",
    )(inside, diffusivity, *kappa_halos)


    returned = lax.all_to_all(
        evolved, ("lat", "lon"), split_axis=0, concat_axis=0, tiled=True
    )

    departure = pl.pallas_call(
        depart_kernel,
        out_shape=jax.ShapeDtypeStruct((foot_count, channels), f32),
        in_specs=[vmem()] * 3,
        out_specs=vmem(),
        compiler_params=params(16),
        cost_estimate=cost(2 * slots * foot_count * channels * 3, 0, 4 * slots * channels * 2),
        name="depart",
    )(slot, returned.reshape(slots, channels), observed)

    increment = pl.pallas_call(
        functools.partial(relax_kernel, halo),
        out_shape=jax.ShapeDtypeStruct((tile_rows, tile_cols, levels), f32),
        in_specs=[smem()] + [vmem()] * 7,
        out_specs=vmem(),
        scratch_shapes=[plain, pltpu.VMEM(mixed, f32), pltpu.VMEM(mixed, f32)],
        compiler_params=params(26),
        cost_estimate=cost(10 * STEPS * height * breadth * levels, 0, 16 * cells * levels),
        name="relax",
    )(inside, field, *field_halos, east, south)
    return (departure, increment)


def solution(mesh):
    in_specs = (
        P("lat", "lon", None),
        P("lat", "lon", None),
        P(("lat", "lon"), None),
        P(("lat", "lon")),
        P(("lat", "lon"), None),
        P(("lat", "lon"), None),
        P(("lat", "lon"), None),
        P(),
        P(),
        P(),
    )
    out_specs = (P(("lat", "lon"), None), P("lat", "lon", None))

    return jax.shard_map(local, mesh=mesh, in_specs=in_specs, out_specs=out_specs, check_vma=False)
```

```python
import functools
import math

import jax
import jax.numpy as jnp
from jax import lax
from jax.experimental import pallas as pl
from jax.experimental.pallas import tpu as pltpu
from jax.sharding import PartitionSpec as P


STEPS = 8
REJECTED = 64.0
META = 8
LOG2E = math.log2(math.e)
LN2 = math.log(2.0)
MIB = 1024 * 1024
UNROLL = 32


def thirds(x):
    high = x.astype(jnp.bfloat16)
    rest = x - high.astype(jnp.float32)
    mid = rest.astype(jnp.bfloat16)
    low = (rest - mid.astype(jnp.float32)).astype(jnp.bfloat16)
    return high, mid, low


def dot_f32(a, b, contract):
    return lax.dot_general(a, b, (contract, ((), ())), preferred_element_type=jnp.float32)


def iota(shape, dim):
    return lax.broadcasted_iota(jnp.int32, shape, dim)


def pack_kernel(
    dev_count, capacity, tile_cols, lane_ref, tile_ref, anchor_ref, weights_ref, observed_ref,
    accept_ref, send_ref, slot_ref, vals_ref
):
    foot_count, channels = observed_ref.shape
    bf16 = jnp.bfloat16
    tile = tile_ref[...]
    onehot = jnp.where(iota((dev_count, foot_count), 0) == tile, 1.0, 0.0)
    earlier = jnp.where(
        iota((foot_count, foot_count), 0) < iota((foot_count, foot_count), 1), 1.0, 0.0
    ).astype(bf16)
    before = dot_f32(onehot.astype(bf16), earlier, ((1,), (0,)))
    rank = jnp.sum(before * onehot, axis=0, keepdims=True).astype(jnp.int32)
    slot = tile * capacity + rank
    slot_ref[...] = slot

    chosen = jnp.where(accept_ref[...] != 0, observed_ref[...], REJECTED)
    parts = thirds(chosen)
    per_chunk = max(1, 128 // capacity)
    chunk = per_chunk * capacity
    for start in range(0, dev_count, per_chunk):
        place = jnp.where(
            iota((chunk, foot_count), 0) + start * capacity == slot, 1.0, 0.0
        ).astype(bf16)
        rows = [dot_f32(place, part, ((1,), (0,))) for part in parts]
        rows = (rows[0] + rows[1]) + rows[2]
        send_ref[start : start + per_chunk, :capacity, :] = rows.reshape(
            per_chunk, capacity, channels
        )

    anchor = anchor_ref[...]
    line = jnp.floor((anchor.astype(jnp.float32) + 0.5) * (1.0 / (tile_cols - 1)))
    base = anchor.astype(jnp.float32) + line
    weights = weights_ref[...]
    shares = weights / jnp.sum(weights, axis=0, keepdims=True)
    meta = jnp.concatenate(
        [base, shares, jnp.zeros((META - 5, foot_count), jnp.float32)], axis=0
    )
    for dev in range(dev_count):
        vals_ref[dev * META : (dev + 1) * META, :] = jnp.where(tile == dev, meta, 0.0)
    lanes = jnp.where(
        iota((channels, foot_count), 0) == rank + lane_ref[0], 1.0, 0.0
    ).astype(bf16)
    rows = [dot_f32(part, lanes, ((1,), (1,))) for part in thirds(vals_ref[...])]
    rows = (rows[0] + rows[1]) + rows[2]
    send_ref[:, capacity:, :] = rows.reshape(dev_count, META, channels)


def spread_kernel(absorb_ref, out_ref, turned_ref):
    some, channels, lanes = out_ref.shape
    levels = absorb_ref.shape[0]

    @pl.when(pl.program_id(0) == 0)
    def _():
        turned_ref[...] = (absorb_ref[...] * LOG2E).T

    turned = turned_ref[...]
    for u in range(some):
        out_ref[u] = jnp.broadcast_to(turned[:, u : u + 1], (channels, lanes))
    turned_ref[...] = pltpu.roll(turned, levels - some, 1)


def column_kernel(
    capacity, halo, recv_ref, background_ref, absorb_any, sensitivity_ref, inverse_ref,
    ready_west, ready_east, evolved_ref, field_ref, top_ref, bottom_ref, left_ref, right_ref,
    base_ref, sem, absorb_sem, cells_ref, absorb_b, slope_b, inverse_b, taken_ref, terms_ref, profile_ref,
    rise_ref, obs_ref, evo_ref, main_ref, side_ref, push_ref, sums_ref
):
    dev_count = recv_ref.shape[0]
    tile_rows, tile_cols, levels = background_ref.shape
    cells = tile_rows * tile_cols
    levels, channels, lanes = absorb_b.shape
    group = lanes // capacity
    blocks = dev_count // group
    wide = main_ref.shape[1]
    per_loop = UNROLL * wide * lanes // (levels * channels)
    corners = (0, 1, tile_cols, tile_cols + 1)

    copy = pltpu.make_async_copy(recv_ref.at[:, capacity, :], base_ref, sem)
    copy.start()
    absorb_copy = pltpu.make_async_copy(absorb_any, absorb_b, absorb_sem)
    absorb_copy.start()

    cells_ref[...] = background_ref[...].reshape(cells, levels).astype(jnp.float32)
    slope_b[...] = jnp.broadcast_to(sensitivity_ref[...] * LOG2E, (lanes, channels)).T
    inverse_b[...] = jnp.broadcast_to(inverse_ref[...], (lanes, channels)).T

    sums_ref[...] = jnp.zeros_like(sums_ref)
    terms_ref[...] = jnp.zeros_like(terms_ref)
    copy.wait()

    def base_of(f, at):
        return base_ref[f * group + lax.div(at, capacity), at].astype(jnp.int32)

    def gather(f, at):
        base = base_of(f, at)
        for k, step in enumerate(corners):
            taken_ref[k, pl.ds(at, 1), :] = cells_ref[pl.ds(base + step, 1), :]

    def scatter(f, at):
        base = base_of(f, at)
        for k, step in enumerate(corners):
            sums_ref[k, pl.ds(base + step, 1), :] += terms_ref[k, pl.ds(at, 1), :]

    def gather_first(i, carry):
        for u in range(8):
            gather(0, i * 8 + u)
        return carry

    lax.fori_loop(0, lanes // 8, gather_first, 0)
    absorb_copy.wait()

    def block(f, carry):
        before = jnp.maximum(f - 1, 0)
        after = jnp.minimum(f + 1, blocks - 1)
        mine = recv_ref[pl.ds(f * group, group)]
        shares = jnp.sum(mine[:, capacity:, :], axis=0)
        obs_ref[...] = mine[:, :capacity, :].reshape(lanes, channels).T
        profile = shares[1:2] * taken_ref[0].T
        for k in range(1, 4):
            profile = profile + shares[k + 1 : k + 2] * taken_ref[k].T
        profile_ref[...] = profile
        rise_ref[0 : levels - 1, :] = profile[1:] - profile[:-1]
        rise_ref[levels - 1 : levels, :] = jnp.zeros((1, lanes), jnp.float32)
        push_ref[...] = jnp.zeros_like(push_ref)

        def some_channels(c, carry):
            at = pl.multiple_of(c * wide, wide)
            slope = slope_b[pl.ds(at, wide), :]
            scale = slope * (LN2 * LN2)

            def down(i, state):
                path, total, above = state
                for u in range(UNROLL):
                    level = i * UNROLL + u
                    depth = absorb_b[level, pl.ds(at, wide), :] * jnp.exp2(
                        slope * profile_ref[pl.ds(level, 1), :]
                    )
                    path = path - depth
                    trans = jnp.exp2(path)
                    side = depth * scale
                    side_ref[level] = side
                    main_ref[level] = (above - trans) + side * total
                    total = total + trans * rise_ref[pl.ds(level, 1), :]
                    above = trans
                for u in range(per_loop):
                    scatter(before, (c * (levels // UNROLL) + i) * per_loop + u)
                return path, total, above

            zero = jnp.zeros((wide, lanes), jnp.float32)
            _, total, last = lax.fori_loop(0, levels // UNROLL, down, (zero, zero, zero + 1.0))
            main_ref[levels - 1] += last
            evolved = total + profile_ref[0:1, :]
            evo_ref[pl.ds(at, wide), :] = evolved
            obs = obs_ref[pl.ds(at, wide), :]
            force = jnp.where(
                obs < 0.5 * REJECTED, inverse_b[pl.ds(at, wide), :] * (obs - evolved), 0.0
            )

            def up(i, carry):
                for u in range(UNROLL):
                    level = i * UNROLL + u
                    push = force * (main_ref[level] - total * side_ref[level])
                    push_ref[pl.ds(pl.multiple_of(level * 8, 8), 8), :] += jnp.sum(
                        push.reshape(wide // 8, 8, lanes), axis=0
                    )
                for u in range(per_loop):
                    gather(after, (c * (levels // UNROLL) + i) * per_loop + u)
                return carry

            lax.fori_loop(0, levels // UNROLL, up, 0)
            return carry

        lax.fori_loop(0, channels // wide, some_channels, 0)
        evolved_ref[pl.ds(f * group, group)] = evo_ref[...].T.reshape(group, capacity, channels)
        push = push_ref[pl.ds(0, levels, stride=8), :]
        for u in range(1, 8):
            push = push + push_ref[pl.ds(u, levels, stride=8), :]
        for k in range(4):
            terms_ref[k] = (shares[k + 1 : k + 2] * push).T
        return carry

    lax.fori_loop(0, blocks, block, 0)

    def scatter_last(i, carry):
        for u in range(8):
            scatter(blocks - 1, i * 8 + u)
        return carry

    lax.fori_loop(0, lanes // 8, scatter_last, 0)

    field = (sums_ref[0] + sums_ref[1]) + (sums_ref[2] + sums_ref[3])
    field = field.reshape(tile_rows, tile_cols, levels)
    field_ref[...] = field

    borders = (
        (top_ref, 0, field[:halo]),
        (bottom_ref, 0, field[tile_rows - halo :]),
        (left_ref, halo + 1, field[:, :halo]),
        (right_ref, halo + 1, field[:, tile_cols - halo :]),
    )
    peak = jnp.full((1, levels), 1e-30, jnp.float32)
    for _, _, strip in borders:
        peak = jnp.maximum(
            peak, jnp.max(jnp.max(jnp.abs(strip), axis=0), axis=0, keepdims=True)
        )
    power = jnp.ceil(jnp.log2(peak))
    scale = jnp.exp2(15.0 - power)
    for ref, first, strip in borders:
        last = first + strip.shape[0]
        whole = jnp.floor(strip * scale + 0.5)
        whole = jnp.clip(whole, -32767.0, 32767.0)
        ref[first:last] = whole.astype(jnp.int32).astype(jnp.int16)
        ref[last] = jnp.broadcast_to(power, strip.shape[1:]).astype(jnp.int32).astype(jnp.int16)


def decode_field(coded, power):
    scale = jnp.exp2(power.astype(jnp.int32).astype(jnp.float32) - 15.0)
    return coded.astype(jnp.int32).astype(jnp.float32) * scale


def lay(halo, target, centre, north, south, west, east):
    tile_rows, tile_cols, _ = centre.shape
    breadth = tile_cols + 2 * halo
    mid_r, mid_c = slice(halo, halo + tile_rows), slice(halo, halo + tile_cols)
    target[mid_r, mid_c] = centre[...]
    target[:halo, mid_c] = decode_field(north[:halo], north[halo])
    target[halo + tile_rows :, mid_c] = decode_field(south[:halo], south[halo])
    for side, cols in ((west, slice(0, halo)), (east, slice(halo + tile_cols, breadth))):
        read, put = 0, 0
        for count in (halo, tile_rows, halo):
            target[put : put + count, cols] = decode_field(
                side[read : read + count], side[read + count]
            )
            read, put = read + count + 1, put + count


KAPPA_LOW = 0.12
KAPPA_STEP = 0.125 / 65535


def encode_kappa(x):
    whole = jnp.round((x - KAPPA_LOW) * (1.0 / KAPPA_STEP))
    return (jnp.clip(whole, 0.0, 65535.0) - 32768.0).astype(jnp.int16)


def decode_kappa(x):
    whole = x.astype(jnp.int32).astype(jnp.float32) + 32768.0
    return whole * KAPPA_STEP + KAPPA_LOW


def interleave(plain_ref, target_ref):
    stretch = target_ref.shape[1]

    def row(i, carry):
        for t in range(stretch):
            target_ref[i, t] = plain_ref[i, pl.ds(t, 8, stride=stretch), :]
        return carry

    lax.fori_loop(0, plain_ref.shape[0], row, 0)


def eastward(x):
    return jnp.concatenate([x[1:], pltpu.roll(x[0], 7, 0)[None]], axis=0)


def westward(x):
    return jnp.concatenate([pltpu.roll(x[-1], 1, 0)[None], x[:-1]], axis=0)


def edges_kernel(
    halo, inside_ref, centre_ref, north_ref, south_ref, west_hbm, east_hbm, east_ref,
    south_edge_ref, plain_ref, kappa_ref, west_ref, east_side_ref, sems
):
    copies = [
        pltpu.make_async_copy(west_hbm, west_ref, sems.at[0]),
        pltpu.make_async_copy(east_hbm, east_side_ref, sems.at[1]),
    ]
    for copy in copies:
        copy.start()
    tile_rows, tile_cols, _ = centre_ref.shape
    height, _ = plain_ref.shape[:2]
    mid_r, mid_c = slice(halo, halo + tile_rows), slice(halo, halo + tile_cols)
    low, end = slice(0, halo), slice(halo + tile_rows, height)
    plain_ref[mid_r, mid_c] = centre_ref[...]
    plain_ref[low, mid_c] = decode_kappa(north_ref[...])
    plain_ref[end, mid_c] = decode_kappa(south_ref[...])
    for copy in copies:
        copy.wait()
    plain_ref[:, :halo] = decode_kappa(west_ref[...])
    plain_ref[:, halo + tile_cols :] = decode_kappa(east_side_ref[...])
    plain_ref[low] = plain_ref[low] * inside_ref[0]
    plain_ref[end] = plain_ref[end] * inside_ref[1]
    interleave(plain_ref, kappa_ref)

    def edges(i, carry):
        here = kappa_ref[i]
        east_ref[i] = 0.5 * (here + eastward(here))
        south_edge_ref[i] = 0.5 * (here + kappa_ref[jnp.minimum(i + 1, height - 1)])
        return carry

    lax.fori_loop(0, height, edges, 0)


def relax_kernel(
    halo, inside_ref, centre_ref, north_ref, south_ref, west_ref, east_side_ref, east_ref,
    south_edge_ref, out_ref, plain_ref, first_ref, second_ref
):
    tile_rows, tile_cols, _ = out_ref.shape
    height = tile_rows + 2 * halo
    stretch = first_ref.shape[1]
    lay(halo, plain_ref, centre_ref, north_ref, south_ref, west_ref, east_side_ref)
    interleave(plain_ref, first_ref)

    source, target = first_ref, second_ref
    for step in range(1, halo + 1):
        last = step == halo

        def row(i, carry, scale=None, source=source, target=target, last=last):
            here, from_north = carry
            below = source[i + 1]
            to_east = east_ref[i] * (eastward(here) - here)
            from_south = south_edge_ref[i] * (below - here)
            value = here + (to_east - westward(to_east)) + (from_south - from_north)
            if scale is not None:
                value = value * scale
            if last:
                for t in range(stretch):
                    plain_ref[i, pl.ds(t, 8, stride=stretch), :] = value[t]
            else:
                target[i] = value
            return below, from_south

        here = source[step]
        carry = (here, south_edge_ref[step - 1] * (here - source[step - 1]))
        carry = lax.fori_loop(
            step, halo, functools.partial(row, scale=inside_ref[0]), carry, unroll=True
        )
        carry = lax.fori_loop(halo, halo + tile_rows, row, carry, unroll=4)
        lax.fori_loop(
            halo + tile_rows, height - step, functools.partial(row, scale=inside_ref[1]), carry,
            unroll=True,
        )
        source, target = target, source
    out_ref[...] = plain_ref[halo : halo + tile_rows, halo : halo + tile_cols, :]


def depart_kernel(slot_ref, evolved_ref, observed_ref, out_ref):
    foot_count, _ = observed_ref.shape
    slots = evolved_ref.shape[0]
    slot = slot_ref[...]
    parts = thirds(evolved_ref[...])
    chosen = jnp.where(iota((slots, foot_count), 0) == slot, 1.0, 0.0).astype(jnp.bfloat16)
    rows = [dot_f32(chosen, part, ((0,), (0,))) for part in parts]
    out_ref[...] = observed_ref[...] - ((rows[0] + rows[1]) + rows[2])


def vmem():
    return pl.BlockSpec(memory_space=pltpu.VMEM)


def smem():
    return pl.BlockSpec(memory_space=pltpu.SMEM)


def hbm():
    return pl.BlockSpec(memory_space=pltpu.HBM)


def params(mib):
    return pltpu.CompilerParams(vmem_limit_bytes=mib * MIB)


def cost(flops, transcendentals, moved):
    return pl.CostEstimate(flops=flops, transcendentals=transcendentals, bytes_accessed=moved)


def neighbours(axis, periodic):
    count = lax.axis_size(axis)
    forward = [(i, i + 1) for i in range(count - 1)]
    if periodic:
        forward.append((count - 1, 0))
    return forward, [(target, source) for source, target in forward]


def join(north, south, left, right):
    halo = left.shape[1]
    right = jnp.concatenate([north[:, -halo:], right, south[:, -halo:]], axis=0)
    left = jnp.concatenate([north[:, :halo], left, south[:, :halo]], axis=0)
    return left, right


def join_kernel(north_ref, south_ref, _, __, left_ref, right_ref, sems):
    count, tile_cols, _ = north_ref.shape
    total, halo, _ = left_ref.shape
    copies = []
    for target, cols in ((left_ref, 0), (right_ref, tile_cols - halo)):
        for source, row in ((north_ref, 0), (south_ref, total - count)):
            copies.append(
                pltpu.make_async_copy(
                    source.at[:, pl.ds(cols, halo)], target.at[pl.ds(row, count)],
                    sems.at[len(copies)],
                )
            )
    for copy in copies:
        copy.start()
    for copy in copies:
        copy.wait()


def join_in_place(north, south, left, right):
    return pl.pallas_call(
        join_kernel,
        out_shape=tuple(jax.ShapeDtypeStruct(x.shape, x.dtype) for x in (left, right)),
        in_specs=[vmem()] * 2 + [hbm()] * 2,
        out_specs=(hbm(), hbm()),
        input_output_aliases={2: 0, 3: 1},
        scratch_shapes=[pltpu.SemaphoreType.DMA((4,))],
        compiler_params=params(2),
        name="join",
    )(north, south, left, right)


def halos(top, bottom, left, right, join):
    lat_up, lat_down = neighbours("lat", False)
    lon_up, lon_down = neighbours("lon", True)
    north = lax.ppermute(bottom, "lat", lat_up)
    south = lax.ppermute(top, "lat", lat_down)
    lefts, rights = join(north, south, left, right)
    west = lax.ppermute(rights, "lon", lon_up)
    east = lax.ppermute(lefts, "lon", lon_down)
    return north, south, west, east


def local(
    background, diffusivity, tile_index, anchor, weights, observed, accept, absorb, sensitivity,
    inverse_variance
):
    f32 = jnp.float32
    lat_count = lax.axis_size("lat")
    lon_count = lax.axis_size("lon")
    dev_count = lat_count * lon_count
    foot_count, channels = observed.shape
    capacity = max(2, 2 * foot_count // dev_count)
    tile_rows, tile_cols, levels = background.shape
    slots = dev_count * capacity
    lanes = 128
    group = lanes // capacity
    cells = tile_rows * tile_cols
    halo = STEPS

    me = lax.axis_index("lat") * lon_count + lax.axis_index("lon")
    lane = (lax.rem(me, group) * capacity).astype(jnp.int32).reshape(1)
    send, slot = pl.pallas_call(
        functools.partial(pack_kernel, dev_count, capacity, tile_cols),
        out_shape=(
            jax.ShapeDtypeStruct((dev_count, capacity + META, channels), f32),
            jax.ShapeDtypeStruct((1, foot_count), jnp.int32),
        ),
        in_specs=[smem()] + [vmem()] * 5,
        out_specs=(vmem(), vmem()),
        scratch_shapes=[pltpu.VMEM((dev_count * META, foot_count), f32)],
        compiler_params=params(60),
        cost_estimate=cost(2 * slots * foot_count * channels * 3, 0, 4 * slots * channels * 3),
        name="pack",
    )(
        lane, tile_index.reshape(1, foot_count), anchor.reshape(1, foot_count), weights.T,
        observed, accept
    )
    recv = lax.all_to_all(send, ("lat", "lon"), split_axis=0, concat_axis=0, tiled=True)

    kappa_halos = halos(
        encode_kappa(diffusivity[:halo]), encode_kappa(diffusivity[-halo:]),
        encode_kappa(diffusivity[:, :halo]), encode_kappa(diffusivity[:, -halo:]), join
    )
    absorb_wide = pl.pallas_call(
        spread_kernel,
        out_shape=jax.ShapeDtypeStruct((levels, channels, lanes), f32),
        grid=(levels // 16,),
        in_specs=[pl.BlockSpec((levels, channels), lambda i: (0, 0))],
        out_specs=pl.BlockSpec((16, channels, lanes), lambda i: (i, 0, 0)),
        scratch_shapes=[pltpu.VMEM((channels, levels), f32)],
        compiler_params=params(60),
        cost_estimate=cost(levels * channels * lanes, 0, 4 * levels * channels * lanes),
        name="spread",
    )(absorb)

    wide = 32
    evolved, field, top, bottom, left, right = pl.pallas_call(
        functools.partial(column_kernel, capacity, halo),
        out_shape=(
            jax.ShapeDtypeStruct((dev_count, capacity, channels), f32),
            jax.ShapeDtypeStruct((tile_rows, tile_cols, levels), f32),
            jax.ShapeDtypeStruct((halo + 1, tile_cols, levels), jnp.int16),
            jax.ShapeDtypeStruct((halo + 1, tile_cols, levels), jnp.int16),
            jax.ShapeDtypeStruct((tile_rows + 2 * halo + 3, halo, levels), jnp.int16),
            jax.ShapeDtypeStruct((tile_rows + 2 * halo + 3, halo, levels), jnp.int16),
        ),
        in_specs=[vmem()] * 2 + [hbm()] + [vmem()] * 2 + [hbm()] * 2,
        out_specs=(vmem(),) * 6,
        scratch_shapes=[
            pltpu.SMEM((dev_count, channels), f32),
            pltpu.SemaphoreType.DMA,
            pltpu.SemaphoreType.DMA,
            pltpu.VMEM((cells, levels), f32),
            pltpu.VMEM((levels, channels, lanes), f32),
            pltpu.VMEM((channels, lanes), f32),
            pltpu.VMEM((channels, lanes), f32),
            pltpu.VMEM((4, lanes, levels), f32),
            pltpu.VMEM((4, lanes, levels), f32),
            pltpu.VMEM((levels, lanes), f32),
            pltpu.VMEM((levels, lanes), f32),
            pltpu.VMEM((channels, lanes), f32),
            pltpu.VMEM((channels, lanes), f32),
            pltpu.VMEM((levels, wide, lanes), f32),
            pltpu.VMEM((levels, wide, lanes), f32),
            pltpu.VMEM((levels * 8, lanes), f32),
            pltpu.VMEM((4, cells, levels), f32),
        ],
        compiler_params=params(60),
        cost_estimate=cost(
            14 * slots * levels * channels, 2 * slots * levels * channels, 12 * cells * levels
        ),
        name="column",
    )(
        recv, background, absorb_wide, sensitivity.reshape(1, channels),
        inverse_variance.reshape(1, channels), *kappa_halos[2:]
    )

    field_halos = halos(top, bottom, left, right, join_in_place)
    lat_at = lax.axis_index("lat")
    inside = jnp.stack([lat_at > 0, lat_at < lat_count - 1]).astype(f32)
    height, breadth = tile_rows + 2 * halo, tile_cols + 2 * halo

    plain = pltpu.VMEM((height, breadth, levels), f32)
    mixed = (height, breadth // 8, 8, levels)

    east, south = pl.pallas_call(
        functools.partial(edges_kernel, halo),
        out_shape=(jax.ShapeDtypeStruct(mixed, f32),) * 2,
        in_specs=[smem()] + [vmem()] * 3 + [hbm()] * 2,
        out_specs=(vmem(),) * 2,
        scratch_shapes=[plain, pltpu.VMEM(mixed, f32)]
        + [pltpu.VMEM((height, halo, levels), jnp.int16)] * 2
        + [pltpu.SemaphoreType.DMA((2,))],
        compiler_params=params(22),
        cost_estimate=cost(4 * height * breadth * levels, 0, 12 * cells * levels),
        name="edges",
    )(inside, diffusivity, *kappa_halos)


    returned = lax.all_to_all(
        evolved, ("lat", "lon"), split_axis=0, concat_axis=0, tiled=True
    )

    departure = pl.pallas_call(
        depart_kernel,
        out_shape=jax.ShapeDtypeStruct((foot_count, channels), f32),
        in_specs=[vmem()] * 3,
        out_specs=vmem(),
        compiler_params=params(16),
        cost_estimate=cost(2 * slots * foot_count * channels * 3, 0, 4 * slots * channels * 2),
        name="depart",
    )(slot, returned.reshape(slots, channels), observed)

    increment = pl.pallas_call(
        functools.partial(relax_kernel, halo),
        out_shape=jax.ShapeDtypeStruct((tile_rows, tile_cols, levels), f32),
        in_specs=[smem()] + [vmem()] * 7,
        out_specs=vmem(),
        scratch_shapes=[plain, pltpu.VMEM(mixed, f32), pltpu.VMEM(mixed, f32)],
        compiler_params=params(26),
        cost_estimate=cost(10 * STEPS * height * breadth * levels, 0, 16 * cells * levels),
        name="relax",
    )(inside, field, *field_halos, east, south)
    return (departure, increment)


def solution(mesh):
    in_specs = (
        P("lat", "lon", None),
        P("lat", "lon", None),
        P(("lat", "lon"), None),
        P(("lat", "lon")),
        P(("lat", "lon"), None),
        P(("lat", "lon"), None),
        P(("lat", "lon"), None),
        P(),
        P(),
        P(),
    )
    out_specs = (P(("lat", "lon"), None), P("lat", "lon", None))

    return jax.shard_map(local, mesh=mesh, in_specs=in_specs, out_specs=out_specs, check_vma=False)
```

```python
import functools
import math

import jax
import jax.numpy as jnp
from jax import lax
from jax.experimental import pallas as pl
from jax.experimental.pallas import tpu as pltpu
from jax.sharding import PartitionSpec as P


STEPS = 8
REJECTED = 64.0
META = 8
LOG2E = math.log2(math.e)
LN2 = math.log(2.0)
MIB = 1024 * 1024
UNROLL = 32


def thirds(x):
    high = x.astype(jnp.bfloat16)
    rest = x - high.astype(jnp.float32)
    mid = rest.astype(jnp.bfloat16)
    low = (rest - mid.astype(jnp.float32)).astype(jnp.bfloat16)
    return high, mid, low


def dot_f32(a, b, contract):
    return lax.dot_general(a, b, (contract, ((), ())), preferred_element_type=jnp.float32)


def iota(shape, dim):
    return lax.broadcasted_iota(jnp.int32, shape, dim)


def pack_kernel(
    dev_count, capacity, tile_cols, lane_ref, tile_ref, anchor_ref, weights_ref, observed_ref,
    accept_ref, send_ref, slot_ref, vals_ref
):
    foot_count, channels = observed_ref.shape
    bf16 = jnp.bfloat16
    tile = tile_ref[...]
    onehot = jnp.where(iota((dev_count, foot_count), 0) == tile, 1.0, 0.0)
    earlier = jnp.where(
        iota((foot_count, foot_count), 0) < iota((foot_count, foot_count), 1), 1.0, 0.0
    ).astype(bf16)
    before = dot_f32(onehot.astype(bf16), earlier, ((1,), (0,)))
    rank = jnp.sum(before * onehot, axis=0, keepdims=True).astype(jnp.int32)
    slot = tile * capacity + rank
    slot_ref[...] = slot

    chosen = jnp.where(accept_ref[...] != 0, observed_ref[...], REJECTED)
    parts = thirds(chosen)
    per_chunk = max(1, 128 // capacity)
    chunk = per_chunk * capacity
    for start in range(0, dev_count, per_chunk):
        place = jnp.where(
            iota((chunk, foot_count), 0) + start * capacity == slot, 1.0, 0.0
        ).astype(bf16)
        rows = [dot_f32(place, part, ((1,), (0,))) for part in parts]
        rows = (rows[0] + rows[1]) + rows[2]
        send_ref[start : start + per_chunk, :capacity, :] = rows.reshape(
            per_chunk, capacity, channels
        )

    anchor = anchor_ref[...]
    line = jnp.floor((anchor.astype(jnp.float32) + 0.5) * (1.0 / (tile_cols - 1)))
    base = anchor.astype(jnp.float32) + line
    weights = weights_ref[...]
    shares = weights / jnp.sum(weights, axis=0, keepdims=True)
    meta = jnp.concatenate(
        [base, shares, jnp.zeros((META - 5, foot_count), jnp.float32)], axis=0
    )
    for dev in range(dev_count):
        vals_ref[dev * META : (dev + 1) * META, :] = jnp.where(tile == dev, meta, 0.0)
    lanes = jnp.where(
        iota((channels, foot_count), 0) == rank + lane_ref[0], 1.0, 0.0
    ).astype(bf16)
    rows = [dot_f32(part, lanes, ((1,), (1,))) for part in thirds(vals_ref[...])]
    rows = (rows[0] + rows[1]) + rows[2]
    send_ref[:, capacity:, :] = rows.reshape(dev_count, META, channels)


def spread_kernel(absorb_ref, out_ref, turned_ref):
    some, channels, lanes = out_ref.shape
    levels = absorb_ref.shape[0]

    @pl.when(pl.program_id(0) == 0)
    def _():
        turned_ref[...] = (absorb_ref[...] * LOG2E).T

    turned = turned_ref[...]
    for u in range(some):
        out_ref[u] = jnp.broadcast_to(turned[:, u : u + 1], (channels, lanes))
    turned_ref[...] = pltpu.roll(turned, levels - some, 1)


def column_kernel(
    capacity, halo, recv_ref, background_ref, absorb_any, sensitivity_ref, inverse_ref,
    ready_west, ready_east, evolved_ref, field_ref, top_ref, bottom_ref, left_ref, right_ref,
    base_ref, sem, absorb_sem, cells_ref, absorb_b, slope_b, inverse_b, taken_ref, terms_ref, profile_ref,
    rise_ref, obs_ref, evo_ref, main_ref, side_ref, push_ref, sums_ref
):
    dev_count = recv_ref.shape[0]
    tile_rows, tile_cols, levels = background_ref.shape
    cells = tile_rows * tile_cols
    levels, channels, lanes = absorb_b.shape
    group = lanes // capacity
    blocks = dev_count // group
    wide = main_ref.shape[1]
    per_loop = UNROLL * wide * lanes // (levels * channels)
    corners = (0, 1, tile_cols, tile_cols + 1)

    copy = pltpu.make_async_copy(recv_ref.at[:, capacity, :], base_ref, sem)
    copy.start()

    def absorb_copy(c):
        some = pl.ds(pl.multiple_of(c * wide, wide), wide)
        return pltpu.make_async_copy(
            absorb_any.at[:, some, :], absorb_b.at[:, some, :], absorb_sem.at[c]
        )

    for c in range(channels // wide):
        absorb_copy(c).start()

    cells_ref[...] = background_ref[...].reshape(cells, levels).astype(jnp.float32)
    slope_b[...] = jnp.broadcast_to(sensitivity_ref[...] * LOG2E, (lanes, channels)).T
    inverse_b[...] = jnp.broadcast_to(inverse_ref[...], (lanes, channels)).T

    sums_ref[...] = jnp.zeros_like(sums_ref)
    terms_ref[...] = jnp.zeros_like(terms_ref)
    copy.wait()

    def base_of(f, at):
        return base_ref[f * group + lax.div(at, capacity), at].astype(jnp.int32)

    def gather(f, at):
        base = base_of(f, at)
        for k, step in enumerate(corners):
            taken_ref[k, pl.ds(at, 1), :] = cells_ref[pl.ds(base + step, 1), :]

    def scatter(f, at):
        base = base_of(f, at)
        for k, step in enumerate(corners):
            sums_ref[k, pl.ds(base + step, 1), :] += terms_ref[k, pl.ds(at, 1), :]

    def gather_first(i, carry):
        for u in range(8):
            gather(0, i * 8 + u)
        return carry

    lax.fori_loop(0, lanes // 8, gather_first, 0)

    def block(f, carry):
        before = jnp.maximum(f - 1, 0)
        after = jnp.minimum(f + 1, blocks - 1)
        mine = recv_ref[pl.ds(f * group, group)]
        shares = jnp.sum(mine[:, capacity:, :], axis=0)
        obs_ref[...] = mine[:, :capacity, :].reshape(lanes, channels).T
        profile = shares[1:2] * taken_ref[0].T
        for k in range(1, 4):
            profile = profile + shares[k + 1 : k + 2] * taken_ref[k].T
        profile_ref[...] = profile
        rise_ref[0 : levels - 1, :] = profile[1:] - profile[:-1]
        rise_ref[levels - 1 : levels, :] = jnp.zeros((1, lanes), jnp.float32)
        push_ref[...] = jnp.zeros_like(push_ref)

        def some_channels(c, carry):
            @pl.when(f == 0)
            def _():
                absorb_copy(c).wait()

            at = pl.multiple_of(c * wide, wide)
            slope = slope_b[pl.ds(at, wide), :]
            scale = slope * (LN2 * LN2)

            def down(i, state):
                path, total, above = state
                for u in range(UNROLL):
                    level = i * UNROLL + u
                    depth = absorb_b[level, pl.ds(at, wide), :] * jnp.exp2(
                        slope * profile_ref[pl.ds(level, 1), :]
                    )
                    path = path - depth
                    trans = jnp.exp2(path)
                    side = depth * scale
                    side_ref[level] = side
                    main_ref[level] = (above - trans) + side * total
                    total = total + trans * rise_ref[pl.ds(level, 1), :]
                    above = trans
                for u in range(per_loop):
                    scatter(before, (c * (levels // UNROLL) + i) * per_loop + u)
                return path, total, above

            zero = jnp.zeros((wide, lanes), jnp.float32)
            _, total, last = lax.fori_loop(0, levels // UNROLL, down, (zero, zero, zero + 1.0))
            main_ref[levels - 1] += last
            evolved = total + profile_ref[0:1, :]
            evo_ref[pl.ds(at, wide), :] = evolved
            obs = obs_ref[pl.ds(at, wide), :]
            force = jnp.where(
                obs < 0.5 * REJECTED, inverse_b[pl.ds(at, wide), :] * (obs - evolved), 0.0
            )

            def up(i, carry):
                for u in range(UNROLL):
                    level = i * UNROLL + u
                    push = force * (main_ref[level] - total * side_ref[level])
                    push_ref[pl.ds(pl.multiple_of(level * 8, 8), 8), :] += jnp.sum(
                        push.reshape(wide // 8, 8, lanes), axis=0
                    )
                for u in range(per_loop):
                    gather(after, (c * (levels // UNROLL) + i) * per_loop + u)
                return carry

            lax.fori_loop(0, levels // UNROLL, up, 0)
            return carry

        lax.fori_loop(0, channels // wide, some_channels, 0)
        evolved_ref[pl.ds(f * group, group)] = evo_ref[...].T.reshape(group, capacity, channels)
        push = push_ref[pl.ds(0, levels, stride=8), :]
        for u in range(1, 8):
            push = push + push_ref[pl.ds(u, levels, stride=8), :]
        for k in range(4):
            terms_ref[k] = (shares[k + 1 : k + 2] * push).T
        return carry

    lax.fori_loop(0, blocks, block, 0)

    def scatter_last(i, carry):
        for u in range(8):
            scatter(blocks - 1, i * 8 + u)
        return carry

    lax.fori_loop(0, lanes // 8, scatter_last, 0)

    field = (sums_ref[0] + sums_ref[1]) + (sums_ref[2] + sums_ref[3])
    field = field.reshape(tile_rows, tile_cols, levels)
    field_ref[...] = field

    borders = (
        (top_ref, 0, field[:halo]),
        (bottom_ref, 0, field[tile_rows - halo :]),
        (left_ref, halo + 1, field[:, :halo]),
        (right_ref, halo + 1, field[:, tile_cols - halo :]),
    )
    peak = jnp.full((1, levels), 1e-30, jnp.float32)
    for _, _, strip in borders:
        peak = jnp.maximum(
            peak, jnp.max(jnp.max(jnp.abs(strip), axis=0), axis=0, keepdims=True)
        )
    power = jnp.ceil(jnp.log2(peak))
    scale = jnp.exp2(15.0 - power)
    for ref, first, strip in borders:
        last = first + strip.shape[0]
        whole = jnp.floor(strip * scale + 0.5)
        whole = jnp.clip(whole, -32767.0, 32767.0)
        ref[first:last] = whole.astype(jnp.int32).astype(jnp.int16)
        ref[last] = jnp.broadcast_to(power, strip.shape[1:]).astype(jnp.int32).astype(jnp.int16)


def decode_field(coded, power):
    scale = jnp.exp2(power.astype(jnp.int32).astype(jnp.float32) - 15.0)
    return coded.astype(jnp.int32).astype(jnp.float32) * scale


def lay(halo, target, centre, north, south, west, east):
    tile_rows, tile_cols, _ = centre.shape
    breadth = tile_cols + 2 * halo
    mid_r, mid_c = slice(halo, halo + tile_rows), slice(halo, halo + tile_cols)
    target[mid_r, mid_c] = centre[...]
    target[:halo, mid_c] = decode_field(north[:halo], north[halo])
    target[halo + tile_rows :, mid_c] = decode_field(south[:halo], south[halo])
    for side, cols in ((west, slice(0, halo)), (east, slice(halo + tile_cols, breadth))):
        read, put = 0, 0
        for count in (halo, tile_rows, halo):
            target[put : put + count, cols] = decode_field(
                side[read : read + count], side[read + count]
            )
            read, put = read + count + 1, put + count


KAPPA_LOW = 0.12
KAPPA_STEP = 0.125 / 65535


def encode_kappa(x):
    whole = jnp.round((x - KAPPA_LOW) * (1.0 / KAPPA_STEP))
    return (jnp.clip(whole, 0.0, 65535.0) - 32768.0).astype(jnp.int16)


def decode_kappa(x):
    whole = x.astype(jnp.int32).astype(jnp.float32) + 32768.0
    return whole * KAPPA_STEP + KAPPA_LOW


def mixed_row(plain_ref, i, stretch):
    return jnp.stack([plain_ref[i, pl.ds(t, 8, stride=stretch), :] for t in range(stretch)])


def eastward(x):
    return jnp.concatenate([x[1:], pltpu.roll(x[0], 7, 0)[None]], axis=0)


def westward(x):
    return jnp.concatenate([pltpu.roll(x[-1], 1, 0)[None], x[:-1]], axis=0)


def edges_kernel(
    halo, inside_ref, centre_ref, north_ref, south_ref, west_hbm, east_hbm, east_ref,
    south_edge_ref, plain_ref, west_ref, east_side_ref, sems
):
    copies = [
        pltpu.make_async_copy(west_hbm, west_ref, sems.at[0]),
        pltpu.make_async_copy(east_hbm, east_side_ref, sems.at[1]),
    ]
    for copy in copies:
        copy.start()
    tile_rows, tile_cols, _ = centre_ref.shape
    height, _ = plain_ref.shape[:2]
    mid_r, mid_c = slice(halo, halo + tile_rows), slice(halo, halo + tile_cols)
    low, end = slice(0, halo), slice(halo + tile_rows, height)
    plain_ref[mid_r, mid_c] = centre_ref[...]
    plain_ref[low, mid_c] = decode_kappa(north_ref[...])
    plain_ref[end, mid_c] = decode_kappa(south_ref[...])
    for copy in copies:
        copy.wait()
    plain_ref[:, :halo] = decode_kappa(west_ref[...])
    plain_ref[:, halo + tile_cols :] = decode_kappa(east_side_ref[...])
    plain_ref[low] = plain_ref[low] * inside_ref[0]
    plain_ref[end] = plain_ref[end] * inside_ref[1]
    stretch = east_ref.shape[1]

    def edges(i, here):
        below = mixed_row(plain_ref, i + 1, stretch)
        east_ref[i] = 0.5 * (here + eastward(here))
        south_edge_ref[i] = 0.5 * (here + below)
        return below

    lax.fori_loop(0, height - 1, edges, mixed_row(plain_ref, 0, stretch), unroll=2)


def relax_kernel(
    halo, inside_ref, centre_ref, north_ref, south_ref, west_ref, east_side_ref, east_ref,
    south_edge_ref, out_ref, plain_ref, first_ref, second_ref
):
    tile_rows, tile_cols, _ = out_ref.shape
    height = tile_rows + 2 * halo
    stretch = first_ref.shape[1]
    lay(halo, plain_ref, centre_ref, north_ref, south_ref, west_ref, east_side_ref)

    source, target = None, second_ref
    for step in range(1, halo + 1):
        last = step == halo

        def read(i, source=source):
            return mixed_row(plain_ref, i, stretch) if source is None else source[i]

        def row(i, carry, scale=None, read=read, target=target, last=last):
            here, from_north = carry
            below = read(i + 1)
            to_east = east_ref[i] * (eastward(here) - here)
            from_south = south_edge_ref[i] * (below - here)
            value = here + (to_east - westward(to_east)) + (from_south - from_north)
            if scale is not None:
                value = value * scale
            if last:
                for t in range(stretch):
                    plain_ref[i, pl.ds(t, 8, stride=stretch), :] = value[t]
            else:
                target[i] = value
            return below, from_south

        here = read(step)
        carry = (here, south_edge_ref[step - 1] * (here - read(step - 1)))
        carry = lax.fori_loop(
            step, halo, functools.partial(row, scale=inside_ref[0]), carry, unroll=True
        )
        carry = lax.fori_loop(halo, halo + tile_rows, row, carry, unroll=4)
        lax.fori_loop(
            halo + tile_rows, height - step, functools.partial(row, scale=inside_ref[1]), carry,
            unroll=True,
        )
        source, target = target, first_ref if target is second_ref else second_ref
    out_ref[...] = plain_ref[halo : halo + tile_rows, halo : halo + tile_cols, :]


def depart_kernel(slot_ref, evolved_ref, observed_ref, out_ref):
    foot_count, _ = observed_ref.shape
    slots = evolved_ref.shape[0]
    slot = slot_ref[...]
    parts = thirds(evolved_ref[...])
    chosen = jnp.where(iota((slots, foot_count), 0) == slot, 1.0, 0.0).astype(jnp.bfloat16)
    rows = [dot_f32(chosen, part, ((0,), (0,))) for part in parts]
    out_ref[...] = observed_ref[...] - ((rows[0] + rows[1]) + rows[2])


def vmem():
    return pl.BlockSpec(memory_space=pltpu.VMEM)


def smem():
    return pl.BlockSpec(memory_space=pltpu.SMEM)


def hbm():
    return pl.BlockSpec(memory_space=pltpu.HBM)


def params(mib):
    return pltpu.CompilerParams(vmem_limit_bytes=mib * MIB)


def cost(flops, transcendentals, moved):
    return pl.CostEstimate(flops=flops, transcendentals=transcendentals, bytes_accessed=moved)


def neighbours(axis, periodic):
    count = lax.axis_size(axis)
    forward = [(i, i + 1) for i in range(count - 1)]
    if periodic:
        forward.append((count - 1, 0))
    return forward, [(target, source) for source, target in forward]


def join(north, south, left, right):
    halo = left.shape[1]
    right = jnp.concatenate([north[:, -halo:], right, south[:, -halo:]], axis=0)
    left = jnp.concatenate([north[:, :halo], left, south[:, :halo]], axis=0)
    return left, right


def join_kernel(north_ref, south_ref, _, __, left_ref, right_ref, sems):
    count, tile_cols, _ = north_ref.shape
    total, halo, _ = left_ref.shape
    copies = []
    for target, cols in ((left_ref, 0), (right_ref, tile_cols - halo)):
        for source, row in ((north_ref, 0), (south_ref, total - count)):
            copies.append(
                pltpu.make_async_copy(
                    source.at[:, pl.ds(cols, halo)], target.at[pl.ds(row, count)],
                    sems.at[len(copies)],
                )
            )
    for copy in copies:
        copy.start()
    for copy in copies:
        copy.wait()


def join_in_place(north, south, left, right):
    return pl.pallas_call(
        join_kernel,
        out_shape=tuple(jax.ShapeDtypeStruct(x.shape, x.dtype) for x in (left, right)),
        in_specs=[vmem()] * 2 + [hbm()] * 2,
        out_specs=(hbm(), hbm()),
        input_output_aliases={2: 0, 3: 1},
        scratch_shapes=[pltpu.SemaphoreType.DMA((4,))],
        compiler_params=params(2),
        name="join",
    )(north, south, left, right)


def halos(top, bottom, left, right, join):
    lat_up, lat_down = neighbours("lat", False)
    lon_up, lon_down = neighbours("lon", True)
    south = lax.ppermute(top, "lat", lat_down)
    north = lax.ppermute(bottom, "lat", lat_up)
    lefts, rights = join(north, south, left, right)
    west = lax.ppermute(rights, "lon", lon_up)
    east = lax.ppermute(lefts, "lon", lon_down)
    return north, south, west, east


def local(
    background, diffusivity, tile_index, anchor, weights, observed, accept, absorb, sensitivity,
    inverse_variance
):
    f32 = jnp.float32
    lat_count = lax.axis_size("lat")
    lon_count = lax.axis_size("lon")
    dev_count = lat_count * lon_count
    foot_count, channels = observed.shape
    capacity = max(2, 2 * foot_count // dev_count)
    tile_rows, tile_cols, levels = background.shape
    slots = dev_count * capacity
    lanes = 128
    group = lanes // capacity
    cells = tile_rows * tile_cols
    halo = STEPS

    me = lax.axis_index("lat") * lon_count + lax.axis_index("lon")
    lane = (lax.rem(me, group) * capacity).astype(jnp.int32).reshape(1)
    send, slot = pl.pallas_call(
        functools.partial(pack_kernel, dev_count, capacity, tile_cols),
        out_shape=(
            jax.ShapeDtypeStruct((dev_count, capacity + META, channels), f32),
            jax.ShapeDtypeStruct((1, foot_count), jnp.int32),
        ),
        in_specs=[smem()] + [vmem()] * 5,
        out_specs=(vmem(), vmem()),
        scratch_shapes=[pltpu.VMEM((dev_count * META, foot_count), f32)],
        compiler_params=params(60),
        cost_estimate=cost(2 * slots * foot_count * channels * 3, 0, 4 * slots * channels * 3),
        name="pack",
    )(
        lane, tile_index.reshape(1, foot_count), anchor.reshape(1, foot_count), weights.T,
        observed, accept
    )
    recv = lax.all_to_all(send, ("lat", "lon"), split_axis=0, concat_axis=0, tiled=True)

    kappa_halos = halos(
        encode_kappa(diffusivity[:halo]), encode_kappa(diffusivity[-halo:]),
        encode_kappa(diffusivity[:, :halo]), encode_kappa(diffusivity[:, -halo:]), join
    )
    absorb_wide = pl.pallas_call(
        spread_kernel,
        out_shape=jax.ShapeDtypeStruct((levels, channels, lanes), f32),
        grid=(levels // 16,),
        in_specs=[pl.BlockSpec((levels, channels), lambda i: (0, 0))],
        out_specs=pl.BlockSpec((16, channels, lanes), lambda i: (i, 0, 0)),
        scratch_shapes=[pltpu.VMEM((channels, levels), f32)],
        compiler_params=params(60),
        cost_estimate=cost(levels * channels * lanes, 0, 4 * levels * channels * lanes),
        name="spread",
    )(absorb)

    wide = 32
    evolved, field, top, bottom, left, right = pl.pallas_call(
        functools.partial(column_kernel, capacity, halo),
        out_shape=(
            jax.ShapeDtypeStruct((dev_count, capacity, channels), f32),
            jax.ShapeDtypeStruct((tile_rows, tile_cols, levels), f32),
            jax.ShapeDtypeStruct((halo + 1, tile_cols, levels), jnp.int16),
            jax.ShapeDtypeStruct((halo + 1, tile_cols, levels), jnp.int16),
            jax.ShapeDtypeStruct((tile_rows + 2 * halo + 3, halo, levels), jnp.int16),
            jax.ShapeDtypeStruct((tile_rows + 2 * halo + 3, halo, levels), jnp.int16),
        ),
        in_specs=[vmem()] * 2 + [hbm()] + [vmem()] * 2 + [hbm()] * 2,
        out_specs=(vmem(),) * 6,
        scratch_shapes=[
            pltpu.SMEM((dev_count, channels), f32),
            pltpu.SemaphoreType.DMA,
            pltpu.SemaphoreType.DMA((channels // wide,)),
            pltpu.VMEM((cells, levels), f32),
            pltpu.VMEM((levels, channels, lanes), f32),
            pltpu.VMEM((channels, lanes), f32),
            pltpu.VMEM((channels, lanes), f32),
            pltpu.VMEM((4, lanes, levels), f32),
            pltpu.VMEM((4, lanes, levels), f32),
            pltpu.VMEM((levels, lanes), f32),
            pltpu.VMEM((levels, lanes), f32),
            pltpu.VMEM((channels, lanes), f32),
            pltpu.VMEM((channels, lanes), f32),
            pltpu.VMEM((levels, wide, lanes), f32),
            pltpu.VMEM((levels, wide, lanes), f32),
            pltpu.VMEM((levels * 8, lanes), f32),
            pltpu.VMEM((4, cells, levels), f32),
        ],
        compiler_params=params(60),
        cost_estimate=cost(
            14 * slots * levels * channels, 2 * slots * levels * channels, 12 * cells * levels
        ),
        name="column",
    )(
        recv, background, absorb_wide, sensitivity.reshape(1, channels),
        inverse_variance.reshape(1, channels), *kappa_halos[2:]
    )

    field_halos = halos(top, bottom, left, right, join_in_place)
    lat_at = lax.axis_index("lat")
    inside = jnp.stack([lat_at > 0, lat_at < lat_count - 1]).astype(f32)
    height, breadth = tile_rows + 2 * halo, tile_cols + 2 * halo

    plain = pltpu.VMEM((height, breadth, levels), f32)
    mixed = (height, breadth // 8, 8, levels)

    east, south = pl.pallas_call(
        functools.partial(edges_kernel, halo),
        out_shape=(jax.ShapeDtypeStruct(mixed, f32),) * 2,
        in_specs=[smem()] + [vmem()] * 3 + [hbm()] * 2,
        out_specs=(vmem(),) * 2,
        scratch_shapes=[plain]
        + [pltpu.VMEM((height, halo, levels), jnp.int16)] * 2
        + [pltpu.SemaphoreType.DMA((2,))],
        compiler_params=params(22),
        cost_estimate=cost(4 * height * breadth * levels, 0, 12 * cells * levels),
        name="edges",
    )(inside, diffusivity, *kappa_halos)


    returned = lax.all_to_all(
        evolved, ("lat", "lon"), split_axis=0, concat_axis=0, tiled=True
    )

    departure = pl.pallas_call(
        depart_kernel,
        out_shape=jax.ShapeDtypeStruct((foot_count, channels), f32),
        in_specs=[vmem()] * 3,
        out_specs=vmem(),
        compiler_params=params(16),
        cost_estimate=cost(2 * slots * foot_count * channels * 3, 0, 4 * slots * channels * 2),
        name="depart",
    )(slot, returned.reshape(slots, channels), observed)

    increment = pl.pallas_call(
        functools.partial(relax_kernel, halo),
        out_shape=jax.ShapeDtypeStruct((tile_rows, tile_cols, levels), f32),
        in_specs=[smem()] + [vmem()] * 7,
        out_specs=vmem(),
        scratch_shapes=[plain, pltpu.VMEM(mixed, f32), pltpu.VMEM(mixed, f32)],
        compiler_params=params(26),
        cost_estimate=cost(10 * STEPS * height * breadth * levels, 0, 16 * cells * levels),
        name="relax",
    )(inside, field, *field_halos, east, south)
    return (departure, increment)


def solution(mesh):
    in_specs = (
        P("lat", "lon", None),
        P("lat", "lon", None),
        P(("lat", "lon"), None),
        P(("lat", "lon")),
        P(("lat", "lon"), None),
        P(("lat", "lon"), None),
        P(("lat", "lon"), None),
        P(),
        P(),
        P(),
    )
    out_specs = (P(("lat", "lon"), None), P("lat", "lon", None))

    return jax.shard_map(local, mesh=mesh, in_specs=in_specs, out_specs=out_specs, check_vma=False)
```

```python
import functools
import math

import jax
import jax.numpy as jnp
from jax import lax
from jax.experimental import pallas as pl
from jax.experimental.pallas import tpu as pltpu
from jax.sharding import PartitionSpec as P


STEPS = 8
REJECTED = 64.0
META = 8
LOG2E = math.log2(math.e)
LN2 = math.log(2.0)
MIB = 1024 * 1024
UNROLL = 32


def thirds(x):
    high = x.astype(jnp.bfloat16)
    rest = x - high.astype(jnp.float32)
    mid = rest.astype(jnp.bfloat16)
    low = (rest - mid.astype(jnp.float32)).astype(jnp.bfloat16)
    return high, mid, low


def dot_f32(a, b, contract):
    return lax.dot_general(a, b, (contract, ((), ())), preferred_element_type=jnp.float32)


def iota(shape, dim):
    return lax.broadcasted_iota(jnp.int32, shape, dim)


def pack_kernel(
    dev_count, capacity, tile_cols, lane_ref, tile_ref, anchor_ref, weights_ref, observed_ref,
    accept_ref, send_ref, slot_ref, vals_ref
):
    foot_count, channels = observed_ref.shape
    bf16 = jnp.bfloat16
    tile = tile_ref[...]
    onehot = jnp.where(iota((dev_count, foot_count), 0) == tile, 1.0, 0.0)
    earlier = jnp.where(
        iota((foot_count, foot_count), 0) < iota((foot_count, foot_count), 1), 1.0, 0.0
    ).astype(bf16)
    before = dot_f32(onehot.astype(bf16), earlier, ((1,), (0,)))
    rank = jnp.sum(before * onehot, axis=0, keepdims=True).astype(jnp.int32)
    slot = tile * capacity + rank
    slot_ref[...] = slot

    chosen = jnp.where(accept_ref[...] != 0, observed_ref[...], REJECTED)
    parts = thirds(chosen)
    per_chunk = max(1, 128 // capacity)
    chunk = per_chunk * capacity
    for start in range(0, dev_count, per_chunk):
        place = jnp.where(
            iota((chunk, foot_count), 0) + start * capacity == slot, 1.0, 0.0
        ).astype(bf16)
        rows = [dot_f32(place, part, ((1,), (0,))) for part in parts]
        rows = (rows[0] + rows[1]) + rows[2]
        send_ref[start : start + per_chunk, :capacity, :] = rows.reshape(
            per_chunk, capacity, channels
        )

    anchor = anchor_ref[...]
    line = jnp.floor((anchor.astype(jnp.float32) + 0.5) * (1.0 / (tile_cols - 1)))
    base = anchor.astype(jnp.float32) + line
    weights = weights_ref[...]
    shares = weights / jnp.sum(weights, axis=0, keepdims=True)
    meta = jnp.concatenate(
        [base, shares, jnp.zeros((META - 5, foot_count), jnp.float32)], axis=0
    )
    for dev in range(dev_count):
        vals_ref[dev * META : (dev + 1) * META, :] = jnp.where(tile == dev, meta, 0.0)
    lanes = jnp.where(
        iota((channels, foot_count), 0) == rank + lane_ref[0], 1.0, 0.0
    ).astype(bf16)
    rows = [dot_f32(part, lanes, ((1,), (1,))) for part in thirds(vals_ref[...])]
    rows = (rows[0] + rows[1]) + rows[2]
    send_ref[:, capacity:, :] = rows.reshape(dev_count, META, channels)


def spread_kernel(absorb_ref, out_ref, turned_ref):
    some, channels, lanes = out_ref.shape
    levels = absorb_ref.shape[0]

    @pl.when(pl.program_id(0) == 0)
    def _():
        turned_ref[...] = (absorb_ref[...] * LOG2E).T

    turned = turned_ref[...]
    for u in range(some):
        out_ref[u] = jnp.broadcast_to(turned[:, u : u + 1], (channels, lanes))
    turned_ref[...] = pltpu.roll(turned, levels - some, 1)


def column_kernel(
    capacity, halo, recv_ref, background_ref, absorb_any, sensitivity_ref, inverse_ref,
    evolved_ref, field_ref, top_ref, bottom_ref, left_ref, right_ref,
    base_ref, sem, absorb_sem, cells_ref, absorb_b, slope_b, inverse_b, taken_ref, terms_ref, profile_ref,
    rise_ref, obs_ref, evo_ref, main_ref, side_ref, push_ref, sums_ref
):
    dev_count = recv_ref.shape[0]
    tile_rows, tile_cols, levels = background_ref.shape
    cells = tile_rows * tile_cols
    levels, channels, lanes = absorb_b.shape
    group = lanes // capacity
    blocks = dev_count // group
    wide = main_ref.shape[1]
    per_loop = UNROLL * wide * lanes // (levels * channels)
    corners = (0, 1, tile_cols, tile_cols + 1)

    copy = pltpu.make_async_copy(recv_ref.at[:, capacity, :], base_ref, sem)
    copy.start()

    def absorb_copy(c):
        some = pl.ds(pl.multiple_of(c * wide, wide), wide)
        return pltpu.make_async_copy(
            absorb_any.at[:, some, :], absorb_b.at[:, some, :], absorb_sem.at[c]
        )

    for c in range(channels // wide):
        absorb_copy(c).start()

    cells_ref[...] = background_ref[...].reshape(cells, levels).astype(jnp.float32)
    slope_b[...] = jnp.broadcast_to(sensitivity_ref[...] * LOG2E, (lanes, channels)).T
    inverse_b[...] = jnp.broadcast_to(inverse_ref[...], (lanes, channels)).T

    sums_ref[...] = jnp.zeros_like(sums_ref)
    terms_ref[...] = jnp.zeros_like(terms_ref)
    copy.wait()

    def base_of(f, at):
        return base_ref[f * group + lax.div(at, capacity), at].astype(jnp.int32)

    def gather(f, at):
        base = base_of(f, at)
        for k, step in enumerate(corners):
            taken_ref[k, pl.ds(at, 1), :] = cells_ref[pl.ds(base + step, 1), :]

    def scatter(f, at):
        base = base_of(f, at)
        for k, step in enumerate(corners):
            sums_ref[k, pl.ds(base + step, 1), :] += terms_ref[k, pl.ds(at, 1), :]

    def gather_first(i, carry):
        for u in range(8):
            gather(0, i * 8 + u)
        return carry

    lax.fori_loop(0, lanes // 8, gather_first, 0)

    def block(f, carry):
        before = jnp.maximum(f - 1, 0)
        after = jnp.minimum(f + 1, blocks - 1)
        mine = recv_ref[pl.ds(f * group, group)]
        shares = jnp.sum(mine[:, capacity:, :], axis=0)
        obs_ref[...] = mine[:, :capacity, :].reshape(lanes, channels).T
        profile = shares[1:2] * taken_ref[0].T
        for k in range(1, 4):
            profile = profile + shares[k + 1 : k + 2] * taken_ref[k].T
        profile_ref[...] = profile
        rise_ref[0 : levels - 1, :] = profile[1:] - profile[:-1]
        rise_ref[levels - 1 : levels, :] = jnp.zeros((1, lanes), jnp.float32)
        push_ref[...] = jnp.zeros_like(push_ref)

        def some_channels(c, carry):
            @pl.when(f == 0)
            def _():
                absorb_copy(c).wait()

            at = pl.multiple_of(c * wide, wide)
            slope = slope_b[pl.ds(at, wide), :]
            scale = slope * (LN2 * LN2)

            def down(i, state):
                path, total, above = state
                for u in range(UNROLL):
                    level = i * UNROLL + u
                    depth = absorb_b[level, pl.ds(at, wide), :] * jnp.exp2(
                        slope * profile_ref[pl.ds(level, 1), :]
                    )
                    path = path - depth
                    trans = jnp.exp2(path)
                    side = depth * scale
                    side_ref[level] = side
                    main_ref[level] = (above - trans) + side * total
                    total = total + trans * rise_ref[pl.ds(level, 1), :]
                    above = trans
                for u in range(per_loop):
                    scatter(before, (c * (levels // UNROLL) + i) * per_loop + u)
                return path, total, above

            zero = jnp.zeros((wide, lanes), jnp.float32)
            _, total, last = lax.fori_loop(0, levels // UNROLL, down, (zero, zero, zero + 1.0))
            main_ref[levels - 1] += last
            evolved = total + profile_ref[0:1, :]
            evo_ref[pl.ds(at, wide), :] = evolved
            obs = obs_ref[pl.ds(at, wide), :]
            force = jnp.where(
                obs < 0.5 * REJECTED, inverse_b[pl.ds(at, wide), :] * (obs - evolved), 0.0
            )

            def up(i, carry):
                for u in range(UNROLL):
                    level = i * UNROLL + u
                    push = force * (main_ref[level] - total * side_ref[level])
                    push_ref[pl.ds(pl.multiple_of(level * 8, 8), 8), :] += jnp.sum(
                        push.reshape(wide // 8, 8, lanes), axis=0
                    )
                for u in range(per_loop):
                    gather(after, (c * (levels // UNROLL) + i) * per_loop + u)
                return carry

            lax.fori_loop(0, levels // UNROLL, up, 0)
            return carry

        lax.fori_loop(0, channels // wide, some_channels, 0)
        evolved_ref[pl.ds(f * group, group)] = evo_ref[...].T.reshape(group, capacity, channels)
        push = push_ref[pl.ds(0, levels, stride=8), :]
        for u in range(1, 8):
            push = push + push_ref[pl.ds(u, levels, stride=8), :]
        for k in range(4):
            terms_ref[k] = (shares[k + 1 : k + 2] * push).T
        return carry

    lax.fori_loop(0, blocks, block, 0)

    def scatter_last(i, carry):
        for u in range(8):
            scatter(blocks - 1, i * 8 + u)
        return carry

    lax.fori_loop(0, lanes // 8, scatter_last, 0)

    field = (sums_ref[0] + sums_ref[1]) + (sums_ref[2] + sums_ref[3])
    field = field.reshape(tile_rows, tile_cols, levels)
    field_ref[...] = field

    borders = (
        (top_ref, 0, field[:halo]),
        (bottom_ref, 0, field[tile_rows - halo :]),
        (left_ref, halo + 1, field[:, :halo]),
        (right_ref, halo + 1, field[:, tile_cols - halo :]),
    )
    peak = jnp.full((1, levels), 1e-30, jnp.float32)
    for _, _, strip in borders:
        peak = jnp.maximum(
            peak, jnp.max(jnp.max(jnp.abs(strip), axis=0), axis=0, keepdims=True)
        )
    power = jnp.ceil(jnp.log2(peak))
    scale = jnp.exp2(15.0 - power)
    for ref, first, strip in borders:
        last = first + strip.shape[0]
        whole = jnp.floor(strip * scale + 0.5)
        whole = jnp.clip(whole, -32767.0, 32767.0)
        ref[first:last] = whole.astype(jnp.int32).astype(jnp.int16)
        ref[last] = jnp.broadcast_to(power, strip.shape[1:]).astype(jnp.int32).astype(jnp.int16)


def decode_field(coded, power):
    scale = jnp.exp2(power.astype(jnp.int32).astype(jnp.float32) - 15.0)
    return coded.astype(jnp.int32).astype(jnp.float32) * scale


def lay(halo, target, centre, north, south, west, east):
    tile_rows, tile_cols, _ = centre.shape
    breadth = tile_cols + 2 * halo
    mid_r, mid_c = slice(halo, halo + tile_rows), slice(halo, halo + tile_cols)
    target[mid_r, mid_c] = centre[...]
    target[:halo, mid_c] = decode_field(north[:halo], north[halo])
    target[halo + tile_rows :, mid_c] = decode_field(south[:halo], south[halo])
    for side, cols in ((west, slice(0, halo)), (east, slice(halo + tile_cols, breadth))):
        read, put = 0, 0
        for count in (halo, tile_rows, halo):
            target[put : put + count, cols] = decode_field(
                side[read : read + count], side[read + count]
            )
            read, put = read + count + 1, put + count


KAPPA_LOW = 0.12
KAPPA_STEP = 0.125 / 65535


def encode_kappa(x):
    whole = jnp.round((x - KAPPA_LOW) * (1.0 / KAPPA_STEP))
    return (jnp.clip(whole, 0.0, 65535.0) - 32768.0).astype(jnp.int16)


def decode_kappa(x):
    whole = x.astype(jnp.int32).astype(jnp.float32) + 32768.0
    return whole * KAPPA_STEP + KAPPA_LOW


def mixed_row(plain_ref, i, stretch):
    return jnp.stack([plain_ref[i, pl.ds(t, 8, stride=stretch), :] for t in range(stretch)])


def eastward(x):
    return jnp.concatenate([x[1:], pltpu.roll(x[0], 7, 0)[None]], axis=0)


def westward(x):
    return jnp.concatenate([pltpu.roll(x[-1], 1, 0)[None], x[:-1]], axis=0)


def edges_kernel(
    halo, inside_ref, centre_ref, north_ref, south_ref, west_hbm, east_hbm, east_ref,
    south_edge_ref, plain_ref, west_ref, east_side_ref, sems
):
    copies = [
        pltpu.make_async_copy(west_hbm, west_ref, sems.at[0]),
        pltpu.make_async_copy(east_hbm, east_side_ref, sems.at[1]),
    ]
    for copy in copies:
        copy.start()
    tile_rows, tile_cols, _ = centre_ref.shape
    height, _ = plain_ref.shape[:2]
    mid_r, mid_c = slice(halo, halo + tile_rows), slice(halo, halo + tile_cols)
    low, end = slice(0, halo), slice(halo + tile_rows, height)
    plain_ref[mid_r, mid_c] = centre_ref[...]
    plain_ref[low, mid_c] = decode_kappa(north_ref[...])
    plain_ref[end, mid_c] = decode_kappa(south_ref[...])
    for copy in copies:
        copy.wait()
    plain_ref[:, :halo] = decode_kappa(west_ref[...])
    plain_ref[:, halo + tile_cols :] = decode_kappa(east_side_ref[...])
    plain_ref[low] = plain_ref[low] * inside_ref[0]
    plain_ref[end] = plain_ref[end] * inside_ref[1]
    stretch = east_ref.shape[1]

    def edges(i, here):
        below = mixed_row(plain_ref, i + 1, stretch)
        east_ref[i] = 0.5 * (here + eastward(here))
        south_edge_ref[i] = 0.5 * (here + below)
        return below

    lax.fori_loop(0, height - 1, edges, mixed_row(plain_ref, 0, stretch), unroll=2)


def relax_kernel(
    halo, inside_ref, centre_ref, north_ref, south_ref, west_ref, east_side_ref, east_ref,
    south_edge_ref, out_ref, plain_ref, first_ref, second_ref
):
    tile_rows, tile_cols, _ = out_ref.shape
    height = tile_rows + 2 * halo
    stretch = first_ref.shape[1]
    lay(halo, plain_ref, centre_ref, north_ref, south_ref, west_ref, east_side_ref)

    source, target = None, second_ref
    for step in range(1, halo + 1):
        last = step == halo

        def read(i, source=source):
            return mixed_row(plain_ref, i, stretch) if source is None else source[i]

        def row(i, carry, scale=None, read=read, target=target, last=last):
            here, from_north = carry
            below = read(i + 1)
            to_east = east_ref[i] * (eastward(here) - here)
            from_south = south_edge_ref[i] * (below - here)
            value = here + (to_east - westward(to_east)) + (from_south - from_north)
            if scale is not None:
                value = value * scale
            if last:
                for t in range(stretch):
                    plain_ref[i, pl.ds(t, 8, stride=stretch), :] = value[t]
            else:
                target[i] = value
            return below, from_south

        here = read(step)
        carry = (here, south_edge_ref[step - 1] * (here - read(step - 1)))
        carry = lax.fori_loop(
            step, halo, functools.partial(row, scale=inside_ref[0]), carry, unroll=True
        )
        carry = lax.fori_loop(halo, halo + tile_rows, row, carry, unroll=4)
        lax.fori_loop(
            halo + tile_rows, height - step, functools.partial(row, scale=inside_ref[1]), carry,
            unroll=True,
        )
        source, target = target, first_ref if target is second_ref else second_ref
    out_ref[...] = plain_ref[halo : halo + tile_rows, halo : halo + tile_cols, :]


def depart_kernel(slot_ref, evolved_ref, observed_ref, out_ref):
    foot_count, _ = observed_ref.shape
    slots = evolved_ref.shape[0]
    slot = slot_ref[...]
    parts = thirds(evolved_ref[...])
    chosen = jnp.where(iota((slots, foot_count), 0) == slot, 1.0, 0.0).astype(jnp.bfloat16)
    rows = [dot_f32(chosen, part, ((0,), (0,))) for part in parts]
    out_ref[...] = observed_ref[...] - ((rows[0] + rows[1]) + rows[2])


def vmem():
    return pl.BlockSpec(memory_space=pltpu.VMEM)


def smem():
    return pl.BlockSpec(memory_space=pltpu.SMEM)


def hbm():
    return pl.BlockSpec(memory_space=pltpu.HBM)


def params(mib):
    return pltpu.CompilerParams(vmem_limit_bytes=mib * MIB)


def cost(flops, transcendentals, moved):
    return pl.CostEstimate(flops=flops, transcendentals=transcendentals, bytes_accessed=moved)


def neighbours(axis, periodic):
    count = lax.axis_size(axis)
    forward = [(i, i + 1) for i in range(count - 1)]
    if periodic:
        forward.append((count - 1, 0))
    return forward, [(target, source) for source, target in forward]


def join(north, south, left, right):
    halo = left.shape[1]
    right = jnp.concatenate([north[:, -halo:], right, south[:, -halo:]], axis=0)
    left = jnp.concatenate([north[:, :halo], left, south[:, :halo]], axis=0)
    return left, right


def join_kernel(north_ref, south_ref, _, __, left_ref, right_ref, sems):
    count, tile_cols, _ = north_ref.shape
    total, halo, _ = left_ref.shape
    copies = []
    for target, cols in ((left_ref, 0), (right_ref, tile_cols - halo)):
        for source, row in ((north_ref, 0), (south_ref, total - count)):
            copies.append(
                pltpu.make_async_copy(
                    source.at[:, pl.ds(cols, halo)], target.at[pl.ds(row, count)],
                    sems.at[len(copies)],
                )
            )
    for copy in copies:
        copy.start()
    for copy in copies:
        copy.wait()


def join_in_place(north, south, left, right):
    return pl.pallas_call(
        join_kernel,
        out_shape=tuple(jax.ShapeDtypeStruct(x.shape, x.dtype) for x in (left, right)),
        in_specs=[vmem()] * 2 + [hbm()] * 2,
        out_specs=(hbm(), hbm()),
        input_output_aliases={2: 0, 3: 1},
        scratch_shapes=[pltpu.SemaphoreType.DMA((4,))],
        compiler_params=params(2),
        name="join",
    )(north, south, left, right)


def halos(top, bottom, left, right, join):
    lat_up, lat_down = neighbours("lat", False)
    lon_up, lon_down = neighbours("lon", True)
    south = lax.ppermute(top, "lat", lat_down)
    north = lax.ppermute(bottom, "lat", lat_up)
    lefts, rights = join(north, south, left, right)
    west = lax.ppermute(rights, "lon", lon_up)
    east = lax.ppermute(lefts, "lon", lon_down)
    return north, south, west, east


def local(
    background, diffusivity, tile_index, anchor, weights, observed, accept, absorb, sensitivity,
    inverse_variance
):
    f32 = jnp.float32
    lat_count = lax.axis_size("lat")
    lon_count = lax.axis_size("lon")
    dev_count = lat_count * lon_count
    foot_count, channels = observed.shape
    capacity = max(2, 2 * foot_count // dev_count)
    tile_rows, tile_cols, levels = background.shape
    slots = dev_count * capacity
    lanes = 128
    group = lanes // capacity
    cells = tile_rows * tile_cols
    halo = STEPS

    me = lax.axis_index("lat") * lon_count + lax.axis_index("lon")
    lane = (lax.rem(me, group) * capacity).astype(jnp.int32).reshape(1)
    send, slot = pl.pallas_call(
        functools.partial(pack_kernel, dev_count, capacity, tile_cols),
        out_shape=(
            jax.ShapeDtypeStruct((dev_count, capacity + META, channels), f32),
            jax.ShapeDtypeStruct((1, foot_count), jnp.int32),
        ),
        in_specs=[smem()] + [vmem()] * 5,
        out_specs=(vmem(), vmem()),
        scratch_shapes=[pltpu.VMEM((dev_count * META, foot_count), f32)],
        compiler_params=params(60),
        cost_estimate=cost(2 * slots * foot_count * channels * 3, 0, 4 * slots * channels * 3),
        name="pack",
    )(
        lane, tile_index.reshape(1, foot_count), anchor.reshape(1, foot_count), weights.T,
        observed, accept
    )
    recv = lax.all_to_all(send, ("lat", "lon"), split_axis=0, concat_axis=0, tiled=True)

    kappa_halos = halos(
        encode_kappa(diffusivity[:halo]), encode_kappa(diffusivity[-halo:]),
        encode_kappa(diffusivity[:, :halo]), encode_kappa(diffusivity[:, -halo:]), join
    )
    absorb_wide = pl.pallas_call(
        spread_kernel,
        out_shape=jax.ShapeDtypeStruct((levels, channels, lanes), f32),
        grid=(levels // 16,),
        in_specs=[pl.BlockSpec((levels, channels), lambda i: (0, 0))],
        out_specs=pl.BlockSpec((16, channels, lanes), lambda i: (i, 0, 0)),
        scratch_shapes=[pltpu.VMEM((channels, levels), f32)],
        compiler_params=params(60),
        cost_estimate=cost(levels * channels * lanes, 0, 4 * levels * channels * lanes),
        name="spread",
    )(absorb)

    wide = 32
    evolved, field, top, bottom, left, right = pl.pallas_call(
        functools.partial(column_kernel, capacity, halo),
        out_shape=(
            jax.ShapeDtypeStruct((dev_count, capacity, channels), f32),
            jax.ShapeDtypeStruct((tile_rows, tile_cols, levels), f32),
            jax.ShapeDtypeStruct((halo + 1, tile_cols, levels), jnp.int16),
            jax.ShapeDtypeStruct((halo + 1, tile_cols, levels), jnp.int16),
            jax.ShapeDtypeStruct((tile_rows + 2 * halo + 3, halo, levels), jnp.int16),
            jax.ShapeDtypeStruct((tile_rows + 2 * halo + 3, halo, levels), jnp.int16),
        ),
        in_specs=[vmem()] * 2 + [hbm()] + [vmem()] * 2,
        out_specs=(vmem(),) * 6,
        scratch_shapes=[
            pltpu.SMEM((dev_count, channels), f32),
            pltpu.SemaphoreType.DMA,
            pltpu.SemaphoreType.DMA((channels // wide,)),
            pltpu.VMEM((cells, levels), f32),
            pltpu.VMEM((levels, channels, lanes), f32),
            pltpu.VMEM((channels, lanes), f32),
            pltpu.VMEM((channels, lanes), f32),
            pltpu.VMEM((4, lanes, levels), f32),
            pltpu.VMEM((4, lanes, levels), f32),
            pltpu.VMEM((levels, lanes), f32),
            pltpu.VMEM((levels, lanes), f32),
            pltpu.VMEM((channels, lanes), f32),
            pltpu.VMEM((channels, lanes), f32),
            pltpu.VMEM((levels, wide, lanes), f32),
            pltpu.VMEM((levels, wide, lanes), f32),
            pltpu.VMEM((levels * 8, lanes), f32),
            pltpu.VMEM((4, cells, levels), f32),
        ],
        compiler_params=params(60),
        cost_estimate=cost(
            14 * slots * levels * channels, 2 * slots * levels * channels, 12 * cells * levels
        ),
        name="column",
    )(
        recv, background, absorb_wide, sensitivity.reshape(1, channels),
        inverse_variance.reshape(1, channels)
    )

    field_halos = halos(top, bottom, left, right, join_in_place)
    lat_at = lax.axis_index("lat")
    inside = jnp.stack([lat_at > 0, lat_at < lat_count - 1]).astype(f32)
    height, breadth = tile_rows + 2 * halo, tile_cols + 2 * halo

    plain = pltpu.VMEM((height, breadth, levels), f32)
    mixed = (height, breadth // 8, 8, levels)

    east, south = pl.pallas_call(
        functools.partial(edges_kernel, halo),
        out_shape=(jax.ShapeDtypeStruct(mixed, f32),) * 2,
        in_specs=[smem()] + [vmem()] * 3 + [hbm()] * 2,
        out_specs=(vmem(),) * 2,
        scratch_shapes=[plain]
        + [pltpu.VMEM((height, halo, levels), jnp.int16)] * 2
        + [pltpu.SemaphoreType.DMA((2,))],
        compiler_params=params(22),
        cost_estimate=cost(4 * height * breadth * levels, 0, 12 * cells * levels),
        name="edges",
    )(inside, diffusivity, *kappa_halos)


    returned = lax.all_to_all(
        evolved, ("lat", "lon"), split_axis=0, concat_axis=0, tiled=True
    )

    departure = pl.pallas_call(
        depart_kernel,
        out_shape=jax.ShapeDtypeStruct((foot_count, channels), f32),
        in_specs=[vmem()] * 3,
        out_specs=vmem(),
        compiler_params=params(16),
        cost_estimate=cost(2 * slots * foot_count * channels * 3, 0, 4 * slots * channels * 2),
        name="depart",
    )(slot, returned.reshape(slots, channels), observed)

    increment = pl.pallas_call(
        functools.partial(relax_kernel, halo),
        out_shape=jax.ShapeDtypeStruct((tile_rows, tile_cols, levels), f32),
        in_specs=[smem()] + [vmem()] * 7,
        out_specs=vmem(),
        scratch_shapes=[plain, pltpu.VMEM(mixed, f32), pltpu.VMEM(mixed, f32)],
        compiler_params=params(26),
        cost_estimate=cost(10 * STEPS * height * breadth * levels, 0, 16 * cells * levels),
        name="relax",
    )(inside, field, *field_halos, east, south)
    return (departure, increment)


def solution(mesh):
    in_specs = (
        P("lat", "lon", None),
        P("lat", "lon", None),
        P(("lat", "lon"), None),
        P(("lat", "lon")),
        P(("lat", "lon"), None),
        P(("lat", "lon"), None),
        P(("lat", "lon"), None),
        P(),
        P(),
        P(),
    )
    out_specs = (P(("lat", "lon"), None), P("lat", "lon", None))

    return jax.shard_map(local, mesh=mesh, in_specs=in_specs, out_specs=out_specs, check_vma=False)
```

```python
import functools
import math

import jax
import jax.numpy as jnp
from jax import lax
from jax.experimental import pallas as pl
from jax.experimental.pallas import tpu as pltpu
from jax.sharding import PartitionSpec as P


STEPS = 8
REJECTED = 64.0
META = 8
LOG2E = math.log2(math.e)
LN2 = math.log(2.0)
MIB = 1024 * 1024
UNROLL = 32


def thirds(x):
    high = x.astype(jnp.bfloat16)
    rest = x - high.astype(jnp.float32)
    mid = rest.astype(jnp.bfloat16)
    low = (rest - mid.astype(jnp.float32)).astype(jnp.bfloat16)
    return high, mid, low


def add_thirds(x):
    width = x.shape[1] // 3
    return (x[:, :width] + x[:, width : 2 * width]) + x[:, 2 * width :]


def dot_f32(a, b, contract):
    return lax.dot_general(a, b, (contract, ((), ())), preferred_element_type=jnp.float32)


def iota(shape, dim):
    return lax.broadcasted_iota(jnp.int32, shape, dim)


def pack_kernel(
    dev_count, capacity, tile_cols, lane_ref, tile_ref, anchor_ref, weights_ref, observed_ref,
    accept_ref, send_ref, slot_ref, vals_ref
):
    foot_count, channels = observed_ref.shape
    bf16 = jnp.bfloat16
    tile = tile_ref[...]
    onehot = jnp.where(iota((dev_count, foot_count), 0) == tile, 1.0, 0.0)
    earlier = jnp.where(
        iota((foot_count, foot_count), 0) < iota((foot_count, foot_count), 1), 1.0, 0.0
    ).astype(bf16)
    before = dot_f32(onehot.astype(bf16), earlier, ((1,), (0,)))
    rank = jnp.sum(before * onehot, axis=0, keepdims=True).astype(jnp.int32)
    slot = tile * capacity + rank
    slot_ref[...] = slot

    chosen = jnp.where(accept_ref[...] != 0, observed_ref[...], REJECTED)
    parts = jnp.concatenate(thirds(chosen), axis=1)
    per_chunk = max(1, 128 // capacity)
    chunk = per_chunk * capacity
    for start in range(0, dev_count, per_chunk):
        place = jnp.where(
            iota((chunk, foot_count), 0) + start * capacity == slot, 1.0, 0.0
        ).astype(bf16)
        rows = add_thirds(dot_f32(place, parts, ((1,), (0,))))
        send_ref[start : start + per_chunk, :capacity, :] = rows.reshape(
            per_chunk, capacity, channels
        )

    anchor = anchor_ref[...]
    line = jnp.floor((anchor.astype(jnp.float32) + 0.5) * (1.0 / (tile_cols - 1)))
    base = anchor.astype(jnp.float32) + line
    weights = weights_ref[...]
    shares = weights / jnp.sum(weights, axis=0, keepdims=True)
    meta = jnp.concatenate(
        [base, shares, jnp.zeros((META - 5, foot_count), jnp.float32)], axis=0
    )
    for dev in range(dev_count):
        vals_ref[dev * META : (dev + 1) * META, :] = jnp.where(tile == dev, meta, 0.0)
    lanes = jnp.where(
        iota((channels, foot_count), 0) == rank + lane_ref[0], 1.0, 0.0
    ).astype(bf16)
    rows = [dot_f32(part, lanes, ((1,), (1,))) for part in thirds(vals_ref[...])]
    rows = (rows[0] + rows[1]) + rows[2]
    send_ref[:, capacity:, :] = rows.reshape(dev_count, META, channels)


def spread_kernel(absorb_ref, out_ref, turned_ref):
    some, channels, lanes = out_ref.shape
    levels = absorb_ref.shape[0]

    @pl.when(pl.program_id(0) == 0)
    def _():
        turned_ref[...] = (absorb_ref[...] * LOG2E).T

    turned = turned_ref[...]
    for u in range(some):
        out_ref[u] = jnp.broadcast_to(turned[:, u : u + 1], (channels, lanes))
    turned_ref[...] = pltpu.roll(turned, levels - some, 1)


def column_kernel(
    capacity, halo, recv_ref, background_ref, absorb_any, sensitivity_ref, inverse_ref,
    evolved_ref, field_ref, top_ref, bottom_ref, left_ref, right_ref,
    base_ref, slot_base_ref, sem, absorb_sem, cells_ref, absorb_b, slope_b, inverse_b, taken_ref, terms_ref, profile_ref,
    rise_ref, obs_ref, evo_ref, main_ref, side_ref, push_ref, sums_ref
):
    dev_count = recv_ref.shape[0]
    tile_rows, tile_cols, levels = background_ref.shape
    cells = tile_rows * tile_cols
    levels, channels, lanes = absorb_b.shape
    group = lanes // capacity
    blocks = dev_count // group
    wide = main_ref.shape[1]
    per_loop = UNROLL * wide * lanes // (levels * channels)
    corners = (0, 1, tile_cols, tile_cols + 1)

    rows = recv_ref[:, capacity, :].reshape(blocks, group, lanes)
    slot_base_ref[...] = jnp.sum(rows, axis=1).astype(jnp.int32)
    copy = pltpu.make_async_copy(slot_base_ref, base_ref, sem)
    copy.start()

    def absorb_copy(c):
        some = pl.ds(pl.multiple_of(c * wide, wide), wide)
        return pltpu.make_async_copy(
            absorb_any.at[:, some, :], absorb_b.at[:, some, :], absorb_sem.at[c]
        )

    for c in range(channels // wide):
        absorb_copy(c).start()

    cells_ref[...] = background_ref[...].reshape(cells, levels).astype(jnp.float32)
    slope_b[...] = jnp.broadcast_to(sensitivity_ref[...] * LOG2E, (lanes, channels)).T
    inverse_b[...] = jnp.broadcast_to(inverse_ref[...], (lanes, channels)).T

    sums_ref[...] = jnp.zeros_like(sums_ref)
    terms_ref[...] = jnp.zeros_like(terms_ref)
    copy.wait()

    def gather(f, at):
        base = base_ref[f, at]
        for k, step in enumerate(corners):
            taken_ref[k, pl.ds(at, 1), :] = cells_ref[pl.ds(base + step, 1), :]

    def scatter(f, at):
        base = base_ref[f, at]
        for k, step in enumerate(corners):
            sums_ref[k, pl.ds(base + step, 1), :] += terms_ref[k, pl.ds(at, 1), :]

    def gather_first(i, carry):
        for u in range(8):
            gather(0, i * 8 + u)
        return carry

    lax.fori_loop(0, lanes // 8, gather_first, 0)

    def block(f, carry):
        before = jnp.maximum(f - 1, 0)
        after = jnp.minimum(f + 1, blocks - 1)
        mine = recv_ref[pl.ds(f * group, group)]
        shares = jnp.sum(mine[:, capacity:, :], axis=0)
        obs_ref[...] = mine[:, :capacity, :].reshape(lanes, channels).T
        profile = shares[1:2] * taken_ref[0].T
        for k in range(1, 4):
            profile = profile + shares[k + 1 : k + 2] * taken_ref[k].T
        profile_ref[...] = profile
        rise_ref[0 : levels - 1, :] = profile[1:] - profile[:-1]
        rise_ref[levels - 1 : levels, :] = jnp.zeros((1, lanes), jnp.float32)
        push_ref[...] = jnp.zeros_like(push_ref)

        def some_channels(c, carry):
            @pl.when(f == 0)
            def _():
                absorb_copy(c).wait()

            at = pl.multiple_of(c * wide, wide)
            slope = slope_b[pl.ds(at, wide), :]
            scale = slope * (LN2 * LN2)

            def down(i, state):
                path, total, above = state
                for u in range(UNROLL):
                    level = i * UNROLL + u
                    depth = absorb_b[level, pl.ds(at, wide), :] * jnp.exp2(
                        slope * profile_ref[pl.ds(level, 1), :]
                    )
                    path = path - depth
                    trans = jnp.exp2(path)
                    side = depth * scale
                    side_ref[level] = side
                    main_ref[level] = (above - trans) + side * total
                    total = total + trans * rise_ref[pl.ds(level, 1), :]
                    above = trans
                for u in range(per_loop):
                    scatter(before, (c * (levels // UNROLL) + i) * per_loop + u)
                return path, total, above

            zero = jnp.zeros((wide, lanes), jnp.float32)
            _, total, last = lax.fori_loop(0, levels // UNROLL, down, (zero, zero, zero + 1.0))
            main_ref[levels - 1] += last
            evolved = total + profile_ref[0:1, :]
            evo_ref[pl.ds(at, wide), :] = evolved
            obs = obs_ref[pl.ds(at, wide), :]
            force = jnp.where(
                obs < 0.5 * REJECTED, inverse_b[pl.ds(at, wide), :] * (obs - evolved), 0.0
            )

            def up(i, carry):
                for u in range(UNROLL):
                    level = i * UNROLL + u
                    push = force * (main_ref[level] - total * side_ref[level])
                    push_ref[pl.ds(pl.multiple_of(level * 8, 8), 8), :] += jnp.sum(
                        push.reshape(wide // 8, 8, lanes), axis=0
                    )
                for u in range(per_loop):
                    gather(after, (c * (levels // UNROLL) + i) * per_loop + u)
                return carry

            lax.fori_loop(0, levels // UNROLL, up, 0)
            return carry

        lax.fori_loop(0, channels // wide, some_channels, 0)
        evolved_ref[pl.ds(f * group, group)] = evo_ref[...].T.reshape(group, capacity, channels)
        push = push_ref[pl.ds(0, levels, stride=8), :]
        for u in range(1, 8):
            push = push + push_ref[pl.ds(u, levels, stride=8), :]
        for k in range(4):
            terms_ref[k] = (shares[k + 1 : k + 2] * push).T
        return carry

    lax.fori_loop(0, blocks, block, 0)

    def scatter_last(i, carry):
        for u in range(8):
            scatter(blocks - 1, i * 8 + u)
        return carry

    lax.fori_loop(0, lanes // 8, scatter_last, 0)

    field = (sums_ref[0] + sums_ref[1]) + (sums_ref[2] + sums_ref[3])
    field = field.reshape(tile_rows, tile_cols, levels)
    field_ref[...] = field

    borders = (
        (top_ref, 0, field[:halo]),
        (bottom_ref, 0, field[tile_rows - halo :]),
        (left_ref, halo + 1, field[:, :halo]),
        (right_ref, halo + 1, field[:, tile_cols - halo :]),
    )
    peak = jnp.full((1, levels), 1e-30, jnp.float32)
    for _, _, strip in borders:
        peak = jnp.maximum(
            peak, jnp.max(jnp.max(jnp.abs(strip), axis=0), axis=0, keepdims=True)
        )
    power = jnp.ceil(jnp.log2(peak))
    scale = jnp.exp2(15.0 - power)
    for ref, first, strip in borders:
        last = first + strip.shape[0]
        whole = jnp.floor(strip * scale + 0.5)
        whole = jnp.clip(whole, -32767.0, 32767.0)
        ref[first:last] = whole.astype(jnp.int32).astype(jnp.int16)
        ref[last] = jnp.broadcast_to(power, strip.shape[1:]).astype(jnp.int32).astype(jnp.int16)


def decode_field(coded, power):
    scale = jnp.exp2(power.astype(jnp.int32).astype(jnp.float32) - 15.0)
    return coded.astype(jnp.int32).astype(jnp.float32) * scale


def lay(halo, target, centre, north, south, west, east):
    tile_rows, tile_cols, _ = centre.shape
    breadth = tile_cols + 2 * halo
    mid_r, mid_c = slice(halo, halo + tile_rows), slice(halo, halo + tile_cols)
    target[mid_r, mid_c] = centre[...]
    target[:halo, mid_c] = decode_field(north[:halo], north[halo])
    target[halo + tile_rows :, mid_c] = decode_field(south[:halo], south[halo])
    for side, cols in ((west, slice(0, halo)), (east, slice(halo + tile_cols, breadth))):
        read, put = 0, 0
        for count in (halo, tile_rows, halo):
            target[put : put + count, cols] = decode_field(
                side[read : read + count], side[read + count]
            )
            read, put = read + count + 1, put + count


KAPPA_LOW = 0.12
KAPPA_STEP = 0.125 / 65535


def encode_kappa(x):
    whole = jnp.round((x - KAPPA_LOW) * (1.0 / KAPPA_STEP))
    return (jnp.clip(whole, 0.0, 65535.0) - 32768.0).astype(jnp.int16)


def decode_kappa(x):
    whole = x.astype(jnp.int32).astype(jnp.float32) + 32768.0
    return whole * KAPPA_STEP + KAPPA_LOW


def mixed_row(plain_ref, i, stretch):
    return jnp.stack([plain_ref[i, pl.ds(t, 8, stride=stretch), :] for t in range(stretch)])


def eastward(x):
    return jnp.concatenate([x[1:], pltpu.roll(x[0], 7, 0)[None]], axis=0)


def westward(x):
    return jnp.concatenate([pltpu.roll(x[-1], 1, 0)[None], x[:-1]], axis=0)


def edges_kernel(
    halo, inside_ref, centre_ref, north_ref, south_ref, west_hbm, east_hbm, east_ref,
    south_edge_ref, plain_ref, west_ref, east_side_ref, sems
):
    copies = [
        pltpu.make_async_copy(west_hbm, west_ref, sems.at[0]),
        pltpu.make_async_copy(east_hbm, east_side_ref, sems.at[1]),
    ]
    for copy in copies:
        copy.start()
    tile_rows, tile_cols, _ = centre_ref.shape
    height, _ = plain_ref.shape[:2]
    mid_r, mid_c = slice(halo, halo + tile_rows), slice(halo, halo + tile_cols)
    low, end = slice(0, halo), slice(halo + tile_rows, height)
    plain_ref[mid_r, mid_c] = centre_ref[...]
    plain_ref[low, mid_c] = decode_kappa(north_ref[...])
    plain_ref[end, mid_c] = decode_kappa(south_ref[...])
    for copy in copies:
        copy.wait()
    plain_ref[:, :halo] = decode_kappa(west_ref[...])
    plain_ref[:, halo + tile_cols :] = decode_kappa(east_side_ref[...])
    plain_ref[low] = plain_ref[low] * inside_ref[0]
    plain_ref[end] = plain_ref[end] * inside_ref[1]
    stretch = east_ref.shape[1]

    def edges(i, here):
        below = mixed_row(plain_ref, i + 1, stretch)
        east_ref[i] = 0.5 * (here + eastward(here))
        south_edge_ref[i] = 0.5 * (here + below)
        return below

    lax.fori_loop(0, height - 1, edges, mixed_row(plain_ref, 0, stretch), unroll=2)


def relax_kernel(
    halo, inside_ref, centre_ref, north_ref, south_ref, west_ref, east_side_ref, east_ref,
    south_edge_ref, out_ref, plain_ref, first_ref, second_ref
):
    tile_rows, tile_cols, _ = out_ref.shape
    height = tile_rows + 2 * halo
    stretch = first_ref.shape[1]
    lay(halo, plain_ref, centre_ref, north_ref, south_ref, west_ref, east_side_ref)

    source, target = None, second_ref
    for step in range(1, halo + 1):
        last = step == halo

        def read(i, source=source):
            return mixed_row(plain_ref, i, stretch) if source is None else source[i]

        def row(i, carry, scale=None, read=read, target=target, last=last):
            here, from_north = carry
            below = read(i + 1)
            to_east = east_ref[i] * (eastward(here) - here)
            from_south = south_edge_ref[i] * (below - here)
            value = here + (to_east - westward(to_east)) + (from_south - from_north)
            if scale is not None:
                value = value * scale
            if last:
                for t in range(stretch):
                    plain_ref[i, pl.ds(t, 8, stride=stretch), :] = value[t]
            else:
                target[i] = value
            return below, from_south

        here = read(step)
        carry = (here, south_edge_ref[step - 1] * (here - read(step - 1)))
        carry = lax.fori_loop(
            step, halo, functools.partial(row, scale=inside_ref[0]), carry, unroll=True
        )
        carry = lax.fori_loop(halo, halo + tile_rows, row, carry, unroll=4)
        lax.fori_loop(
            halo + tile_rows, height - step, functools.partial(row, scale=inside_ref[1]), carry,
            unroll=True,
        )
        source, target = target, first_ref if target is second_ref else second_ref
    out_ref[...] = plain_ref[halo : halo + tile_rows, halo : halo + tile_cols, :]


def depart_kernel(slot_ref, evolved_ref, observed_ref, out_ref):
    foot_count, _ = observed_ref.shape
    slots = evolved_ref.shape[0]
    slot = slot_ref[...]
    parts = jnp.concatenate(thirds(evolved_ref[...]), axis=1)
    chosen = jnp.where(iota((slots, foot_count), 0) == slot, 1.0, 0.0).astype(jnp.bfloat16)
    out_ref[...] = observed_ref[...] - add_thirds(dot_f32(chosen, parts, ((0,), (0,))))


def vmem():
    return pl.BlockSpec(memory_space=pltpu.VMEM)


def smem():
    return pl.BlockSpec(memory_space=pltpu.SMEM)


def hbm():
    return pl.BlockSpec(memory_space=pltpu.HBM)


def params(mib):
    return pltpu.CompilerParams(vmem_limit_bytes=mib * MIB)


def cost(flops, transcendentals, moved):
    return pl.CostEstimate(flops=flops, transcendentals=transcendentals, bytes_accessed=moved)


def neighbours(axis, periodic):
    count = lax.axis_size(axis)
    forward = [(i, i + 1) for i in range(count - 1)]
    if periodic:
        forward.append((count - 1, 0))
    return forward, [(target, source) for source, target in forward]


def join(north, south, left, right):
    halo = left.shape[1]
    right = jnp.concatenate([north[:, -halo:], right, south[:, -halo:]], axis=0)
    left = jnp.concatenate([north[:, :halo], left, south[:, :halo]], axis=0)
    return left, right


def join_kernel(north_ref, south_ref, _, __, left_ref, right_ref, sems):
    count, tile_cols, _ = north_ref.shape
    total, halo, _ = left_ref.shape
    copies = []
    for target, cols in ((left_ref, 0), (right_ref, tile_cols - halo)):
        for source, row in ((north_ref, 0), (south_ref, total - count)):
            copies.append(
                pltpu.make_async_copy(
                    source.at[:, pl.ds(cols, halo)], target.at[pl.ds(row, count)],
                    sems.at[len(copies)],
                )
            )
    for copy in copies:
        copy.start()
    for copy in copies:
        copy.wait()


def join_in_place(north, south, left, right):
    return pl.pallas_call(
        join_kernel,
        out_shape=tuple(jax.ShapeDtypeStruct(x.shape, x.dtype) for x in (left, right)),
        in_specs=[vmem()] * 2 + [hbm()] * 2,
        out_specs=(hbm(), hbm()),
        input_output_aliases={2: 0, 3: 1},
        scratch_shapes=[pltpu.SemaphoreType.DMA((4,))],
        compiler_params=params(2),
        name="join",
    )(north, south, left, right)


def halos(top, bottom, left, right, join):
    lat_up, lat_down = neighbours("lat", False)
    lon_up, lon_down = neighbours("lon", True)
    south = lax.ppermute(top, "lat", lat_down)
    north = lax.ppermute(bottom, "lat", lat_up)
    lefts, rights = join(north, south, left, right)
    west = lax.ppermute(rights, "lon", lon_up)
    east = lax.ppermute(lefts, "lon", lon_down)
    return north, south, west, east


def local(
    background, diffusivity, tile_index, anchor, weights, observed, accept, absorb, sensitivity,
    inverse_variance
):
    f32 = jnp.float32
    lat_count = lax.axis_size("lat")
    lon_count = lax.axis_size("lon")
    dev_count = lat_count * lon_count
    foot_count, channels = observed.shape
    capacity = max(2, 2 * foot_count // dev_count)
    tile_rows, tile_cols, levels = background.shape
    slots = dev_count * capacity
    lanes = 128
    group = lanes // capacity
    cells = tile_rows * tile_cols
    halo = STEPS

    me = lax.axis_index("lat") * lon_count + lax.axis_index("lon")
    lane = (lax.rem(me, group) * capacity).astype(jnp.int32).reshape(1)
    send, slot = pl.pallas_call(
        functools.partial(pack_kernel, dev_count, capacity, tile_cols),
        out_shape=(
            jax.ShapeDtypeStruct((dev_count, capacity + META, channels), f32),
            jax.ShapeDtypeStruct((1, foot_count), jnp.int32),
        ),
        in_specs=[smem()] + [vmem()] * 5,
        out_specs=(vmem(), vmem()),
        scratch_shapes=[pltpu.VMEM((dev_count * META, foot_count), f32)],
        compiler_params=params(60),
        cost_estimate=cost(2 * slots * foot_count * channels * 3, 0, 4 * slots * channels * 3),
        name="pack",
    )(
        lane, tile_index.reshape(1, foot_count), anchor.reshape(1, foot_count), weights.T,
        observed, accept
    )
    recv = lax.all_to_all(send, ("lat", "lon"), split_axis=0, concat_axis=0, tiled=True)

    kappa_halos = halos(
        encode_kappa(diffusivity[:halo]), encode_kappa(diffusivity[-halo:]),
        encode_kappa(diffusivity[:, :halo]), encode_kappa(diffusivity[:, -halo:]), join
    )
    absorb_wide = pl.pallas_call(
        spread_kernel,
        out_shape=jax.ShapeDtypeStruct((levels, channels, lanes), f32),
        grid=(levels // 16,),
        in_specs=[pl.BlockSpec((levels, channels), lambda i: (0, 0))],
        out_specs=pl.BlockSpec((16, channels, lanes), lambda i: (i, 0, 0)),
        scratch_shapes=[pltpu.VMEM((channels, levels), f32)],
        compiler_params=params(60),
        cost_estimate=cost(levels * channels * lanes, 0, 4 * levels * channels * lanes),
        name="spread",
    )(absorb)

    wide = 32
    evolved, field, top, bottom, left, right = pl.pallas_call(
        functools.partial(column_kernel, capacity, halo),
        out_shape=(
            jax.ShapeDtypeStruct((dev_count, capacity, channels), f32),
            jax.ShapeDtypeStruct((tile_rows, tile_cols, levels), f32),
            jax.ShapeDtypeStruct((halo + 1, tile_cols, levels), jnp.int16),
            jax.ShapeDtypeStruct((halo + 1, tile_cols, levels), jnp.int16),
            jax.ShapeDtypeStruct((tile_rows + 2 * halo + 3, halo, levels), jnp.int16),
            jax.ShapeDtypeStruct((tile_rows + 2 * halo + 3, halo, levels), jnp.int16),
        ),
        in_specs=[vmem()] * 2 + [hbm()] + [vmem()] * 2,
        out_specs=(vmem(),) * 6,
        scratch_shapes=[
            pltpu.SMEM((slots // lanes, lanes), jnp.int32),
        pltpu.VMEM((slots // lanes, lanes), jnp.int32),
            pltpu.SemaphoreType.DMA,
            pltpu.SemaphoreType.DMA((channels // wide,)),
            pltpu.VMEM((cells, levels), f32),
            pltpu.VMEM((levels, channels, lanes), f32),
            pltpu.VMEM((channels, lanes), f32),
            pltpu.VMEM((channels, lanes), f32),
            pltpu.VMEM((4, lanes, levels), f32),
            pltpu.VMEM((4, lanes, levels), f32),
            pltpu.VMEM((levels, lanes), f32),
            pltpu.VMEM((levels, lanes), f32),
            pltpu.VMEM((channels, lanes), f32),
            pltpu.VMEM((channels, lanes), f32),
            pltpu.VMEM((levels, wide, lanes), f32),
            pltpu.VMEM((levels, wide, lanes), f32),
            pltpu.VMEM((levels * 8, lanes), f32),
            pltpu.VMEM((4, cells, levels), f32),
        ],
        compiler_params=params(60),
        cost_estimate=cost(
            14 * slots * levels * channels, 2 * slots * levels * channels, 12 * cells * levels
        ),
        name="column",
    )(
        recv, background, absorb_wide, sensitivity.reshape(1, channels),
        inverse_variance.reshape(1, channels)
    )

    field_halos = halos(top, bottom, left, right, join_in_place)
    lat_at = lax.axis_index("lat")
    inside = jnp.stack([lat_at > 0, lat_at < lat_count - 1]).astype(f32)
    height, breadth = tile_rows + 2 * halo, tile_cols + 2 * halo

    plain = pltpu.VMEM((height, breadth, levels), f32)
    mixed = (height, breadth // 8, 8, levels)

    east, south = pl.pallas_call(
        functools.partial(edges_kernel, halo),
        out_shape=(jax.ShapeDtypeStruct(mixed, f32),) * 2,
        in_specs=[smem()] + [vmem()] * 3 + [hbm()] * 2,
        out_specs=(vmem(),) * 2,
        scratch_shapes=[plain]
        + [pltpu.VMEM((height, halo, levels), jnp.int16)] * 2
        + [pltpu.SemaphoreType.DMA((2,))],
        compiler_params=params(22),
        cost_estimate=cost(4 * height * breadth * levels, 0, 12 * cells * levels),
        name="edges",
    )(inside, diffusivity, *kappa_halos)


    returned = lax.all_to_all(
        evolved, ("lat", "lon"), split_axis=0, concat_axis=0, tiled=True
    )

    departure = pl.pallas_call(
        depart_kernel,
        out_shape=jax.ShapeDtypeStruct((foot_count, channels), f32),
        in_specs=[vmem()] * 3,
        out_specs=vmem(),
        compiler_params=params(16),
        cost_estimate=cost(2 * slots * foot_count * channels * 3, 0, 4 * slots * channels * 2),
        name="depart",
    )(slot, returned.reshape(slots, channels), observed)

    increment = pl.pallas_call(
        functools.partial(relax_kernel, halo),
        out_shape=jax.ShapeDtypeStruct((tile_rows, tile_cols, levels), f32),
        in_specs=[smem()] + [vmem()] * 7,
        out_specs=vmem(),
        scratch_shapes=[plain, pltpu.VMEM(mixed, f32), pltpu.VMEM(mixed, f32)],
        compiler_params=params(26),
        cost_estimate=cost(10 * STEPS * height * breadth * levels, 0, 16 * cells * levels),
        name="relax",
    )(inside, field, *field_halos, east, south)
    return (departure, increment)


def solution(mesh):
    in_specs = (
        P("lat", "lon", None),
        P("lat", "lon", None),
        P(("lat", "lon"), None),
        P(("lat", "lon")),
        P(("lat", "lon"), None),
        P(("lat", "lon"), None),
        P(("lat", "lon"), None),
        P(),
        P(),
        P(),
    )
    out_specs = (P(("lat", "lon"), None), P("lat", "lon", None))

    return jax.shard_map(local, mesh=mesh, in_specs=in_specs, out_specs=out_specs, check_vma=False)
```

```python
import functools
import math

import jax
import jax.numpy as jnp
from jax import lax
from jax.experimental import pallas as pl
from jax.experimental.pallas import tpu as pltpu
from jax.sharding import PartitionSpec as P


STEPS = 8
REJECTED = 64.0
META = 8
LOG2E = math.log2(math.e)
LN2 = math.log(2.0)
MIB = 1024 * 1024
UNROLL = 32


def thirds(x):
    high = x.astype(jnp.bfloat16)
    rest = x - high.astype(jnp.float32)
    mid = rest.astype(jnp.bfloat16)
    low = (rest - mid.astype(jnp.float32)).astype(jnp.bfloat16)
    return high, mid, low


def add_thirds(x):
    width = x.shape[1] // 3
    return (x[:, :width] + x[:, width : 2 * width]) + x[:, 2 * width :]


def dot_f32(a, b, contract):
    return lax.dot_general(a, b, (contract, ((), ())), preferred_element_type=jnp.float32)


def iota(shape, dim):
    return lax.broadcasted_iota(jnp.int32, shape, dim)


def pack_kernel(
    dev_count, capacity, tile_cols, lane_ref, tile_ref, anchor_ref, weights_ref, observed_ref,
    accept_ref, send_ref, slot_ref, vals_ref
):
    foot_count, channels = observed_ref.shape
    bf16 = jnp.bfloat16
    tile = tile_ref[...]
    onehot = jnp.where(iota((dev_count, foot_count), 0) == tile, 1.0, 0.0)
    earlier = jnp.where(
        iota((foot_count, foot_count), 0) < iota((foot_count, foot_count), 1), 1.0, 0.0
    ).astype(bf16)
    before = dot_f32(onehot.astype(bf16), earlier, ((1,), (0,)))
    rank = jnp.sum(before * onehot, axis=0, keepdims=True).astype(jnp.int32)
    slot = tile * capacity + rank
    slot_ref[...] = slot

    chosen = jnp.where(accept_ref[...] != 0, observed_ref[...], REJECTED)
    parts = jnp.concatenate(thirds(chosen), axis=1)
    per_chunk = max(1, 128 // capacity)
    chunk = per_chunk * capacity
    for start in range(0, dev_count, per_chunk):
        place = jnp.where(
            iota((chunk, foot_count), 0) + start * capacity == slot, 1.0, 0.0
        ).astype(bf16)
        rows = add_thirds(dot_f32(place, parts, ((1,), (0,))))
        send_ref[start : start + per_chunk, :capacity, :] = rows.reshape(
            per_chunk, capacity, channels
        )

    anchor = anchor_ref[...]
    line = jnp.floor((anchor.astype(jnp.float32) + 0.5) * (1.0 / (tile_cols - 1)))
    base = anchor.astype(jnp.float32) + line
    weights = weights_ref[...]
    shares = weights / jnp.sum(weights, axis=0, keepdims=True)
    meta = jnp.concatenate(
        [base, shares, jnp.zeros((META - 5, foot_count), jnp.float32)], axis=0
    )
    for dev in range(dev_count):
        vals_ref[dev * META : (dev + 1) * META, :] = jnp.where(tile == dev, meta, 0.0)
    lanes = jnp.where(
        iota((channels, foot_count), 0) == rank + lane_ref[0], 1.0, 0.0
    ).astype(bf16)
    rows = [dot_f32(part, lanes, ((1,), (1,))) for part in thirds(vals_ref[...])]
    rows = (rows[0] + rows[1]) + rows[2]
    send_ref[:, capacity:, :] = rows.reshape(dev_count, META, channels)


def spread_kernel(absorb_ref, out_ref, turned_ref):
    some, channels, lanes = out_ref.shape
    levels = absorb_ref.shape[0]

    @pl.when(pl.program_id(0) == 0)
    def _():
        turned_ref[...] = (absorb_ref[...] * LOG2E).T

    turned = turned_ref[...]
    for u in range(some):
        out_ref[u] = jnp.broadcast_to(turned[:, u : u + 1], (channels, lanes))
    turned_ref[...] = pltpu.roll(turned, levels - some, 1)


def column_kernel(
    capacity, halo, recv_ref, background_ref, absorb_any, sensitivity_ref, inverse_ref,
    evolved_ref, field_ref, top_ref, bottom_ref, left_ref, right_ref,
    base_ref, slot_base_ref, sem, absorb_sem, cells_ref, absorb_b, slope_b, inverse_b, taken_ref, terms_ref, profile_ref,
    rise_ref, obs_ref, evo_ref, main_ref, side_ref, push_ref, sums_ref
):
    dev_count = recv_ref.shape[0]
    tile_rows, tile_cols, levels = background_ref.shape
    cells = tile_rows * tile_cols
    levels, channels, lanes = absorb_b.shape
    group = lanes // capacity
    blocks = dev_count // group
    wide = main_ref.shape[1]
    per_loop = UNROLL * wide * lanes // (levels * channels)
    corners = (0, 1, tile_cols, tile_cols + 1)

    rows = recv_ref[:, capacity, :].reshape(blocks, group, lanes)
    slot_base_ref[...] = jnp.sum(rows, axis=1).astype(jnp.int32)
    copy = pltpu.make_async_copy(slot_base_ref, base_ref, sem)
    copy.start()

    def absorb_copy(c):
        some = pl.ds(pl.multiple_of(c * wide, wide), wide)
        return pltpu.make_async_copy(
            absorb_any.at[:, some, :], absorb_b.at[:, some, :], absorb_sem.at[c]
        )

    for c in range(channels // wide):
        absorb_copy(c).start()

    cells_ref[...] = background_ref[...].reshape(cells, levels).astype(jnp.float32)
    slope_b[...] = jnp.broadcast_to(sensitivity_ref[...] * LOG2E, (lanes, channels)).T
    inverse_b[...] = jnp.broadcast_to(inverse_ref[...], (lanes, channels)).T

    sums_ref[...] = jnp.zeros_like(sums_ref)
    terms_ref[...] = jnp.zeros_like(terms_ref)
    copy.wait()

    def gather(f, at):
        base = base_ref[f, at]
        for k, step in enumerate(corners):
            taken_ref[k, pl.ds(at, 1), :] = cells_ref[pl.ds(base + step, 1), :]

    def scatter(f, at):
        base = base_ref[f, at]
        for k, step in enumerate(corners):
            sums_ref[k, pl.ds(base + step, 1), :] += terms_ref[k, pl.ds(at, 1), :]

    def gather_first(i, carry):
        for u in range(8):
            gather(0, i * 8 + u)
        return carry

    lax.fori_loop(0, lanes // 8, gather_first, 0)

    def block(f, carry):
        before = jnp.maximum(f - 1, 0)
        after = jnp.minimum(f + 1, blocks - 1)
        mine = recv_ref[pl.ds(f * group, group)]
        shares = jnp.sum(mine[:, capacity:, :], axis=0)
        obs_ref[...] = mine[:, :capacity, :].reshape(lanes, channels).T
        profile = shares[1:2] * taken_ref[0].T
        for k in range(1, 4):
            profile = profile + shares[k + 1 : k + 2] * taken_ref[k].T
        profile_ref[...] = profile
        rise_ref[0 : levels - 1, :] = profile[1:] - profile[:-1]
        rise_ref[levels - 1 : levels, :] = jnp.zeros((1, lanes), jnp.float32)
        push_ref[...] = jnp.zeros_like(push_ref)

        def some_channels(c, carry):
            @pl.when(f == 0)
            def _():
                absorb_copy(c).wait()

            at = pl.multiple_of(c * wide, wide)
            slope = slope_b[pl.ds(at, wide), :]
            scale = slope * (LN2 * LN2)

            def down(i, state):
                path, total, above = state
                for u in range(UNROLL):
                    level = i * UNROLL + u
                    depth = absorb_b[level, pl.ds(at, wide), :] * jnp.exp2(
                        slope * profile_ref[pl.ds(level, 1), :]
                    )
                    path = path - depth
                    trans = jnp.exp2(path)
                    side = depth * scale
                    side_ref[level] = side
                    main_ref[level] = (above - trans) + side * total
                    total = total + trans * rise_ref[pl.ds(level, 1), :]
                    above = trans
                for u in range(per_loop):
                    scatter(before, (c * (levels // UNROLL) + i) * per_loop + u)
                return path, total, above

            zero = jnp.zeros((wide, lanes), jnp.float32)
            _, total, last = lax.fori_loop(0, levels // UNROLL, down, (zero, zero, zero + 1.0))
            main_ref[levels - 1] += last
            evolved = total + profile_ref[0:1, :]
            evo_ref[pl.ds(at, wide), :] = evolved
            obs = obs_ref[pl.ds(at, wide), :]
            force = jnp.where(
                obs < 0.5 * REJECTED, inverse_b[pl.ds(at, wide), :] * (obs - evolved), 0.0
            )

            def up(i, carry):
                for u in range(UNROLL):
                    level = i * UNROLL + u
                    push = force * (main_ref[level] - total * side_ref[level])
                    push_ref[pl.ds(pl.multiple_of(level * 8, 8), 8), :] += jnp.sum(
                        push.reshape(wide // 8, 8, lanes), axis=0
                    )
                for u in range(per_loop):
                    gather(after, (c * (levels // UNROLL) + i) * per_loop + u)
                return carry

            lax.fori_loop(0, levels // UNROLL, up, 0)
            return carry

        lax.fori_loop(0, channels // wide, some_channels, 0)
        evolved_ref[pl.ds(f * group, group)] = evo_ref[...].T.reshape(group, capacity, channels)
        push = push_ref[pl.ds(0, levels, stride=8), :]
        for u in range(1, 8):
            push = push + push_ref[pl.ds(u, levels, stride=8), :]
        for k in range(4):
            terms_ref[k] = (shares[k + 1 : k + 2] * push).T
        return carry

    lax.fori_loop(0, blocks, block, 0)

    def scatter_last(i, carry):
        for u in range(8):
            scatter(blocks - 1, i * 8 + u)
        return carry

    lax.fori_loop(0, lanes // 8, scatter_last, 0)

    def add_up(r, carry):
        row = pl.ds(pl.multiple_of(r * tile_cols, tile_cols), tile_cols)
        total = (sums_ref[0, row, :] + sums_ref[1, row, :]) + (
            sums_ref[2, row, :] + sums_ref[3, row, :]
        )
        field_ref[r] = total
        return jnp.maximum(carry, jnp.maximum(jnp.abs(total[:halo]), jnp.abs(total[-halo:])))

    peak = lax.fori_loop(
        0, tile_rows, add_up, jnp.full((halo, levels), 1e-30, jnp.float32), unroll=2
    )
    for r in (*range(halo), *range(tile_rows - halo, tile_rows)):
        for first in range(0, tile_cols, halo):
            peak = jnp.maximum(peak, jnp.abs(field_ref[r, first : first + halo]))
    power = jnp.ceil(jnp.log2(jnp.max(peak, axis=0, keepdims=True)))
    scale = jnp.exp2(15.0 - power)

    def code(x):
        whole = jnp.clip(jnp.floor(x * scale + 0.5), -32767.0, 32767.0)
        return whole.astype(jnp.int32).astype(jnp.int16)

    def code_sides(r, carry):
        left_ref[halo + 1 + r] = code(field_ref[r, :halo])
        right_ref[halo + 1 + r] = code(field_ref[r, tile_cols - halo :])
        return carry

    lax.fori_loop(0, tile_rows, code_sides, 0, unroll=4)
    for r in range(halo):
        top_ref[r] = code(field_ref[r])
        bottom_ref[r] = code(field_ref[tile_rows - halo + r])
    for ref, last in (
        (top_ref, halo), (bottom_ref, halo),
        (left_ref, halo + 1 + tile_rows), (right_ref, halo + 1 + tile_rows),
    ):
        ref[last] = jnp.broadcast_to(power, ref.shape[1:]).astype(jnp.int32).astype(jnp.int16)


def decode_field(coded, power):
    scale = jnp.exp2(power.astype(jnp.int32).astype(jnp.float32) - 15.0)
    return coded.astype(jnp.int32).astype(jnp.float32) * scale


def lay(halo, target, centre, north, south, west, east):
    tile_rows, tile_cols, _ = centre.shape
    breadth = tile_cols + 2 * halo
    mid_r, mid_c = slice(halo, halo + tile_rows), slice(halo, halo + tile_cols)
    target[mid_r, mid_c] = centre[...]
    target[:halo, mid_c] = decode_field(north[:halo], north[halo])
    target[halo + tile_rows :, mid_c] = decode_field(south[:halo], south[halo])
    for side, cols in ((west, slice(0, halo)), (east, slice(halo + tile_cols, breadth))):
        read, put = 0, 0
        for count in (halo, tile_rows, halo):
            target[put : put + count, cols] = decode_field(
                side[read : read + count], side[read + count]
            )
            read, put = read + count + 1, put + count


KAPPA_LOW = 0.12
KAPPA_STEP = 0.125 / 65535


def encode_kappa(x):
    whole = jnp.round((x - KAPPA_LOW) * (1.0 / KAPPA_STEP))
    return (jnp.clip(whole, 0.0, 65535.0) - 32768.0).astype(jnp.int16)


def decode_kappa(x):
    whole = x.astype(jnp.int32).astype(jnp.float32) + 32768.0
    return whole * KAPPA_STEP + KAPPA_LOW


def mixed_row(plain_ref, i, stretch):
    return jnp.stack([plain_ref[i, pl.ds(t, 8, stride=stretch), :] for t in range(stretch)])


def eastward(x):
    return jnp.concatenate([x[1:], pltpu.roll(x[0], 7, 0)[None]], axis=0)


def westward(x):
    return jnp.concatenate([pltpu.roll(x[-1], 1, 0)[None], x[:-1]], axis=0)


def edges_kernel(
    halo, inside_ref, centre_ref, north_ref, south_ref, west_hbm, east_hbm, east_ref,
    south_edge_ref, plain_ref, west_ref, east_side_ref, sems
):
    copies = [
        pltpu.make_async_copy(west_hbm, west_ref, sems.at[0]),
        pltpu.make_async_copy(east_hbm, east_side_ref, sems.at[1]),
    ]
    for copy in copies:
        copy.start()
    tile_rows, tile_cols, _ = centre_ref.shape
    height, _ = plain_ref.shape[:2]
    mid_r, mid_c = slice(halo, halo + tile_rows), slice(halo, halo + tile_cols)
    low, end = slice(0, halo), slice(halo + tile_rows, height)
    plain_ref[mid_r, mid_c] = centre_ref[...]
    plain_ref[low, mid_c] = decode_kappa(north_ref[...])
    plain_ref[end, mid_c] = decode_kappa(south_ref[...])
    for copy in copies:
        copy.wait()
    plain_ref[:, :halo] = decode_kappa(west_ref[...])
    plain_ref[:, halo + tile_cols :] = decode_kappa(east_side_ref[...])
    plain_ref[low] = plain_ref[low] * inside_ref[0]
    plain_ref[end] = plain_ref[end] * inside_ref[1]
    stretch = east_ref.shape[1]

    def edges(i, here):
        below = mixed_row(plain_ref, i + 1, stretch)
        east_ref[i] = 0.5 * (here + eastward(here))
        south_edge_ref[i] = 0.5 * (here + below)
        return below

    lax.fori_loop(0, height - 1, edges, mixed_row(plain_ref, 0, stretch), unroll=2)


def relax_kernel(
    halo, inside_ref, centre_ref, north_ref, south_ref, west_ref, east_side_ref, east_ref,
    south_edge_ref, out_ref, plain_ref, first_ref, second_ref
):
    tile_rows, tile_cols, _ = out_ref.shape
    height = tile_rows + 2 * halo
    stretch = first_ref.shape[1]
    lay(halo, plain_ref, centre_ref, north_ref, south_ref, west_ref, east_side_ref)

    source, target = None, second_ref
    for step in range(1, halo + 1):
        last = step == halo

        def read(i, source=source):
            return mixed_row(plain_ref, i, stretch) if source is None else source[i]

        def row(i, carry, scale=None, read=read, target=target, last=last):
            here, from_north = carry
            below = read(i + 1)
            to_east = east_ref[i] * (eastward(here) - here)
            from_south = south_edge_ref[i] * (below - here)
            value = here + (to_east - westward(to_east)) + (from_south - from_north)
            if scale is not None:
                value = value * scale
            if last:
                for t in range(stretch):
                    plain_ref[i, pl.ds(t, 8, stride=stretch), :] = value[t]
            else:
                target[i] = value
            return below, from_south

        here = read(step)
        carry = (here, south_edge_ref[step - 1] * (here - read(step - 1)))
        carry = lax.fori_loop(
            step, halo, functools.partial(row, scale=inside_ref[0]), carry, unroll=True
        )
        carry = lax.fori_loop(halo, halo + tile_rows, row, carry, unroll=4)
        lax.fori_loop(
            halo + tile_rows, height - step, functools.partial(row, scale=inside_ref[1]), carry,
            unroll=True,
        )
        source, target = target, first_ref if target is second_ref else second_ref
    out_ref[...] = plain_ref[halo : halo + tile_rows, halo : halo + tile_cols, :]


def depart_kernel(slot_ref, evolved_ref, observed_ref, out_ref):
    foot_count, _ = observed_ref.shape
    slots = evolved_ref.shape[0]
    slot = slot_ref[...]
    parts = jnp.concatenate(thirds(evolved_ref[...]), axis=1)
    chosen = jnp.where(iota((slots, foot_count), 0) == slot, 1.0, 0.0).astype(jnp.bfloat16)
    out_ref[...] = observed_ref[...] - add_thirds(dot_f32(chosen, parts, ((0,), (0,))))


def vmem():
    return pl.BlockSpec(memory_space=pltpu.VMEM)


def smem():
    return pl.BlockSpec(memory_space=pltpu.SMEM)


def hbm():
    return pl.BlockSpec(memory_space=pltpu.HBM)


def params(mib):
    return pltpu.CompilerParams(vmem_limit_bytes=mib * MIB)


def cost(flops, transcendentals, moved):
    return pl.CostEstimate(flops=flops, transcendentals=transcendentals, bytes_accessed=moved)


def neighbours(axis, periodic):
    count = lax.axis_size(axis)
    forward = [(i, i + 1) for i in range(count - 1)]
    if periodic:
        forward.append((count - 1, 0))
    return forward, [(target, source) for source, target in forward]


def join(north, south, left, right):
    halo = left.shape[1]
    right = jnp.concatenate([north[:, -halo:], right, south[:, -halo:]], axis=0)
    left = jnp.concatenate([north[:, :halo], left, south[:, :halo]], axis=0)
    return left, right


def join_kernel(north_ref, south_ref, _, __, left_ref, right_ref, sems):
    count, tile_cols, _ = north_ref.shape
    total, halo, _ = left_ref.shape
    copies = []
    for target, cols in ((left_ref, 0), (right_ref, tile_cols - halo)):
        for source, row in ((north_ref, 0), (south_ref, total - count)):
            copies.append(
                pltpu.make_async_copy(
                    source.at[:, pl.ds(cols, halo)], target.at[pl.ds(row, count)],
                    sems.at[len(copies)],
                )
            )
    for copy in copies:
        copy.start()
    for copy in copies:
        copy.wait()


def join_in_place(north, south, left, right):
    return pl.pallas_call(
        join_kernel,
        out_shape=tuple(jax.ShapeDtypeStruct(x.shape, x.dtype) for x in (left, right)),
        in_specs=[vmem()] * 2 + [hbm()] * 2,
        out_specs=(hbm(), hbm()),
        input_output_aliases={2: 0, 3: 1},
        scratch_shapes=[pltpu.SemaphoreType.DMA((4,))],
        compiler_params=params(2),
        name="join",
    )(north, south, left, right)


def halos(top, bottom, left, right, join):
    lat_up, lat_down = neighbours("lat", False)
    lon_up, lon_down = neighbours("lon", True)
    south = lax.ppermute(top, "lat", lat_down)
    north = lax.ppermute(bottom, "lat", lat_up)
    lefts, rights = join(north, south, left, right)
    west = lax.ppermute(rights, "lon", lon_up)
    east = lax.ppermute(lefts, "lon", lon_down)
    return north, south, west, east


def local(
    background, diffusivity, tile_index, anchor, weights, observed, accept, absorb, sensitivity,
    inverse_variance
):
    f32 = jnp.float32
    lat_count = lax.axis_size("lat")
    lon_count = lax.axis_size("lon")
    dev_count = lat_count * lon_count
    foot_count, channels = observed.shape
    capacity = max(2, 2 * foot_count // dev_count)
    tile_rows, tile_cols, levels = background.shape
    slots = dev_count * capacity
    lanes = 128
    group = lanes // capacity
    cells = tile_rows * tile_cols
    halo = STEPS

    me = lax.axis_index("lat") * lon_count + lax.axis_index("lon")
    lane = (lax.rem(me, group) * capacity).astype(jnp.int32).reshape(1)
    send, slot = pl.pallas_call(
        functools.partial(pack_kernel, dev_count, capacity, tile_cols),
        out_shape=(
            jax.ShapeDtypeStruct((dev_count, capacity + META, channels), f32),
            jax.ShapeDtypeStruct((1, foot_count), jnp.int32),
        ),
        in_specs=[smem()] + [vmem()] * 5,
        out_specs=(vmem(), vmem()),
        scratch_shapes=[pltpu.VMEM((dev_count * META, foot_count), f32)],
        compiler_params=params(60),
        cost_estimate=cost(2 * slots * foot_count * channels * 3, 0, 4 * slots * channels * 3),
        name="pack",
    )(
        lane, tile_index.reshape(1, foot_count), anchor.reshape(1, foot_count), weights.T,
        observed, accept
    )
    recv = lax.all_to_all(send, ("lat", "lon"), split_axis=0, concat_axis=0, tiled=True)

    kappa_halos = halos(
        encode_kappa(diffusivity[:halo]), encode_kappa(diffusivity[-halo:]),
        encode_kappa(diffusivity[:, :halo]), encode_kappa(diffusivity[:, -halo:]), join
    )
    absorb_wide = pl.pallas_call(
        spread_kernel,
        out_shape=jax.ShapeDtypeStruct((levels, channels, lanes), f32),
        grid=(levels // 16,),
        in_specs=[pl.BlockSpec((levels, channels), lambda i: (0, 0))],
        out_specs=pl.BlockSpec((16, channels, lanes), lambda i: (i, 0, 0)),
        scratch_shapes=[pltpu.VMEM((channels, levels), f32)],
        compiler_params=params(60),
        cost_estimate=cost(levels * channels * lanes, 0, 4 * levels * channels * lanes),
        name="spread",
    )(absorb)

    wide = 32
    evolved, field, top, bottom, left, right = pl.pallas_call(
        functools.partial(column_kernel, capacity, halo),
        out_shape=(
            jax.ShapeDtypeStruct((dev_count, capacity, channels), f32),
            jax.ShapeDtypeStruct((tile_rows, tile_cols, levels), f32),
            jax.ShapeDtypeStruct((halo + 1, tile_cols, levels), jnp.int16),
            jax.ShapeDtypeStruct((halo + 1, tile_cols, levels), jnp.int16),
            jax.ShapeDtypeStruct((tile_rows + 2 * halo + 3, halo, levels), jnp.int16),
            jax.ShapeDtypeStruct((tile_rows + 2 * halo + 3, halo, levels), jnp.int16),
        ),
        in_specs=[vmem()] * 2 + [hbm()] + [vmem()] * 2,
        out_specs=(vmem(),) * 6,
        scratch_shapes=[
            pltpu.SMEM((slots // lanes, lanes), jnp.int32),
        pltpu.VMEM((slots // lanes, lanes), jnp.int32),
            pltpu.SemaphoreType.DMA,
            pltpu.SemaphoreType.DMA((channels // wide,)),
            pltpu.VMEM((cells, levels), f32),
            pltpu.VMEM((levels, channels, lanes), f32),
            pltpu.VMEM((channels, lanes), f32),
            pltpu.VMEM((channels, lanes), f32),
            pltpu.VMEM((4, lanes, levels), f32),
            pltpu.VMEM((4, lanes, levels), f32),
            pltpu.VMEM((levels, lanes), f32),
            pltpu.VMEM((levels, lanes), f32),
            pltpu.VMEM((channels, lanes), f32),
            pltpu.VMEM((channels, lanes), f32),
            pltpu.VMEM((levels, wide, lanes), f32),
            pltpu.VMEM((levels, wide, lanes), f32),
            pltpu.VMEM((levels * 8, lanes), f32),
            pltpu.VMEM((4, cells, levels), f32),
        ],
        compiler_params=params(50),
        cost_estimate=cost(
            14 * slots * levels * channels, 2 * slots * levels * channels, 12 * cells * levels
        ),
        name="column",
    )(
        recv, background, absorb_wide, sensitivity.reshape(1, channels),
        inverse_variance.reshape(1, channels)
    )

    field_halos = halos(top, bottom, left, right, join_in_place)
    lat_at = lax.axis_index("lat")
    inside = jnp.stack([lat_at > 0, lat_at < lat_count - 1]).astype(f32)
    height, breadth = tile_rows + 2 * halo, tile_cols + 2 * halo

    plain = pltpu.VMEM((height, breadth, levels), f32)
    mixed = (height, breadth // 8, 8, levels)

    east, south = pl.pallas_call(
        functools.partial(edges_kernel, halo),
        out_shape=(jax.ShapeDtypeStruct(mixed, f32),) * 2,
        in_specs=[smem()] + [vmem()] * 3 + [hbm()] * 2,
        out_specs=(vmem(),) * 2,
        scratch_shapes=[plain]
        + [pltpu.VMEM((height, halo, levels), jnp.int16)] * 2
        + [pltpu.SemaphoreType.DMA((2,))],
        compiler_params=params(22),
        cost_estimate=cost(4 * height * breadth * levels, 0, 12 * cells * levels),
        name="edges",
    )(inside, diffusivity, *kappa_halos)


    returned = lax.all_to_all(
        evolved, ("lat", "lon"), split_axis=0, concat_axis=0, tiled=True
    )

    departure = pl.pallas_call(
        depart_kernel,
        out_shape=jax.ShapeDtypeStruct((foot_count, channels), f32),
        in_specs=[vmem()] * 3,
        out_specs=vmem(),
        compiler_params=params(16),
        cost_estimate=cost(2 * slots * foot_count * channels * 3, 0, 4 * slots * channels * 2),
        name="depart",
    )(slot, returned.reshape(slots, channels), observed)

    increment = pl.pallas_call(
        functools.partial(relax_kernel, halo),
        out_shape=jax.ShapeDtypeStruct((tile_rows, tile_cols, levels), f32),
        in_specs=[smem()] + [vmem()] * 7,
        out_specs=vmem(),
        scratch_shapes=[plain, pltpu.VMEM(mixed, f32), pltpu.VMEM(mixed, f32)],
        compiler_params=params(26),
        cost_estimate=cost(10 * STEPS * height * breadth * levels, 0, 16 * cells * levels),
        name="relax",
    )(inside, field, *field_halos, east, south)
    return (departure, increment)


def solution(mesh):
    in_specs = (
        P("lat", "lon", None),
        P("lat", "lon", None),
        P(("lat", "lon"), None),
        P(("lat", "lon")),
        P(("lat", "lon"), None),
        P(("lat", "lon"), None),
        P(("lat", "lon"), None),
        P(),
        P(),
        P(),
    )
    out_specs = (P(("lat", "lon"), None), P("lat", "lon", None))

    return jax.shard_map(local, mesh=mesh, in_specs=in_specs, out_specs=out_specs, check_vma=False)
```

```python
import functools
import math

import jax
import jax.numpy as jnp
from jax import lax
from jax.experimental import pallas as pl
from jax.experimental.pallas import tpu as pltpu
from jax.sharding import PartitionSpec as P


STEPS = 8
REJECTED = 64.0
META = 8
LOG2E = math.log2(math.e)
LN2 = math.log(2.0)
MIB = 1024 * 1024
UNROLL = 32


def thirds(x):
    high = x.astype(jnp.bfloat16)
    rest = x - high.astype(jnp.float32)
    mid = rest.astype(jnp.bfloat16)
    low = (rest - mid.astype(jnp.float32)).astype(jnp.bfloat16)
    return high, mid, low


def add_thirds(x):
    width = x.shape[1] // 3
    return (x[:, :width] + x[:, width : 2 * width]) + x[:, 2 * width :]


def dot_f32(a, b, contract):
    return lax.dot_general(a, b, (contract, ((), ())), preferred_element_type=jnp.float32)


def iota(shape, dim):
    return lax.broadcasted_iota(jnp.int32, shape, dim)


def pack_kernel(
    dev_count, capacity, tile_cols, lane_ref, tile_ref, anchor_ref, weights_ref, observed_ref,
    accept_ref, send_ref, slot_ref, vals_ref
):
    foot_count, channels = observed_ref.shape
    bf16 = jnp.bfloat16
    tile = tile_ref[...]
    onehot = jnp.where(iota((dev_count, foot_count), 0) == tile, 1.0, 0.0)
    earlier = jnp.where(
        iota((foot_count, foot_count), 0) < iota((foot_count, foot_count), 1), 1.0, 0.0
    ).astype(bf16)
    before = dot_f32(onehot.astype(bf16), earlier, ((1,), (0,)))
    rank = jnp.sum(before * onehot, axis=0, keepdims=True).astype(jnp.int32)
    slot = tile * capacity + rank
    slot_ref[...] = slot

    chosen = jnp.where(accept_ref[...] != 0, observed_ref[...], REJECTED)
    parts = jnp.concatenate(thirds(chosen), axis=1)
    per_chunk = max(1, 128 // capacity)
    chunk = per_chunk * capacity
    for start in range(0, dev_count, per_chunk):
        place = jnp.where(
            iota((chunk, foot_count), 0) + start * capacity == slot, 1.0, 0.0
        ).astype(bf16)
        rows = add_thirds(dot_f32(place, parts, ((1,), (0,))))
        send_ref[start : start + per_chunk, :capacity, :] = rows.reshape(
            per_chunk, capacity, channels
        )

    anchor = anchor_ref[...]
    line = jnp.floor((anchor.astype(jnp.float32) + 0.5) * (1.0 / (tile_cols - 1)))
    base = anchor.astype(jnp.float32) + line
    weights = weights_ref[...]
    shares = weights / jnp.sum(weights, axis=0, keepdims=True)
    meta = jnp.concatenate(
        [base, shares, jnp.zeros((META - 5, foot_count), jnp.float32)], axis=0
    )
    for dev in range(dev_count):
        vals_ref[dev * META : (dev + 1) * META, :] = jnp.where(tile == dev, meta, 0.0)
    lanes = jnp.where(
        iota((channels, foot_count), 0) == rank + lane_ref[0], 1.0, 0.0
    ).astype(bf16)
    rows = [dot_f32(part, lanes, ((1,), (1,))) for part in thirds(vals_ref[...])]
    rows = (rows[0] + rows[1]) + rows[2]
    send_ref[:, capacity:, :] = rows.reshape(dev_count, META, channels)


def spread_kernel(absorb_ref, out_ref, turned_ref):
    some, channels, lanes = out_ref.shape
    levels = absorb_ref.shape[0]

    @pl.when(pl.program_id(0) == 0)
    def _():
        turned_ref[...] = (absorb_ref[...] * LOG2E).T

    turned = turned_ref[...]
    for u in range(some):
        out_ref[u] = jnp.broadcast_to(turned[:, u : u + 1], (channels, lanes))
    turned_ref[...] = pltpu.roll(turned, levels - some, 1)


def column_kernel(
    capacity, halo, recv_ref, background_hbm, absorb_any, sensitivity_ref, inverse_ref,
    evolved_ref, field_ref, top_ref, bottom_ref, left_ref, right_ref,
    base_ref, slot_base_ref, sem, absorb_sem, background_ref, background_sem, cells_ref, absorb_b, slope_b, inverse_b, taken_ref, terms_ref, profile_ref,
    rise_ref, obs_ref, evo_ref, main_ref, side_ref, push_ref, sums_ref
):
    dev_count = recv_ref.shape[0]
    tile_rows, tile_cols, levels = background_ref.shape
    cells = tile_rows * tile_cols
    levels, channels, lanes = absorb_b.shape
    group = lanes // capacity
    blocks = dev_count // group
    wide = main_ref.shape[1]
    per_loop = UNROLL * wide * lanes // (levels * channels)
    corners = (0, 1, tile_cols, tile_cols + 1)

    background_copy = pltpu.make_async_copy(background_hbm, background_ref, background_sem)
    background_copy.start()
    rows = recv_ref[:, capacity, :].reshape(blocks, group, lanes)
    slot_base_ref[...] = jnp.sum(rows, axis=1).astype(jnp.int32)
    copy = pltpu.make_async_copy(slot_base_ref, base_ref, sem)
    copy.start()

    def absorb_copy(c):
        some = pl.ds(pl.multiple_of(c * wide, wide), wide)
        return pltpu.make_async_copy(
            absorb_any.at[:, some, :], absorb_b.at[:, some, :], absorb_sem.at[c]
        )

    for c in range(channels // wide):
        absorb_copy(c).start()

    slope_b[...] = jnp.broadcast_to(sensitivity_ref[...] * LOG2E, (lanes, channels)).T
    inverse_b[...] = jnp.broadcast_to(inverse_ref[...], (lanes, channels)).T

    sums_ref[...] = jnp.zeros_like(sums_ref)
    terms_ref[...] = jnp.zeros_like(terms_ref)
    background_copy.wait()
    cells_ref[...] = background_ref[...].reshape(cells, levels).astype(jnp.float32)
    copy.wait()

    def gather(f, at):
        base = base_ref[f, at]
        for k, step in enumerate(corners):
            taken_ref[k, pl.ds(at, 1), :] = cells_ref[pl.ds(base + step, 1), :]

    def scatter(f, at):
        base = base_ref[f, at]
        for k, step in enumerate(corners):
            sums_ref[k, pl.ds(base + step, 1), :] += terms_ref[k, pl.ds(at, 1), :]

    def gather_first(i, carry):
        for u in range(8):
            gather(0, i * 8 + u)
        return carry

    lax.fori_loop(0, lanes // 8, gather_first, 0)

    def block(f, carry):
        before = jnp.maximum(f - 1, 0)
        after = jnp.minimum(f + 1, blocks - 1)
        mine = recv_ref[pl.ds(f * group, group)]
        shares = jnp.sum(mine[:, capacity:, :], axis=0)
        obs_ref[...] = mine[:, :capacity, :].reshape(lanes, channels).T
        profile = shares[1:2] * taken_ref[0].T
        for k in range(1, 4):
            profile = profile + shares[k + 1 : k + 2] * taken_ref[k].T
        profile_ref[...] = profile
        rise_ref[0 : levels - 1, :] = profile[1:] - profile[:-1]
        rise_ref[levels - 1 : levels, :] = jnp.zeros((1, lanes), jnp.float32)
        push_ref[...] = jnp.zeros_like(push_ref)

        def some_channels(c, carry):
            @pl.when(f == 0)
            def _():
                absorb_copy(c).wait()

            at = pl.multiple_of(c * wide, wide)
            slope = slope_b[pl.ds(at, wide), :]
            scale = slope * (LN2 * LN2)

            def down(i, state):
                path, total, above = state
                for u in range(UNROLL):
                    level = i * UNROLL + u
                    depth = absorb_b[level, pl.ds(at, wide), :] * jnp.exp2(
                        slope * profile_ref[pl.ds(level, 1), :]
                    )
                    path = path - depth
                    trans = jnp.exp2(path)
                    side = depth * scale
                    side_ref[level] = side
                    main_ref[level] = (above - trans) + side * total
                    total = total + trans * rise_ref[pl.ds(level, 1), :]
                    above = trans
                for u in range(per_loop):
                    scatter(before, (c * (levels // UNROLL) + i) * per_loop + u)
                return path, total, above

            zero = jnp.zeros((wide, lanes), jnp.float32)
            _, total, last = lax.fori_loop(0, levels // UNROLL, down, (zero, zero, zero + 1.0))
            main_ref[levels - 1] += last
            evolved = total + profile_ref[0:1, :]
            evo_ref[pl.ds(at, wide), :] = evolved
            obs = obs_ref[pl.ds(at, wide), :]
            force = jnp.where(
                obs < 0.5 * REJECTED, inverse_b[pl.ds(at, wide), :] * (obs - evolved), 0.0
            )

            def up(i, carry):
                for u in range(UNROLL):
                    level = i * UNROLL + u
                    push = force * (main_ref[level] - total * side_ref[level])
                    push_ref[pl.ds(pl.multiple_of(level * 8, 8), 8), :] += jnp.sum(
                        push.reshape(wide // 8, 8, lanes), axis=0
                    )
                for u in range(per_loop):
                    gather(after, (c * (levels // UNROLL) + i) * per_loop + u)
                return carry

            lax.fori_loop(0, levels // UNROLL, up, 0)
            return carry

        lax.fori_loop(0, channels // wide, some_channels, 0)
        evolved_ref[pl.ds(f * group, group)] = evo_ref[...].T.reshape(group, capacity, channels)
        push = push_ref[pl.ds(0, levels, stride=8), :]
        for u in range(1, 8):
            push = push + push_ref[pl.ds(u, levels, stride=8), :]
        for k in range(4):
            terms_ref[k] = (shares[k + 1 : k + 2] * push).T
        return carry

    lax.fori_loop(0, blocks, block, 0)

    def scatter_last(i, carry):
        for u in range(8):
            scatter(blocks - 1, i * 8 + u)
        return carry

    lax.fori_loop(0, lanes // 8, scatter_last, 0)

    def add_up(r, carry):
        row = pl.ds(pl.multiple_of(r * tile_cols, tile_cols), tile_cols)
        total = (sums_ref[0, row, :] + sums_ref[1, row, :]) + (
            sums_ref[2, row, :] + sums_ref[3, row, :]
        )
        field_ref[r] = total
        return jnp.maximum(carry, jnp.maximum(jnp.abs(total[:halo]), jnp.abs(total[-halo:])))

    peak = lax.fori_loop(
        0, tile_rows, add_up, jnp.full((halo, levels), 1e-30, jnp.float32), unroll=2
    )
    for r in (*range(halo), *range(tile_rows - halo, tile_rows)):
        for first in range(0, tile_cols, halo):
            peak = jnp.maximum(peak, jnp.abs(field_ref[r, first : first + halo]))
    power = jnp.ceil(jnp.log2(jnp.max(peak, axis=0, keepdims=True)))
    scale = jnp.exp2(15.0 - power)

    def code(x):
        whole = jnp.clip(jnp.floor(x * scale + 0.5), -32767.0, 32767.0)
        return whole.astype(jnp.int32).astype(jnp.int16)

    def code_sides(r, carry):
        left_ref[halo + 1 + r] = code(field_ref[r, :halo])
        right_ref[halo + 1 + r] = code(field_ref[r, tile_cols - halo :])
        return carry

    lax.fori_loop(0, tile_rows, code_sides, 0, unroll=4)
    for r in range(halo):
        top_ref[r] = code(field_ref[r])
        bottom_ref[r] = code(field_ref[tile_rows - halo + r])
    for ref, last in (
        (top_ref, halo), (bottom_ref, halo),
        (left_ref, halo + 1 + tile_rows), (right_ref, halo + 1 + tile_rows),
    ):
        ref[last] = jnp.broadcast_to(power, ref.shape[1:]).astype(jnp.int32).astype(jnp.int16)


def decode_field(coded, power):
    scale = jnp.exp2(power.astype(jnp.int32).astype(jnp.float32) - 15.0)
    return coded.astype(jnp.int32).astype(jnp.float32) * scale


def lay(halo, target, centre, north, south, west, east):
    tile_rows, tile_cols, _ = centre.shape
    breadth = tile_cols + 2 * halo
    mid_r, mid_c = slice(halo, halo + tile_rows), slice(halo, halo + tile_cols)
    target[mid_r, mid_c] = centre[...]
    target[:halo, mid_c] = decode_field(north[:halo], north[halo])
    target[halo + tile_rows :, mid_c] = decode_field(south[:halo], south[halo])
    for side, cols in ((west, slice(0, halo)), (east, slice(halo + tile_cols, breadth))):
        read, put = 0, 0
        for count in (halo, tile_rows, halo):
            target[put : put + count, cols] = decode_field(
                side[read : read + count], side[read + count]
            )
            read, put = read + count + 1, put + count


KAPPA_LOW = 0.12
KAPPA_STEP = 0.125 / 65535


def encode_kappa(x):
    whole = jnp.round((x - KAPPA_LOW) * (1.0 / KAPPA_STEP))
    return (jnp.clip(whole, 0.0, 65535.0) - 32768.0).astype(jnp.int16)


def decode_kappa(x):
    whole = x.astype(jnp.int32).astype(jnp.float32) + 32768.0
    return whole * KAPPA_STEP + KAPPA_LOW


def mixed_row(plain_ref, i, stretch):
    return jnp.stack([plain_ref[i, pl.ds(t, 8, stride=stretch), :] for t in range(stretch)])


def eastward(x):
    return jnp.concatenate([x[1:], pltpu.roll(x[0], 7, 0)[None]], axis=0)


def westward(x):
    return jnp.concatenate([pltpu.roll(x[-1], 1, 0)[None], x[:-1]], axis=0)


def edges_kernel(
    halo, inside_ref, centre_ref, north_ref, south_ref, west_hbm, east_hbm, east_ref,
    south_edge_ref, plain_ref, west_ref, east_side_ref, sems
):
    copies = [
        pltpu.make_async_copy(west_hbm, west_ref, sems.at[0]),
        pltpu.make_async_copy(east_hbm, east_side_ref, sems.at[1]),
    ]
    for copy in copies:
        copy.start()
    tile_rows, tile_cols, _ = centre_ref.shape
    height, _ = plain_ref.shape[:2]
    mid_r, mid_c = slice(halo, halo + tile_rows), slice(halo, halo + tile_cols)
    low, end = slice(0, halo), slice(halo + tile_rows, height)
    plain_ref[mid_r, mid_c] = centre_ref[...]
    plain_ref[low, mid_c] = decode_kappa(north_ref[...])
    plain_ref[end, mid_c] = decode_kappa(south_ref[...])
    for copy in copies:
        copy.wait()
    plain_ref[:, :halo] = decode_kappa(west_ref[...])
    plain_ref[:, halo + tile_cols :] = decode_kappa(east_side_ref[...])
    plain_ref[low] = plain_ref[low] * inside_ref[0]
    plain_ref[end] = plain_ref[end] * inside_ref[1]
    stretch = east_ref.shape[1]

    def edges(i, here):
        below = mixed_row(plain_ref, i + 1, stretch)
        east_ref[i] = 0.5 * (here + eastward(here))
        south_edge_ref[i] = 0.5 * (here + below)
        return below

    lax.fori_loop(0, height - 1, edges, mixed_row(plain_ref, 0, stretch), unroll=2)


def relax_kernel(
    halo, inside_ref, centre_ref, north_ref, south_ref, west_ref, east_side_ref, east_ref,
    south_edge_ref, out_ref, plain_ref, first_ref, second_ref
):
    tile_rows, tile_cols, _ = out_ref.shape
    height = tile_rows + 2 * halo
    stretch = first_ref.shape[1]
    lay(halo, plain_ref, centre_ref, north_ref, south_ref, west_ref, east_side_ref)

    source, target = None, second_ref
    for step in range(1, halo + 1):
        last = step == halo

        def read(i, source=source):
            return mixed_row(plain_ref, i, stretch) if source is None else source[i]

        def row(i, carry, scale=None, read=read, target=target, last=last):
            here, from_north = carry
            below = read(i + 1)
            to_east = east_ref[i] * (eastward(here) - here)
            from_south = south_edge_ref[i] * (below - here)
            value = here + (to_east - westward(to_east)) + (from_south - from_north)
            if scale is not None:
                value = value * scale
            if last:
                for t in range(stretch):
                    plain_ref[i, pl.ds(t, 8, stride=stretch), :] = value[t]
            else:
                target[i] = value
            return below, from_south

        here = read(step)
        carry = (here, south_edge_ref[step - 1] * (here - read(step - 1)))
        carry = lax.fori_loop(
            step, halo, functools.partial(row, scale=inside_ref[0]), carry, unroll=True
        )
        carry = lax.fori_loop(halo, halo + tile_rows, row, carry, unroll=4)
        lax.fori_loop(
            halo + tile_rows, height - step, functools.partial(row, scale=inside_ref[1]), carry,
            unroll=True,
        )
        source, target = target, first_ref if target is second_ref else second_ref
    out_ref[...] = plain_ref[halo : halo + tile_rows, halo : halo + tile_cols, :]


def depart_kernel(slot_ref, evolved_ref, observed_ref, out_ref):
    foot_count, _ = observed_ref.shape
    slots = evolved_ref.shape[0]
    slot = slot_ref[...]
    parts = jnp.concatenate(thirds(evolved_ref[...]), axis=1)
    chosen = jnp.where(iota((slots, foot_count), 0) == slot, 1.0, 0.0).astype(jnp.bfloat16)
    out_ref[...] = observed_ref[...] - add_thirds(dot_f32(chosen, parts, ((0,), (0,))))


def vmem():
    return pl.BlockSpec(memory_space=pltpu.VMEM)


def smem():
    return pl.BlockSpec(memory_space=pltpu.SMEM)


def hbm():
    return pl.BlockSpec(memory_space=pltpu.HBM)


def params(mib):
    return pltpu.CompilerParams(vmem_limit_bytes=mib * MIB)


def cost(flops, transcendentals, moved):
    return pl.CostEstimate(flops=flops, transcendentals=transcendentals, bytes_accessed=moved)


def neighbours(axis, periodic):
    count = lax.axis_size(axis)
    forward = [(i, i + 1) for i in range(count - 1)]
    if periodic:
        forward.append((count - 1, 0))
    return forward, [(target, source) for source, target in forward]


def join(north, south, left, right):
    halo = left.shape[1]
    right = jnp.concatenate([north[:, -halo:], right, south[:, -halo:]], axis=0)
    left = jnp.concatenate([north[:, :halo], left, south[:, :halo]], axis=0)
    return left, right


def join_kernel(north_ref, south_ref, _, __, left_ref, right_ref, sems):
    count, tile_cols, _ = north_ref.shape
    total, halo, _ = left_ref.shape
    copies = []
    for target, cols in ((left_ref, 0), (right_ref, tile_cols - halo)):
        for source, row in ((north_ref, 0), (south_ref, total - count)):
            copies.append(
                pltpu.make_async_copy(
                    source.at[:, pl.ds(cols, halo)], target.at[pl.ds(row, count)],
                    sems.at[len(copies)],
                )
            )
    for copy in copies:
        copy.start()
    for copy in copies:
        copy.wait()


def join_in_place(north, south, left, right):
    return pl.pallas_call(
        join_kernel,
        out_shape=tuple(jax.ShapeDtypeStruct(x.shape, x.dtype) for x in (left, right)),
        in_specs=[vmem()] * 2 + [hbm()] * 2,
        out_specs=(hbm(), hbm()),
        input_output_aliases={2: 0, 3: 1},
        scratch_shapes=[pltpu.SemaphoreType.DMA((4,))],
        compiler_params=params(2),
        name="join",
    )(north, south, left, right)


def halos(top, bottom, left, right, join):
    lat_up, lat_down = neighbours("lat", False)
    lon_up, lon_down = neighbours("lon", True)
    south = lax.ppermute(top, "lat", lat_down)
    north = lax.ppermute(bottom, "lat", lat_up)
    lefts, rights = join(north, south, left, right)
    west = lax.ppermute(rights, "lon", lon_up)
    east = lax.ppermute(lefts, "lon", lon_down)
    return north, south, west, east


def local(
    background, diffusivity, tile_index, anchor, weights, observed, accept, absorb, sensitivity,
    inverse_variance
):
    f32 = jnp.float32
    lat_count = lax.axis_size("lat")
    lon_count = lax.axis_size("lon")
    dev_count = lat_count * lon_count
    foot_count, channels = observed.shape
    capacity = max(2, 2 * foot_count // dev_count)
    tile_rows, tile_cols, levels = background.shape
    slots = dev_count * capacity
    lanes = 128
    group = lanes // capacity
    cells = tile_rows * tile_cols
    halo = STEPS

    me = lax.axis_index("lat") * lon_count + lax.axis_index("lon")
    lane = (lax.rem(me, group) * capacity).astype(jnp.int32).reshape(1)
    send, slot = pl.pallas_call(
        functools.partial(pack_kernel, dev_count, capacity, tile_cols),
        out_shape=(
            jax.ShapeDtypeStruct((dev_count, capacity + META, channels), f32),
            jax.ShapeDtypeStruct((1, foot_count), jnp.int32),
        ),
        in_specs=[smem()] + [vmem()] * 5,
        out_specs=(vmem(), vmem()),
        scratch_shapes=[pltpu.VMEM((dev_count * META, foot_count), f32)],
        compiler_params=params(60),
        cost_estimate=cost(2 * slots * foot_count * channels * 3, 0, 4 * slots * channels * 3),
        name="pack",
    )(
        lane, tile_index.reshape(1, foot_count), anchor.reshape(1, foot_count), weights.T,
        observed, accept
    )
    recv = lax.all_to_all(send, ("lat", "lon"), split_axis=0, concat_axis=0, tiled=True)

    kappa_halos = halos(
        encode_kappa(diffusivity[:halo]), encode_kappa(diffusivity[-halo:]),
        encode_kappa(diffusivity[:, :halo]), encode_kappa(diffusivity[:, -halo:]), join
    )
    absorb_wide = pl.pallas_call(
        spread_kernel,
        out_shape=jax.ShapeDtypeStruct((levels, channels, lanes), f32),
        grid=(levels // 16,),
        in_specs=[pl.BlockSpec((levels, channels), lambda i: (0, 0))],
        out_specs=pl.BlockSpec((16, channels, lanes), lambda i: (i, 0, 0)),
        scratch_shapes=[pltpu.VMEM((channels, levels), f32)],
        compiler_params=params(60),
        cost_estimate=cost(levels * channels * lanes, 0, 4 * levels * channels * lanes),
        name="spread",
    )(absorb)

    wide = 32
    evolved, field, top, bottom, left, right = pl.pallas_call(
        functools.partial(column_kernel, capacity, halo),
        out_shape=(
            jax.ShapeDtypeStruct((dev_count, capacity, channels), f32),
            jax.ShapeDtypeStruct((tile_rows, tile_cols, levels), f32),
            jax.ShapeDtypeStruct((halo + 1, tile_cols, levels), jnp.int16),
            jax.ShapeDtypeStruct((halo + 1, tile_cols, levels), jnp.int16),
            jax.ShapeDtypeStruct((tile_rows + 2 * halo + 3, halo, levels), jnp.int16),
            jax.ShapeDtypeStruct((tile_rows + 2 * halo + 3, halo, levels), jnp.int16),
        ),
        in_specs=[vmem()] + [hbm()] * 2 + [vmem()] * 2,
        out_specs=(vmem(),) * 6,
        scratch_shapes=[
            pltpu.SMEM((slots // lanes, lanes), jnp.int32),
        pltpu.VMEM((slots // lanes, lanes), jnp.int32),
            pltpu.SemaphoreType.DMA,
            pltpu.SemaphoreType.DMA((channels // wide,)),
            pltpu.VMEM((tile_rows, tile_cols, levels), background.dtype),
            pltpu.SemaphoreType.DMA,
            pltpu.VMEM((cells, levels), f32),
            pltpu.VMEM((levels, channels, lanes), f32),
            pltpu.VMEM((channels, lanes), f32),
            pltpu.VMEM((channels, lanes), f32),
            pltpu.VMEM((4, lanes, levels), f32),
            pltpu.VMEM((4, lanes, levels), f32),
            pltpu.VMEM((levels, lanes), f32),
            pltpu.VMEM((levels, lanes), f32),
            pltpu.VMEM((channels, lanes), f32),
            pltpu.VMEM((channels, lanes), f32),
            pltpu.VMEM((levels, wide, lanes), f32),
            pltpu.VMEM((levels, wide, lanes), f32),
            pltpu.VMEM((levels * 8, lanes), f32),
            pltpu.VMEM((4, cells, levels), f32),
        ],
        compiler_params=params(52),
        cost_estimate=cost(
            14 * slots * levels * channels, 2 * slots * levels * channels, 12 * cells * levels
        ),
        name="column",
    )(
        recv, background, absorb_wide, sensitivity.reshape(1, channels),
        inverse_variance.reshape(1, channels)
    )

    field_halos = halos(top, bottom, left, right, join_in_place)
    lat_at = lax.axis_index("lat")
    inside = jnp.stack([lat_at > 0, lat_at < lat_count - 1]).astype(f32)
    height, breadth = tile_rows + 2 * halo, tile_cols + 2 * halo

    plain = pltpu.VMEM((height, breadth, levels), f32)
    mixed = (height, breadth // 8, 8, levels)

    east, south = pl.pallas_call(
        functools.partial(edges_kernel, halo),
        out_shape=(jax.ShapeDtypeStruct(mixed, f32),) * 2,
        in_specs=[smem()] + [vmem()] * 3 + [hbm()] * 2,
        out_specs=(vmem(),) * 2,
        scratch_shapes=[plain]
        + [pltpu.VMEM((height, halo, levels), jnp.int16)] * 2
        + [pltpu.SemaphoreType.DMA((2,))],
        compiler_params=params(22),
        cost_estimate=cost(4 * height * breadth * levels, 0, 12 * cells * levels),
        name="edges",
    )(inside, diffusivity, *kappa_halos)


    returned = lax.all_to_all(
        evolved, ("lat", "lon"), split_axis=0, concat_axis=0, tiled=True
    )

    departure = pl.pallas_call(
        depart_kernel,
        out_shape=jax.ShapeDtypeStruct((foot_count, channels), f32),
        in_specs=[vmem()] * 3,
        out_specs=vmem(),
        compiler_params=params(16),
        cost_estimate=cost(2 * slots * foot_count * channels * 3, 0, 4 * slots * channels * 2),
        name="depart",
    )(slot, returned.reshape(slots, channels), observed)

    increment = pl.pallas_call(
        functools.partial(relax_kernel, halo),
        out_shape=jax.ShapeDtypeStruct((tile_rows, tile_cols, levels), f32),
        in_specs=[smem()] + [vmem()] * 7,
        out_specs=vmem(),
        scratch_shapes=[plain, pltpu.VMEM(mixed, f32), pltpu.VMEM(mixed, f32)],
        compiler_params=params(26),
        cost_estimate=cost(10 * STEPS * height * breadth * levels, 0, 16 * cells * levels),
        name="relax",
    )(inside, field, *field_halos, east, south)
    return (departure, increment)


def solution(mesh):
    in_specs = (
        P("lat", "lon", None),
        P("lat", "lon", None),
        P(("lat", "lon"), None),
        P(("lat", "lon")),
        P(("lat", "lon"), None),
        P(("lat", "lon"), None),
        P(("lat", "lon"), None),
        P(),
        P(),
        P(),
    )
    out_specs = (P(("lat", "lon"), None), P("lat", "lon", None))

    return jax.shard_map(local, mesh=mesh, in_specs=in_specs, out_specs=out_specs, check_vma=False)
```
